256 devices in a mesh: tm: 64 (over y, z, core), space: 4 (over x).
Axes of the slice: x: 4, y: 4, z: 8, core: 2. Of those that a mesh axis runs over, the one named last changes fastest.
Arguments:
- snapshots: float32 [1024, 32, 2048], P('tm', None, 'space'), may hold values from -12 to 12
- quad_weights: float32 [2048], P('space'), may hold values from 0.25 to 4
Outputs:
- modes: float32 [2, 1024, 2048], P(None, 'tm', 'space')
- energies: float32 [1024], P('tm')
The draws below stay inside these ranges and needn't reach their ends.
All inputs are finite; a program needn't handle non-finite values.
Results may differ from the reference program's by a relative error of at most 0.0001.
Values sent between devices are 32-bit elements; how exact they have to be, the bound alone decides.
A program may use at most 64 MiB of HBM per device.

```python
import math
import jax
import jax.numpy as jnp
from jax import lax

NT = 1024
B = 32
POWER = 3
NT_DEV = 16
NS = 2048
N_TM = 64


def draw_snapshots(key, part):
    key_noise, key_common, key_amp = jax.random.split(key, 3)
    noise = jnp.clip(jax.random.normal(key_noise, (NT, B, NS), jnp.float32), -6.0, 6.0)
    common = jnp.clip(jax.random.normal(key_common, (NT, 1, NS), jnp.float32), -6.0, 6.0)
    amplitude = jax.random.uniform(key_amp, (1, B, 1), jnp.float32, 0.15, 0.5)
    return (noise + amplitude * common).astype(jnp.float32)


def block_scale(stream_key, extent, cuts, smallest, largest):
    gain = 1.0
    for dim, blocks in cuts:
        steps = jax.random.uniform(jax.random.fold_in(jax.random.fold_in(stream_key, 6), dim), (blocks,), jnp.float32, smallest / len(cuts), largest / len(cuts))
        gain = gain * jnp.repeat(jnp.exp(steps), extent[dim] // blocks).reshape((-1,) + (1,) * (len(extent) - 1 - dim))
    return gain


def setup_inputs(seed: int = 0) -> dict:
    arg_keys = jax.random.split(jax.random.key(seed), 3)
    return {
        "snapshots": draw_snapshots(jax.random.fold_in(arg_keys[2], 71), 0),
        "quad_weights": jnp.clip(jnp.exp(math.log(4.0) - 2.7725887 * jax.random.uniform(arg_keys[1], (NS,), jnp.float32) ** block_scale(arg_keys[1], (NS,), ((0, 4),), -0.2, 0.2)), 0.25, 4.0),
    }


def bit_reverse(values, bit_count):
    result = jnp.zeros_like(values)
    for position in range(bit_count):
        result = result + ((values >> position & 1) << bit_count - 1 - position)
    return result

def matvec(matrix, vector):
    return jnp.einsum('fbc,fc->fb', matrix, vector, precision=lax.Precision.HIGHEST)

def power_modes(real_gram, imag_gram):
    vec_real = jnp.ones(real_gram.shape[:2], jnp.float32) / math.sqrt(real_gram.shape[1])
    vec_imag = jnp.zeros(real_gram.shape[:2], jnp.float32)
    for sweep_idx in range(POWER):
        new_real = matvec(real_gram, vec_real) - matvec(imag_gram, vec_imag)
        new_imag = matvec(real_gram, vec_imag) + matvec(imag_gram, vec_real)
        length = lax.rsqrt(lax.optimization_barrier(jnp.sum(new_real * new_real + new_imag * new_imag, axis=1, keepdims=True)) + 1e-06)
        vec_real = new_real * length
        vec_imag = new_imag * length
    image_real = matvec(real_gram, vec_real) - matvec(imag_gram, vec_imag)
    image_imag = matvec(real_gram, vec_imag) + matvec(imag_gram, vec_real)
    energy = lax.optimization_barrier(jnp.sum(vec_real * image_real + vec_imag * image_imag, axis=1))
    return (vec_real, vec_imag, energy)

def reference(snapshots, quad_weights):
    time_ids = jnp.arange(NT).astype(jnp.float32)
    window = (0.5 - 0.5 * jnp.cos(2.0 * math.pi * time_ids / NT)) / math.sqrt(0.375 * NT)
    spectrum = jnp.fft.fft(snapshots * window[:, None, None], axis=0)
    row_ids = jnp.arange(NT, dtype=jnp.int32)
    bit_count = N_TM.bit_length() - 1
    reorder = bit_reverse(row_ids // NT_DEV, bit_count) + N_TM * (row_ids % NT_DEV)
    spectrum = spectrum[reorder]
    spectral = jnp.stack([jnp.real(spectrum), jnp.imag(spectrum)]).astype(jnp.float32)
    weighted = spectral * quad_weights
    gram_full = jnp.einsum('pfbx,qfcx->fpbqc', weighted, spectral, precision=lax.Precision.HIGHEST) / NS
    real_gram = gram_full[:, 0, :, 0] + gram_full[:, 1, :, 1]
    imag_gram = gram_full[:, 0, :, 1] - gram_full[:, 1, :, 0]
    vec_real, vec_imag, energy = power_modes(real_gram, imag_gram)
    inverse_root = lax.rsqrt(energy + 1e-06)[:, None]
    modes_real = jnp.einsum('fb,fbx->fx', vec_real, spectral[0], precision=lax.Precision.HIGHEST) - jnp.einsum('fb,fbx->fx', vec_imag, spectral[1], precision=lax.Precision.HIGHEST)
    modes_imag = jnp.einsum('fb,fbx->fx', vec_imag, spectral[0], precision=lax.Precision.HIGHEST) + jnp.einsum('fb,fbx->fx', vec_real, spectral[1], precision=lax.Precision.HIGHEST)
    return (jnp.stack([modes_real * inverse_root, modes_imag * inverse_root]), energy)
```

```python
import math

import jax
import jax.numpy as jnp
import numpy as np
from jax import lax
from jax.experimental import pallas as pl
from jax.experimental.pallas import tpu as pltpu
from jax.sharding import PartitionSpec as P

POWER = 3
F32 = jnp.float32
BF16 = jnp.bfloat16
MESH = pl.DeviceIdType.MESH
HIGHEST = lax.Precision.HIGHEST
NT = 1024
NX, NY, NZ, NC = 4, 4, 8, 2


def transform_table():
    t = np.arange(NT // 2)
    rows = []
    for unit in list(range(0, 32, 2)) + list(range(1, 32, 2)):
        if unit == 0:
            freq = np.array([64 * j for j in range(8)] + [32 + 64 * j for j in range(8)])
        else:
            freq = unit + 64 * np.arange(16)
        angle = 2.0 * np.pi * ((freq[:, None] * t[None, :]) % NT) / NT
        real, imag = np.cos(angle), -np.sin(angle)
        if unit == 0:
            imag[0] = np.cos(np.pi * t)
        rows += [real, imag]
    table = np.concatenate(rows).astype(np.float32)
    high = table.astype(jnp.bfloat16)
    low = (table - high.astype(np.float32)).astype(jnp.bfloat16)
    return np.stack([high, low])


def window_table():
    t = np.arange(NT)
    window = (0.5 - 0.5 * np.cos(2.0 * np.pi * t / NT)) / np.sqrt(0.375 * NT)
    return np.broadcast_to(window.astype(np.float32)[:, None], (NT, 128)).reshape(64, 16, 128)


def split(x):
    high = x.astype(BF16)
    return high, (x - high.astype(F32)).astype(BF16)


def dot(a, b):
    return jnp.dot(a, b, preferred_element_type=F32)


def dot_nt(a, b):
    return lax.dot_general(a, b, (((1,), (1,)), ((), ())), preferred_element_type=F32)


def interleave(first, second, low):
    crossed = pltpu.roll(jnp.where(low, second, first), 64, 1)
    return jnp.where(low, first, crossed), jnp.where(low, crossed, second)


def bit_reverse(value):
    result = 0
    for position in range(6):
        result = result + ((value >> position) & 1) * (1 << (5 - position))
    return result


def kernel(
    x_hbm, tab_hbm, win_hbm, w_ref, out_ref, e_ref,
    xin, win, tab, sb, rb, eh, ob, db, mh, ml, go, gr, vs, va, fs, fb,
    in_sem, tab_sem, s1, r1, s2, r2, s3, r3, s4, r4, s5, r5,
):
    me = lax.axis_index("tm")
    sx = lax.axis_index("space")
    y, z, c = me // 16, (me // 2) % 8, me % 2
    p = y * 2 + c
    yo = 3 - y
    unit = c * 16 + sx * 4 + (yo % 2) * 2 + yo // 2

    loads = [
        pltpu.make_async_copy(x_hbm.at[:, pl.ds(q * 128, 128)], xin.at[q], in_sem.at[q])
        for q in range(4)
    ]
    for load in loads:
        load.start()
    load_win = pltpu.make_async_copy(win_hbm.at[me], win, tab_sem.at[1])
    load_win.start()
    load_tab = pltpu.make_async_copy(tab_hbm, tab, tab_sem.at[0])
    load_tab.start()

    def unit_place(g):
        oy = (g % 2) * 2 + (g // 2) % 2
        return (g // 4) % 4, 3 - oy, g // 16

    barrier = pltpu.get_barrier_semaphore()

    @pl.loop(1, 64)
    def _(k):
        pl.semaphore_signal(barrier, 1, device_id=((me + k) % 64, sx), device_id_type=MESH)

    def peer(k):
        return (sx + k % 4) % 4, (y + k // 8) % 4, (c + (k // 4) % 2) % 2

    @pl.loop(1, 32)
    def _(k):
        px, py, pc = peer(k)
        pl.semaphore_signal(barrier, 1, device_id=(py * 16 + z * 2 + pc, px), device_id_type=MESH)

    mine = bit_reverse(me)
    my_unit = jnp.where(mine == 32, 0, jnp.where(mine > 32, 64 - mine, mine))
    ux, uy, uc = unit_place(my_unit)

    @pl.loop(0, 8)
    def _(k):
        pl.semaphore_signal(barrier, 1, device_id=(uy * 16 + k * 2 + uc, ux), device_id_type=MESH)

    lane = lax.broadcasted_iota(jnp.int32, (8, 128), 1)
    row = lax.broadcasted_iota(jnp.int32, (8, 128), 0)
    low = lane < 64
    root_w = jnp.sqrt(w_ref[...])
    load_win.wait()
    for load in loads:
        load.wait()
    factor = [
        [win[8 * sh : 8 * sh + 8, :] * root_w[:, 128 * q : 128 * q + 128] for q in range(4)]
        for sh in range(2)
    ]

    @pl.loop(0, 16)
    def _(bp):
        half, owner = bp % 2, bp // 2
        base = (owner // 2) * 16 + owner % 2
        for q in range(4):
            for sh in range(2):
                t0 = xin[q, pl.ds(sh * 256 + 2 * bp, 8, stride=32), :] * factor[sh][q]
                t1 = xin[q, pl.ds(sh * 256 + 2 * bp + 1, 8, stride=32), :] * factor[sh][q]
                even, odd = interleave(t0, t1, low)
                sb[half, base + 4 * q, 8 * sh : 8 * sh + 8, :] = even
                sb[half, base + 4 * q + 2, 8 * sh : 8 * sh + 8, :] = odd

    pl.semaphore_wait(barrier, 63 + 31 + 8)

    for h in range(2):

        @pl.loop(1, 64)
        def _(k):
            i = k % 8
            dz = jnp.where(i % 2 == 1, (i + 1) // 2, (8 - i // 2) % 8)
            py, pz, pc = (y + k // 16) % 4, (z + dz) % 8, (c + (k // 8) % 2) % 2
            to = py * 16 + pz * 2 + pc
            pltpu.make_async_remote_copy(
                sb.at[h, to], rb.at[h, me], s1.at[h], r1.at[h],
                device_id=(to, sx), device_id_type=MESH,
            ).start()

    for h in range(2):
        rb[h, me] = sb[h, me]

    load_tab.wait()
    for h in range(2):
        pltpu.make_async_copy(rb.at[h, pl.ds(0, 63)], rb.at[h, pl.ds(0, 63)], r1.at[h]).wait()

        @pl.loop(0, 8)
        def _(i):
            first = rb[h, pl.ds(i * 4, 4)].reshape(64, 128)
            second = rb[h, pl.ds(32 + i * 4, 4)].reshape(64, 128)
            for parity, value in enumerate((first + second, first - second)):
                high, rest = split(value)
                eh[parity, pl.ds(i * 64, 64), 0:128] = high
                eh[parity, pl.ds(i * 64, 64), 128:256] = rest

        @pl.loop(0, 8)
        def _(i):
            data = eh[i // 4]
            main = dot(tab[0, pl.ds(i * 128, 128), :], data)
            rest = dot(tab[1, pl.ds(i * 128, 128), :], data[:, 0:128])
            total = main[:, 0:128] + (main[:, 128:256] + rest)
            ob[h, pl.ds(i * 4, 4)] = total.reshape(4, 32, 128)

        here = pl.ds(pl.multiple_of((sx * 16 + 2 * p + h) * 32, 32), 32)

        @pl.loop(1, 32)
        def _(k):
            px, py, pc = peer(k)
            oy = 3 - py
            g = pc * 16 + px * 4 + (oy % 2) * 2 + oy // 2
            pltpu.make_async_remote_copy(
                ob.at[h, (g % 2) * 16 + g // 2], db.at[here], s2, r2,
                device_id=(py * 16 + z * 2 + pc, px), device_id_type=MESH,
            ).start()

        db[here, :] = ob[h, (unit % 2) * 16 + unit // 2]

    pltpu.make_async_copy(db.at[pl.ds(0, 62 * 32)], db.at[pl.ds(0, 62 * 32)], r2).wait()

    low16 = lax.broadcasted_iota(jnp.int32, (16, 128), 1) < 64

    @pl.loop(0, 8)
    def _(i):
        zt = (z + 1 + i) % 8
        grams = []
        for f in range(2):
            j = zt * 2 + f
            special = jnp.where((unit == 0) & (j == 0), 1.0, 0.0).astype(F32)
            planes = []
            for ri in range(2):
                tiles = []
                for q in range(2):
                    ta = db[pl.ds((2 * q) * 512 + ri * 16 + j, 16, stride=32), :]
                    tb = db[pl.ds((2 * q + 1) * 512 + ri * 16 + j, 16, stride=32), :]
                    tiles.append(jnp.concatenate(interleave(ta, tb, low16), axis=0))
                planes.append(jnp.concatenate(tiles, axis=1))
            real, imag = planes
            rh, rl = split(real)
            ih, il = split(imag)
            base = pl.multiple_of(j * 64, 64)
            mh[pl.ds(base, 32), :] = rh
            mh[pl.ds(base + 32, 32), :] = ih
            ml[pl.ds(base, 32), :] = rl
            ml[pl.ds(base + 32, 32), :] = il
            sh_, sl_ = split(imag * (1.0 - special))
            ch, cl = split(imag * special - real * (1.0 - special))
            left_h = jnp.concatenate([rh, ih], axis=1)
            left_l = jnp.concatenate([rl, il], axis=1)
            right_h = jnp.concatenate(
                [jnp.concatenate([rh, sh_], axis=1), jnp.concatenate([sh_, ch], axis=1)], axis=0
            )
            right_l = jnp.concatenate(
                [jnp.concatenate([rl, sl_], axis=1), jnp.concatenate([sl_, cl], axis=1)], axis=0
            )
            grams.append(
                dot_nt(left_h, right_h) + (dot_nt(left_h, right_l) + dot_nt(left_l, right_h))
            )
        pair = jnp.concatenate(grams, axis=1)

        @pl.when(i < 7)
        def _():
            go[zt] = pair
            pltpu.make_async_remote_copy(
                go.at[zt], gr.at[z], s3, r3,
                device_id=(y * 16 + zt * 2 + c, sx), device_id_type=MESH,
            ).start()

        @pl.when(i == 7)
        def _():
            gr[z] = pair

    pltpu.make_async_copy(gr.at[pl.ds(0, 7)], gr.at[pl.ds(0, 7)], r3).wait()
    gram = gr[0]
    for k in range(1, 8):
        gram = gram + gr[k]
    gram = gram * (1.0 / 2048.0)

    even = row % 2 == 0
    lone = (row < 2) & (unit == 0) & (z == 0)
    valid = (lane < 32) & (row < 4)

    def swap_rows(v):
        return jnp.where(even, pltpu.roll(v, 7, 0), pltpu.roll(v, 1, 0))

    def image_of(v):
        product = jnp.dot(v[:, 0:32], gram, preferred_element_type=F32, precision=HIGHEST)
        chosen = jnp.where(row < 2, product, pltpu.roll(product, 64, 1))
        other = pltpu.roll(chosen, 96, 1)
        crossed = swap_rows(other)
        normal = jnp.where(even, chosen + crossed, chosen - crossed)
        alone = jnp.where(even, chosen, other)
        return jnp.where(valid, jnp.where(lone, alone, normal), 0.0)

    def pair_sum(v):
        total = jnp.broadcast_to(jnp.sum(v, axis=1, keepdims=True), (8, 128))
        return jnp.where(lone, total, total + swap_rows(total))

    vec = jnp.where(valid & (even | lone), 1.0 / math.sqrt(32.0), 0.0).astype(F32)
    for _ in range(POWER):
        new = image_of(vec)
        vec = new * lax.rsqrt(pair_sum(new * new) + 1e-06)
    energy = pair_sum(vec * image_of(vec))
    scaled = vec * lax.rsqrt(energy + 1e-06)
    spread = scaled + pltpu.roll(scaled, 32, 1)
    spread = spread + pltpu.roll(spread, 64, 1)
    placed = lane // 32 == row
    vec_row = jnp.sum(jnp.where(placed, spread, 0.0), axis=0, keepdims=True)
    energy_row = jnp.sum(jnp.where(placed, energy, 0.0), axis=0, keepdims=True)
    message = jnp.where(row == 0, vec_row, jnp.where(row == 1, energy_row, 0.0))
    vs[...] = message
    va[z] = message

    @pl.loop(1, 8)
    def _(i):
        zt = (z + i) % 8
        pltpu.make_async_remote_copy(
            vs, va.at[z], s4, r4,
            device_id=(y * 16 + zt * 2 + c, sx), device_id_type=MESH,
        ).start()

    rows = lax.broadcasted_iota(jnp.int32, (64, 128), 0)
    lanes = lax.broadcasted_iota(jnp.int32, (64, 128), 1)
    ver, ri, j = rows // 32, (rows // 16) % 2, rows % 16
    first_unit = unit == 0
    slot = jnp.where(ver == 0, j, 15 - j)
    slot_first = jnp.where(
        ver == 0,
        jnp.where(j < 8, j, jnp.where(j == 8, 0, 16 - j)),
        jnp.where(j < 8, 8 + j, 23 - j),
    )
    slot = jnp.where(first_unit, slot_first, slot)
    mirrored = jnp.where(first_unit, j // 8, ver) == 1
    direct = first_unit & (ver == 0) & (j == 0)
    nyquist = first_unit & (ver == 0) & (j == 8)
    lane_imag = (lanes // 32) % 2 == 1
    lane_slot = lanes // 64
    straight = jnp.where(
        direct, jnp.where(lane_imag, 0.0, 1.0),
        jnp.where(nyquist, jnp.where(lane_imag, 1.0, 0.0), jnp.where(lane_imag, -1.0, 1.0)),
    )
    straight = jnp.where(ri == 0, straight, 0.0).astype(F32)
    across = jnp.where(direct | nyquist, 0.0, jnp.where(mirrored, -1.0, 1.0))
    across = jnp.where(ri == 0, 0.0, across).astype(F32)
    picked = lanes % 64 == jnp.where(nyquist, 32, 0)

    pltpu.make_async_copy(va.at[pl.ds(0, 7)], va.at[pl.ds(0, 7)], r4).wait()

    modes = jnp.zeros((64, 256), F32)
    energies = jnp.zeros((64, 128), F32)
    imag_row = (lax.broadcasted_iota(jnp.int32, (1, 128), 1) // 32) % 2 == 1
    for k in range(8):
        v = va[k, 0:1, :]
        e = va[k, 1:2, :]
        v_swapped = jnp.where(imag_row, pltpu.roll(v, 32, 1), pltpu.roll(v, 96, 1))
        here = slot == 2 * k + lane_slot
        left = jnp.where(here, straight * v + across * v_swapped, 0.0)
        energies = energies + jnp.where(here & picked, e, 0.0)
        lh, ll = split(left)
        high = mh[128 * k : 128 * k + 128, :]
        modes = modes + (dot(lh, high) + (dot(lh, ml[128 * k : 128 * k + 128, :]) + dot(ll, high)))
    energies = jnp.broadcast_to(jnp.sum(energies, axis=1, keepdims=True), (64, 128))

    sends = []
    for ver in range(2):
        if ver == 0:
            klass = unit
        else:
            klass = jnp.where(unit == 0, 32, 64 - unit)
        to = bit_reverse(klass)
        base = 32 * ver
        energy_tile = jnp.where(low, energies[base : base + 8], energies[base + 8 : base + 16])
        for px in range(4):
            n = ver * 4 + px
            q = 128 * (px // 2)
            for ri in range(2):
                a = modes[base + 16 * ri : base + 16 * ri + 8, q : q + 128]
                b = modes[base + 16 * ri + 8 : base + 16 * ri + 16, q : q + 128]
                if px % 2 == 0:
                    tile = jnp.where(low, a, pltpu.roll(b, 64, 1))
                else:
                    tile = jnp.where(low, pltpu.roll(a, 64, 1), b)
                fs[n, 8 * ri : 8 * ri + 8, :] = tile
            fs[n, 16:24, :] = energy_tile
            send = pltpu.make_async_remote_copy(
                fs.at[n], fb.at[z], s5.at[n], r5.at[z],
                device_id=(to, px), device_id_type=MESH,
            )
            send.start()
            sends.append(send)

    for k in range(8):
        pltpu.make_async_copy(fb.at[k], fb.at[k], r5.at[k]).wait()
    unscale = lax.rsqrt(w_ref[...])
    for q in range(4):
        for ri in range(2):
            a = fb[2 * q, 8 * ri : 8 * ri + 8, :]
            b = fb[2 * q + 1, 8 * ri : 8 * ri + 8, :]
            first, second = interleave(a, b, low)
            scale = unscale[:, 128 * q : 128 * q + 128]
            out_ref[16 * ri : 16 * ri + 8, 128 * q : 128 * q + 128] = first * scale
            out_ref[16 * ri + 8 : 16 * ri + 16, 128 * q : 128 * q + 128] = second * scale
    e_tile = fb[0, 16:24, :]
    e_ref[0:8, :] = e_tile
    e_ref[8:16, :] = pltpu.roll(e_tile, 64, 1)

    for h in range(2):
        pltpu.make_async_copy(sb.at[h, pl.ds(0, 63)], sb.at[h, pl.ds(0, 63)], s1.at[h]).wait()
    pltpu.make_async_copy(db.at[pl.ds(0, 62 * 32)], db.at[pl.ds(0, 62 * 32)], s2).wait()
    pltpu.make_async_copy(gr.at[pl.ds(0, 7)], gr.at[pl.ds(0, 7)], s3).wait()
    pltpu.make_async_copy(va.at[pl.ds(0, 7)], va.at[pl.ds(0, 7)], s4).wait()
    for send in sends:
        send.wait_send()


def body(snapshots, quad_weights):
    times, blocks, points = snapshots.shape
    table = jnp.asarray(transform_table())
    window = jnp.asarray(window_table())
    any_spec = pl.BlockSpec(memory_space=pl.ANY)
    vmem = pl.BlockSpec(memory_space=pltpu.VMEM)
    dma = pltpu.SemaphoreType.DMA
    modes, energies = pl.pallas_call(
        kernel,
        out_shape=(
            jax.ShapeDtypeStruct((32, 512), F32),
            jax.ShapeDtypeStruct((16, 128), F32),
        ),
        in_specs=[any_spec, any_spec, any_spec, vmem],
        out_specs=(vmem, vmem),
        scratch_shapes=[
            pltpu.VMEM((4, 512, 128), F32),
            pltpu.VMEM((16, 128), F32),
            pltpu.VMEM((2, 1024, 512), BF16),
            pltpu.VMEM((2, 64, 16, 128), F32),
            pltpu.VMEM((2, 64, 16, 128), F32),
            pltpu.VMEM((2, 512, 256), BF16),
            pltpu.VMEM((2, 32, 32, 128), F32),
            pltpu.VMEM((2048, 128), F32),
            pltpu.VMEM((1024, 256), BF16),
            pltpu.VMEM((1024, 256), BF16),
            pltpu.VMEM((8, 32, 128), F32),
            pltpu.VMEM((8, 32, 128), F32),
            pltpu.VMEM((8, 128), F32),
            pltpu.VMEM((8, 8, 128), F32),
            pltpu.VMEM((8, 24, 128), F32),
            pltpu.VMEM((8, 24, 128), F32),
            dma((4,)), dma((2,)),
            dma((2,)), dma((2,)),
            dma, dma, dma, dma, dma, dma,
            dma((8,)), dma((8,)),
        ],
        compiler_params=pltpu.CompilerParams(collective_id=0, has_side_effects=True),
        name="spod",
    )(
        snapshots.reshape(times * blocks, points), table, window, quad_weights.reshape(1, points)
    )
    return modes.reshape(2, 16, points), energies[:, 0]


def solution(mesh):
    return jax.shard_map(
        body,
        mesh=mesh,
        in_specs=(P("tm", None, "space"), P("space")),
        out_specs=(P(None, "tm", "space"), P("tm")),
        check_vma=False,
    )
```

```python
import math

import jax
import jax.numpy as jnp
import numpy as np
from jax import lax
from jax.experimental import pallas as pl
from jax.experimental.pallas import tpu as pltpu
from jax.sharding import PartitionSpec as P

POWER = 3
F32 = jnp.float32
BF16 = jnp.bfloat16
MESH = pl.DeviceIdType.MESH
HIGHEST = lax.Precision.HIGHEST
NT = 1024
NX, NY, NZ, NC = 4, 4, 8, 2


def transform_table():
    t = np.arange(NT // 2)
    rows = []
    for unit in list(range(0, 32, 2)) + list(range(1, 32, 2)):
        if unit == 0:
            freq = np.array([64 * j for j in range(8)] + [32 + 64 * j for j in range(8)])
        else:
            freq = unit + 64 * np.arange(16)
        angle = 2.0 * np.pi * ((freq[:, None] * t[None, :]) % NT) / NT
        real, imag = np.cos(angle), -np.sin(angle)
        if unit == 0:
            imag[0] = np.cos(np.pi * t)
        rows += [real, imag]
    table = np.concatenate(rows).astype(np.float32)
    high = table.astype(jnp.bfloat16)
    low = (table - high.astype(np.float32)).astype(jnp.bfloat16)
    return np.stack([high, low])


def split(x):
    high = x.astype(BF16)
    return high, (x - high.astype(F32)).astype(BF16)


def dot(a, b):
    return jnp.dot(a, b, preferred_element_type=F32)


def dot_nt(a, b):
    return lax.dot_general(a, b, (((1,), (1,)), ((), ())), preferred_element_type=F32)


def interleave(first, second, low):
    crossed = pltpu.roll(jnp.where(low, second, first), 64, 1)
    return jnp.where(low, first, crossed), jnp.where(low, crossed, second)


def bit_reverse(value):
    result = 0
    for position in range(6):
        result = result + ((value >> position) & 1) * (1 << (5 - position))
    return result


def unit_of(x, y, c):
    return c * 16 + x * 4 + ((y & 1) << 1) + (y >> 1)


def far_first(z, i):
    return (z + jnp.where((i & 1) == 1, 4 - ((i + 1) >> 1), 4 + (i >> 1))) & 7


def kernel(
    x_hbm, tab_hbm, w_ref, out_ref,
    xin, tab, sb, rb, eh, ob, db, mh, ml, go, gr, vs, va, fs, fb,
    in_sem, tab_sem, row_sem, s1, r1, s2, r2, s3, r3, s4, r4, s5, r5,
):
    me = lax.axis_index("tm")
    sx = lax.axis_index("space")
    y, z, c = me >> 4, (me >> 1) & 7, me & 1
    p = y * 2 + c
    unit = unit_of(sx, y, c)

    loads = [
        pltpu.make_async_copy(x_hbm.at[:, pl.ds(q * 128, 128)], xin.at[q], in_sem.at[q])
        for q in range(4)
    ]
    for load in loads:
        load.start()
    load_tab = pltpu.make_async_copy(tab_hbm, tab, tab_sem)
    load_tab.start()

    barrier = pltpu.get_barrier_semaphore()

    def greet(semaphore, tm, space):
        pl.semaphore_signal(semaphore, 1, device_id=(tm, space), device_id_type=MESH)

    @pl.loop(1, 16)
    def _(k):
        greet(barrier, (me & 48) + ((me + k) & 15), sx)

    @pl.loop(1, 4)
    def _(k):
        greet(barrier, (me + 16 * k) & 63, sx)
        greet(barrier, me, (sx + k) & 3)

    def peer(k):
        return (sx + k) & 3, (y + (k >> 3)) & 3, c ^ ((k >> 2) & 1)

    lane = lax.broadcasted_iota(jnp.int32, (8, 128), 1)
    row = lax.broadcasted_iota(jnp.int32, (8, 128), 0)
    low = lane < 64
    root_w = jnp.sqrt(w_ref[...])
    for load in loads:
        load.wait()
    factor = []
    for sh in range(2):
        phase = (row + (16 * me + 8 * sh - NT // 2)).astype(F32) * (math.pi / NT)
        square = phase * phase
        cosine = jnp.full((8, 128), 1.0 / math.factorial(16), F32)
        for n in range(14, -1, -2):
            cosine = cosine * square + (-1.0) ** (n // 2) / math.factorial(n)
        window = cosine * cosine * (1.0 / math.sqrt(0.375 * NT))
        factor.append([window * root_w[:, 128 * q : 128 * q + 128] for q in range(4)])

    @pl.loop(0, 16)
    def _(bp):
        half, owner = bp & 1, bp >> 1
        base = (owner >> 1) * 16 + (owner & 1)
        for q in range(4):
            for sh in range(2):
                t0 = xin[q, pl.ds(sh * 256 + 2 * bp, 8, stride=32), :] * factor[sh][q]
                t1 = xin[q, pl.ds(sh * 256 + 2 * bp + 1, 8, stride=32), :] * factor[sh][q]
                even, odd = interleave(t0, t1, low)
                sb[half, base + 4 * q, 8 * sh : 8 * sh + 8, :] = even
                sb[half, base + 4 * q + 2, 8 * sh : 8 * sh + 8, :] = odd

    pl.semaphore_wait(barrier, 15 + 3 + 3)
    for k in range(1, 4):
        greet(row_sem, (me + 16 * k) & 63, sx)

    def send_columns(h):
        def send(k):
            i = k & 7
            dz = jnp.where((i & 1) == 1, (i + 1) >> 1, 8 - (i >> 1))
            to = (((y + (k >> 4)) & 3) << 4) + (((z + dz) & 7) << 1) + (c ^ ((k >> 3) & 1))
            pltpu.make_async_remote_copy(
                sb.at[h, to], rb.at[h, me], s1.at[h], r1.at[h],
                device_id=(to, sx), device_id_type=MESH,
            ).start()

        return send

    pl.loop(1, 16)(send_columns(0))
    pl.semaphore_wait(row_sem, 3)
    pl.loop(16, 64)(send_columns(0))
    pl.loop(1, 64)(send_columns(1))

    for h in range(2):
        rb[h, me] = sb[h, me]

    load_tab.wait()
    for h in range(2):
        pltpu.make_async_copy(rb.at[h, pl.ds(0, 63)], rb.at[h, pl.ds(0, 63)], r1.at[h]).wait()

        @pl.loop(0, 8)
        def _(i):
            first = rb[h, pl.ds(i * 4, 4)].reshape(64, 128)
            second = rb[h, pl.ds(32 + i * 4, 4)].reshape(64, 128)
            for parity, value in enumerate((first + second, first - second)):
                high, rest = split(value)
                eh[parity, pl.ds(i * 64, 64), 0:128] = high
                eh[parity, pl.ds(i * 64, 64), 128:256] = rest

        @pl.loop(0, 8)
        def _(i):
            data = eh[i >> 2]
            main = dot(tab[0, pl.ds(i * 128, 128), :], data)
            rest = dot(tab[1, pl.ds(i * 128, 128), :], data[:, 0:128])
            total = main[:, 0:128] + (main[:, 128:256] + rest)
            ob[h, pl.ds(i * 4, 4)] = total.reshape(4, 32, 128)

        here = pl.ds(pl.multiple_of((sx * 16 + 2 * p + h) * 32, 32), 32)

        @pl.loop(1, 32)
        def _(k):
            px, py, pc = peer(k)
            g = unit_of(px, py, pc)
            pltpu.make_async_remote_copy(
                ob.at[h, (g & 1) * 16 + (g >> 1)], db.at[here], s2, r2,
                device_id=((py << 4) + (z << 1) + pc, px), device_id_type=MESH,
            ).start()

        db[here, :] = ob[h, (unit & 1) * 16 + (unit >> 1)]

    pltpu.make_async_copy(db.at[pl.ds(0, 62 * 32)], db.at[pl.ds(0, 62 * 32)], r2).wait()

    low16 = lax.broadcasted_iota(jnp.int32, (16, 128), 1) < 64

    @pl.loop(0, 8)
    def _(i):
        zt = far_first(z, i)
        grams = []
        for f in range(2):
            j = zt * 2 + f
            special = jnp.where((unit == 0) & (j == 0), 1.0, 0.0).astype(F32)
            planes = []
            for ri in range(2):
                tiles = []
                for q in range(2):
                    ta = db[pl.ds((2 * q) * 512 + ri * 16 + j, 16, stride=32), :]
                    tb = db[pl.ds((2 * q + 1) * 512 + ri * 16 + j, 16, stride=32), :]
                    tiles.append(jnp.concatenate(interleave(ta, tb, low16), axis=0))
                planes.append(jnp.concatenate(tiles, axis=1))
            real, imag = planes
            rh, rl = split(real)
            ih, il = split(imag)
            base = pl.multiple_of(j * 64, 64)
            mh[pl.ds(base, 32), :] = rh
            mh[pl.ds(base + 32, 32), :] = ih
            ml[pl.ds(base, 32), :] = rl
            ml[pl.ds(base + 32, 32), :] = il
            sh_, sl_ = split(imag * (1.0 - special))
            ch, cl = split(imag * special - real * (1.0 - special))
            left_h = jnp.concatenate([rh, ih], axis=1)
            left_l = jnp.concatenate([rl, il], axis=1)
            right_h = jnp.concatenate(
                [jnp.concatenate([rh, sh_], axis=1), jnp.concatenate([sh_, ch], axis=1)], axis=0
            )
            right_l = jnp.concatenate(
                [jnp.concatenate([rl, sl_], axis=1), jnp.concatenate([sl_, cl], axis=1)], axis=0
            )
            grams.append(
                dot_nt(left_h, right_h) + (dot_nt(left_h, right_l) + dot_nt(left_l, right_h))
            )
        pair = jnp.concatenate(grams, axis=1)

        @pl.when(i < 7)
        def _():
            go[zt] = pair
            pltpu.make_async_remote_copy(
                go.at[zt], gr.at[z], s3, r3,
                device_id=((y << 4) + (zt << 1) + c, sx), device_id_type=MESH,
            ).start()

        @pl.when(i == 7)
        def _():
            gr[z] = pair

    pltpu.make_async_copy(gr.at[pl.ds(0, 7)], gr.at[pl.ds(0, 7)], r3).wait()
    gram = gr[0]
    for k in range(1, 8):
        gram = gram + gr[k]
    gram = gram * (1.0 / 2048.0)

    even = row % 2 == 0
    lone = (row < 2) & (unit == 0) & (z == 0)
    valid = (lane < 32) & (row < 4)

    def swap_rows(v):
        return jnp.where(even, pltpu.roll(v, 7, 0), pltpu.roll(v, 1, 0))

    def image_of(v):
        product = jnp.dot(v[:, 0:32], gram, preferred_element_type=F32, precision=HIGHEST)
        chosen = jnp.where(row < 2, product, pltpu.roll(product, 64, 1))
        other = pltpu.roll(chosen, 96, 1)
        crossed = swap_rows(other)
        normal = jnp.where(even, chosen + crossed, chosen - crossed)
        alone = jnp.where(even, chosen, other)
        return jnp.where(valid, jnp.where(lone, alone, normal), 0.0)

    def pair_sum(v):
        total = jnp.broadcast_to(jnp.sum(v, axis=1, keepdims=True), (8, 128))
        return jnp.where(lone, total, total + swap_rows(total))

    vec = jnp.where(valid & (even | lone), 1.0 / math.sqrt(32.0), 0.0).astype(F32)
    for _ in range(POWER):
        new = image_of(vec)
        vec = new * lax.rsqrt(pair_sum(new * new) + 1e-06)
    energy = pair_sum(vec * image_of(vec))
    scaled = vec * lax.rsqrt(energy + 1e-06)
    spread = scaled + pltpu.roll(scaled, 32, 1)
    spread = spread + pltpu.roll(spread, 64, 1)
    placed = lane // 32 == row
    vec_row = jnp.sum(jnp.where(placed, spread, 0.0), axis=0, keepdims=True)
    energy_row = jnp.sum(jnp.where(placed, energy, 0.0), axis=0, keepdims=True)
    message = jnp.where(row == 0, vec_row, jnp.where(row == 1, energy_row, 0.0))
    vs[...] = message
    va[z] = message

    @pl.loop(0, 7)
    def _(i):
        zt = far_first(z, i)
        pltpu.make_async_remote_copy(
            vs, va.at[z], s4, r4,
            device_id=((y << 4) + (zt << 1) + c, sx), device_id_type=MESH,
        ).start()

    rows = lax.broadcasted_iota(jnp.int32, (64, 128), 0)
    lanes = lax.broadcasted_iota(jnp.int32, (64, 128), 1)
    ver, ri, j = rows // 32, (rows // 16) % 2, rows % 16
    first_unit = unit == 0
    slot = jnp.where(ver == 0, j, 15 - j)
    slot_first = jnp.where(
        ver == 0,
        jnp.where(j < 8, j, jnp.where(j == 8, 0, 16 - j)),
        jnp.where(j < 8, 8 + j, 23 - j),
    )
    slot = jnp.where(first_unit, slot_first, slot)
    mirrored = jnp.where(first_unit, j // 8, ver) == 1
    direct = first_unit & (ver == 0) & (j == 0)
    nyquist = first_unit & (ver == 0) & (j == 8)
    lane_imag = (lanes // 32) % 2 == 1
    lane_slot = lanes // 64
    straight = jnp.where(
        direct, jnp.where(lane_imag, 0.0, 1.0),
        jnp.where(nyquist, jnp.where(lane_imag, 1.0, 0.0), jnp.where(lane_imag, -1.0, 1.0)),
    )
    straight = jnp.where(ri == 0, straight, 0.0).astype(F32)
    across = jnp.where(direct | nyquist, 0.0, jnp.where(mirrored, -1.0, 1.0))
    across = jnp.where(ri == 0, 0.0, across).astype(F32)
    picked = lanes % 64 == jnp.where(nyquist, 32, 0)

    pltpu.make_async_copy(va.at[pl.ds(0, 7)], va.at[pl.ds(0, 7)], r4).wait()

    modes = jnp.zeros((64, 256), F32)
    energies = jnp.zeros((64, 128), F32)
    imag_row = (lax.broadcasted_iota(jnp.int32, (1, 128), 1) // 32) % 2 == 1
    for k in range(8):
        v = va[k, 0:1, :]
        e = va[k, 1:2, :]
        v_swapped = jnp.where(imag_row, pltpu.roll(v, 32, 1), pltpu.roll(v, 96, 1))
        here = slot == 2 * k + lane_slot
        left = jnp.where(here, straight * v + across * v_swapped, 0.0)
        energies = energies + jnp.where(here & picked, e, 0.0)
        lh, ll = split(left)
        high = mh[128 * k : 128 * k + 128, :]
        modes = modes + (dot(lh, high) + (dot(lh, ml[128 * k : 128 * k + 128, :]) + dot(ll, high)))
    energies = jnp.broadcast_to(jnp.sum(energies, axis=1, keepdims=True), (64, 128))

    sends = []
    for ver in range(2):
        if ver == 0:
            klass = unit
        else:
            klass = jnp.where(unit == 0, 32, 64 - unit)
        to = bit_reverse(klass)
        base = 32 * ver
        energy_tile = jnp.where(low, energies[base : base + 8], energies[base + 8 : base + 16])
        for px in range(4):
            n = ver * 4 + px
            q = 128 * (px // 2)
            for ri in range(2):
                a = modes[base + 16 * ri : base + 16 * ri + 8, q : q + 128]
                b = modes[base + 16 * ri + 8 : base + 16 * ri + 16, q : q + 128]
                if px % 2 == 0:
                    tile = jnp.where(low, a, pltpu.roll(b, 64, 1))
                else:
                    tile = jnp.where(low, pltpu.roll(a, 64, 1), b)
                fs[n, 8 * ri : 8 * ri + 8, :] = tile
            fs[n, 16:24, :] = energy_tile
            send = pltpu.make_async_remote_copy(
                fs.at[n], fb.at[z], s5.at[n], r5.at[z],
                device_id=(to, px), device_id_type=MESH,
            )
            kept = (to == me) & (px == sx)
            sends.append((send, kept))

            @pl.when(jnp.logical_not(kept))
            def _():
                send.start()

            @pl.when(kept)
            def _():
                fb[z] = fs[n]

    mine = bit_reverse(me)
    my_unit = jnp.where(mine == 32, 0, jnp.where(mine > 32, 64 - mine, mine))
    same_group = my_unit == unit
    for k in range(8):

        @pl.when(jnp.logical_not(same_group & (z == k)))
        def _():
            pltpu.make_async_copy(fb.at[k], fb.at[k], r5.at[k]).wait()

    for k in range(8):
        out_ref[k] = fb[k]

    for h in range(2):
        pltpu.make_async_copy(sb.at[h, pl.ds(0, 63)], sb.at[h, pl.ds(0, 63)], s1.at[h]).wait()
    pltpu.make_async_copy(db.at[pl.ds(0, 62 * 32)], db.at[pl.ds(0, 62 * 32)], s2).wait()
    pltpu.make_async_copy(gr.at[pl.ds(0, 7)], gr.at[pl.ds(0, 7)], s3).wait()
    pltpu.make_async_copy(va.at[pl.ds(0, 7)], va.at[pl.ds(0, 7)], s4).wait()
    for send, kept in sends:

        @pl.when(jnp.logical_not(kept))
        def _():
            send.wait_send()


def unpack(fb, w_ref, out_ref, e_ref):
    lane = lax.broadcasted_iota(jnp.int32, (8, 128), 1)
    row = lax.broadcasted_iota(jnp.int32, (8, 128), 0)
    low = lane < 64
    unscale = lax.rsqrt(w_ref[...])
    for q in range(4):
        for ri in range(2):
            a = fb[2 * q, 8 * ri : 8 * ri + 8, :]
            b = fb[2 * q + 1, 8 * ri : 8 * ri + 8, :]
            first, second = interleave(a, b, low)
            scale = unscale[:, 128 * q : 128 * q + 128]
            out_ref[16 * ri : 16 * ri + 8, 128 * q : 128 * q + 128] = first * scale
            out_ref[16 * ri + 8 : 16 * ri + 16, 128 * q : 128 * q + 128] = second * scale
    tile = fb[0, 16:24, :]
    turned = pltpu.roll(tile, 64, 1)
    diagonal = jnp.where(lane == row, tile, 0.0) + jnp.where(lane == row + 8, turned, 0.0)
    e_ref[...] = jnp.sum(diagonal, axis=0, keepdims=True)[:, 0:16]


def body(snapshots, quad_weights):
    times, blocks, points = snapshots.shape
    table = jnp.asarray(transform_table())
    any_spec = pl.BlockSpec(memory_space=pl.ANY)
    vmem = pl.BlockSpec(memory_space=pltpu.VMEM)
    dma = pltpu.SemaphoreType.DMA
    weights = quad_weights.reshape(1, points)
    packed = pl.pallas_call(
        kernel,
        out_shape=jax.ShapeDtypeStruct((8, 24, 128), F32),
        in_specs=[any_spec, any_spec, vmem],
        out_specs=vmem,
        scratch_shapes=[
            pltpu.VMEM((4, 512, 128), F32),
            pltpu.VMEM((2, 1024, 512), BF16),
            pltpu.VMEM((2, 64, 16, 128), F32),
            pltpu.VMEM((2, 64, 16, 128), F32),
            pltpu.VMEM((2, 512, 256), BF16),
            pltpu.VMEM((2, 32, 32, 128), F32),
            pltpu.VMEM((2048, 128), F32),
            pltpu.VMEM((1024, 256), BF16),
            pltpu.VMEM((1024, 256), BF16),
            pltpu.VMEM((8, 32, 128), F32),
            pltpu.VMEM((8, 32, 128), F32),
            pltpu.VMEM((8, 128), F32),
            pltpu.VMEM((8, 8, 128), F32),
            pltpu.VMEM((8, 24, 128), F32),
            pltpu.VMEM((8, 24, 128), F32),
            dma((4,)), dma, pltpu.SemaphoreType.REGULAR,
            dma((2,)), dma((2,)),
            dma, dma, dma, dma, dma, dma,
            dma((8,)), dma((8,)),
        ],
        compiler_params=pltpu.CompilerParams(collective_id=0, has_side_effects=True),
        name="spod",
    )(snapshots.reshape(times * blocks, points), table, weights)
    modes, energies = pl.pallas_call(
        unpack,
        out_shape=(
            jax.ShapeDtypeStruct((32, points), F32),
            jax.ShapeDtypeStruct((1, 16), F32),
        ),
        in_specs=[vmem, vmem],
        out_specs=(vmem, vmem),
        name="unpack",
    )(packed, weights)
    return modes.reshape(2, 16, points), energies.reshape(16)


def solution(mesh):
    return jax.shard_map(
        body,
        mesh=mesh,
        in_specs=(P("tm", None, "space"), P("space")),
        out_specs=(P(None, "tm", "space"), P("tm")),
        check_vma=False,
    )
```

```python
import math

import jax
import jax.numpy as jnp
import numpy as np
from jax import lax
from jax.experimental import pallas as pl
from jax.experimental.pallas import tpu as pltpu
from jax.sharding import PartitionSpec as P

POWER = 3
F32 = jnp.float32
BF16 = jnp.bfloat16
MESH = pl.DeviceIdType.MESH
HIGHEST = lax.Precision.HIGHEST
NT = 1024
NX, NY, NZ, NC = 4, 4, 8, 2


def transform_table():
    t = np.arange(NT // 2).reshape(32, 2, 8).transpose(1, 0, 2).reshape(-1)
    rows = []
    for unit in list(range(0, 32, 2)) + list(range(1, 32, 2)):
        if unit == 0:
            freq = np.array([64 * j for j in range(8)] + [32 + 64 * j for j in range(8)])
        else:
            freq = unit + 64 * np.arange(16)
        angle = 2.0 * np.pi * ((freq[:, None] * t[None, :]) % NT) / NT
        real, imag = np.cos(angle), -np.sin(angle)
        if unit == 0:
            imag[0] = np.cos(np.pi * t)
        rows += [real, imag]
    table = np.concatenate(rows).astype(np.float32)
    high = table.astype(jnp.bfloat16)
    low = (table - high.astype(np.float32)).astype(jnp.bfloat16)
    return np.stack([high, low])


def split(x):
    high = x.astype(BF16)
    return high, (x - high.astype(F32)).astype(BF16)


def dot(a, b):
    return jnp.dot(a, b, preferred_element_type=F32)


def dot_nt(a, b):
    return lax.dot_general(a, b, (((1,), (1,)), ((), ())), preferred_element_type=F32)


def interleave(first, second, low):
    crossed = pltpu.roll(jnp.where(low, second, first), 64, 1)
    return jnp.where(low, first, crossed), jnp.where(low, crossed, second)


def bit_reverse(value):
    result = 0
    for position in range(6):
        result = result + ((value >> position) & 1) * (1 << (5 - position))
    return result


def unit_of(x, y, c):
    return c * 16 + x * 4 + ((y & 1) << 1) + (y >> 1)


def far_first(z, i):
    return (z + jnp.where((i & 1) == 1, 4 - ((i + 1) >> 1), 4 + (i >> 1))) & 7


def kernel(
    x_hbm, tab_hbm, w_ref, out_ref,
    xin, tab, sb, rb, eh, ob, db, mh, ml, go, gr, vs, va, fs, fb,
    in_sem, tab_sem, row_sem, s1, r1, s2, r2, s3, r3, s4, r4, s5, r5,
):
    me = lax.axis_index("tm")
    sx = lax.axis_index("space")
    y, z, c = me >> 4, (me >> 1) & 7, me & 1
    p = y * 2 + c
    unit = unit_of(sx, y, c)

    loads = [
        pltpu.make_async_copy(x_hbm.at[:, pl.ds(q * 128, 128)], xin.at[q], in_sem.at[q])
        for q in range(4)
    ]
    for load in loads:
        load.start()
    load_tab = pltpu.make_async_copy(tab_hbm, tab, tab_sem)
    load_tab.start()

    barrier = pltpu.get_barrier_semaphore()

    def greet(semaphore, tm, space):
        pl.semaphore_signal(semaphore, 1, device_id=(tm, space), device_id_type=MESH)

    @pl.loop(1, 16)
    def _(k):
        greet(barrier, (me & 48) + ((me + k) & 15), sx)

    @pl.loop(1, 4)
    def _(k):
        greet(barrier, (me + 16 * k) & 63, sx)
        greet(barrier, me, (sx + k) & 3)

    def peer(k):
        return (sx + k) & 3, (y + (k >> 3)) & 3, c ^ ((k >> 2) & 1)

    lane = lax.broadcasted_iota(jnp.int32, (8, 128), 1)
    row = lax.broadcasted_iota(jnp.int32, (8, 128), 0)
    low = lane < 64
    root_w = jnp.sqrt(w_ref[...])
    for load in loads:
        load.wait()
    factor = []
    for sh in range(2):
        phase = (row + (16 * me + 8 * sh - NT // 2)).astype(F32) * (math.pi / NT)
        square = phase * phase
        cosine = jnp.full((8, 128), 1.0 / math.factorial(16), F32)
        for n in range(14, -1, -2):
            cosine = cosine * square + (-1.0) ** (n // 2) / math.factorial(n)
        window = cosine * cosine * (1.0 / math.sqrt(0.375 * NT))
        factor.append([window * root_w[:, 128 * q : 128 * q + 128] for q in range(4)])

    @pl.loop(0, 32)
    def _(b):
        owner = b >> 2
        base = (owner >> 1) * 16 + (owner & 1)
        for q in range(4):
            t0 = xin[q, pl.ds(b, 8, stride=32), :] * factor[0][q]
            t1 = xin[q, pl.ds(256 + b, 8, stride=32), :] * factor[1][q]
            even, odd = interleave(t0, t1, low)
            sb[b & 3, base + 4 * q] = even
            sb[b & 3, base + 4 * q + 2] = odd

    pl.semaphore_wait(barrier, 15 + 3 + 3)
    for k in range(1, 4):
        greet(row_sem, (me + 16 * k) & 63, sx)

    def send_columns(h):
        def send(k):
            i = k & 7
            dz = jnp.where((i & 1) == 1, (i + 1) >> 1, 8 - (i >> 1))
            to = (((y + (k >> 4)) & 3) << 4) + (((z + dz) & 7) << 1) + (c ^ ((k >> 3) & 1))
            pltpu.make_async_remote_copy(
                sb.at[h, to], rb.at[h, me], s1.at[h], r1.at[h],
                device_id=(to, sx), device_id_type=MESH,
            ).start()

        return send

    pl.loop(1, 16)(send_columns(0))
    pl.semaphore_wait(row_sem, 3)
    pl.loop(16, 64)(send_columns(0))
    for h in range(1, 4):
        pl.loop(1, 64)(send_columns(h))

    for h in range(4):
        rb[h, me] = sb[h, me]

    load_tab.wait()
    low64 = lax.broadcasted_iota(jnp.int32, (64, 128), 1) < 64
    low16 = lax.broadcasted_iota(jnp.int32, (16, 128), 1) < 64
    for h in range(4):
        pltpu.make_async_copy(rb.at[h, pl.ds(0, 63)], rb.at[h, pl.ds(0, 63)], r1.at[h]).wait()

        @pl.loop(0, 4)
        def _(i):
            first = rb[h, pl.ds(i * 8, 8)].reshape(64, 128)
            second = rb[h, pl.ds(32 + i * 8, 8)].reshape(64, 128)
            for parity, value in enumerate((first + second, first - second)):
                high = value.astype(BF16).astype(F32)
                early, late = interleave(high, value - high, low64)
                eh[parity, pl.ds(i * 64, 64), :] = early.astype(BF16)
                eh[parity, pl.ds(256 + i * 64, 64), :] = late.astype(BF16)

        @pl.loop(0, 8)
        def _(i):
            data = eh[i >> 2]
            total = dot(tab[0, pl.ds(i * 128, 128), :], data)
            total = total + dot(tab[1, pl.ds(i * 128, 128), :], data)
            total = total + pltpu.roll(total, 64, 1)
            for n in range(4):
                ob[h, i * 4 + n] = jnp.where(
                    low16, total[32 * n : 32 * n + 16], total[32 * n + 16 : 32 * n + 32]
                )

        here = pl.ds(pl.multiple_of((sx * 32 + 4 * p + h) * 16, 16), 16)

        @pl.loop(1, 32)
        def _(k):
            px, py, pc = peer(k)
            g = unit_of(px, py, pc)
            pltpu.make_async_remote_copy(
                ob.at[h, (g & 1) * 16 + (g >> 1)], db.at[here], s2, r2,
                device_id=((py << 4) + (z << 1) + pc, px), device_id_type=MESH,
            ).start()

        db[here, :] = ob[h, (unit & 1) * 16 + (unit >> 1)]

    pltpu.make_async_copy(db.at[pl.ds(0, 124 * 16)], db.at[pl.ds(0, 124 * 16)], r2).wait()

    low32 = lax.broadcasted_iota(jnp.int32, (32, 128), 1) < 64

    @pl.loop(0, 8)
    def _(i):
        zt = far_first(z, i)
        grams = []
        for f in range(2):
            j = zt * 2 + f
            special = jnp.where((unit == 0) & (j == 0), 1.0, 0.0).astype(F32)
            left, same, across = [], [], []
            for x in range(NX):
                tile = db[pl.ds(x * 512 + j, 32, stride=16), :]
                turned = pltpu.roll(tile, 64, 1)
                left.append(tile)
                same.append(jnp.where(low32, tile, tile * (1.0 - special)))
                across.append(
                    jnp.where(
                        low32,
                        turned * (1.0 - special),
                        tile * special - turned * (1.0 - special),
                    )
                )
            left_h, left_l = split(jnp.concatenate(left, axis=1))
            base = pl.multiple_of(j * 32, 32)
            mh[pl.ds(base, 32), :] = left_h
            ml[pl.ds(base, 32), :] = left_l
            right = jnp.concatenate(
                [jnp.concatenate(same, axis=1), jnp.concatenate(across, axis=1)], axis=0
            )
            right_h, right_l = split(right)
            grams.append(
                dot_nt(left_h, right_h) + (dot_nt(left_h, right_l) + dot_nt(left_l, right_h))
            )
        pair = jnp.concatenate(grams, axis=1)

        @pl.when(i < 7)
        def _():
            go[zt] = pair
            pltpu.make_async_remote_copy(
                go.at[zt], gr.at[z], s3, r3,
                device_id=((y << 4) + (zt << 1) + c, sx), device_id_type=MESH,
            ).start()

        @pl.when(i == 7)
        def _():
            gr[z] = pair

    pltpu.make_async_copy(gr.at[pl.ds(0, 7)], gr.at[pl.ds(0, 7)], r3).wait()
    gram = gr[0]
    for k in range(1, 8):
        gram = gram + gr[k]
    gram = gram * (1.0 / 2048.0)

    even = row % 2 == 0
    lone = (row < 2) & (unit == 0) & (z == 0)
    valid = (lane < 32) & (row < 4)

    def swap_rows(v):
        return jnp.where(even, pltpu.roll(v, 7, 0), pltpu.roll(v, 1, 0))

    def image_of(v):
        product = jnp.dot(v[:, 0:32], gram, preferred_element_type=F32, precision=HIGHEST)
        chosen = jnp.where(row < 2, product, pltpu.roll(product, 64, 1))
        other = pltpu.roll(chosen, 96, 1)
        crossed = swap_rows(other)
        normal = jnp.where(even, chosen + crossed, chosen - crossed)
        alone = jnp.where(even, chosen, other)
        return jnp.where(valid, jnp.where(lone, alone, normal), 0.0)

    def pair_sum(v):
        total = jnp.broadcast_to(jnp.sum(v, axis=1, keepdims=True), (8, 128))
        return jnp.where(lone, total, total + swap_rows(total))

    vec = jnp.where(valid & (even | lone), 1.0 / math.sqrt(32.0), 0.0).astype(F32)
    for _ in range(POWER):
        new = image_of(vec)
        vec = new * lax.rsqrt(pair_sum(new * new) + 1e-06)
    energy = pair_sum(vec * image_of(vec))
    scaled = vec * lax.rsqrt(energy + 1e-06)
    spread = scaled + pltpu.roll(scaled, 32, 1)
    spread = spread + pltpu.roll(spread, 64, 1)
    place = (z & 1) * 2 + row // 2 == lane // 32
    message = jnp.zeros((8, 128), F32)
    for n, value in enumerate((spread, spread, energy, energy)):
        chosen = jnp.where(place & (row & 1 == n % 2), value, 0.0)
        message = jnp.where(row == n, jnp.sum(chosen, axis=0, keepdims=True), message)
    vs[...] = message
    va[z] = message

    @pl.loop(0, 7)
    def _(i):
        zt = far_first(z, i)
        pltpu.make_async_remote_copy(
            vs, va.at[z], s4, r4,
            device_id=((y << 4) + (zt << 1) + c, sx), device_id_type=MESH,
        ).start()

    rows = lax.broadcasted_iota(jnp.int32, (32, 128), 0)
    lanes = lax.broadcasted_iota(jnp.int32, (32, 128), 1)
    ver, j = rows // 16, rows % 16
    first_unit = unit == 0
    slot = jnp.where(ver == 0, j, 15 - j)
    slot_first = jnp.where(
        ver == 0,
        jnp.where(j < 8, j, jnp.where(j == 8, 0, 16 - j)),
        jnp.where(j < 8, 8 + j, 23 - j),
    )
    slot = jnp.where(first_unit, slot_first, slot)
    flip = jnp.where(jnp.where(first_unit, j // 8, ver) == 1, -1.0, 1.0)
    direct = first_unit & (ver == 0) & (j == 0)
    nyquist = first_unit & (ver == 0) & (j == 8)
    alone = direct | nyquist
    by_real = jnp.where(low32, jnp.where(nyquist, 0.0, 1.0), jnp.where(alone, 0.0, flip))
    by_imag = jnp.where(
        low32,
        jnp.where(alone, jnp.where(nyquist, 1.0, 0.0), -1.0),
        jnp.where(alone, 0.0, flip),
    )
    lane_slot = lanes // 32
    lead = lanes % 32 == 0

    pltpu.make_async_copy(va.at[pl.ds(0, 7)], va.at[pl.ds(0, 7)], r4).wait()

    modes = jnp.zeros((64, 512), F32)
    energies = jnp.zeros((32, 128), F32)
    for k in range(4):
        v = va[2 * k] + va[2 * k + 1]
        here = slot == 4 * k + lane_slot
        left = jnp.concatenate(
            [jnp.where(here, v[0:1, :], 0.0), jnp.where(here, v[1:2, :], 0.0)], axis=0
        )
        energy = jnp.where(nyquist, v[3:4, :], v[2:3, :])
        energies = energies + jnp.where(here & lead, energy, 0.0)
        lh, ll = split(left)
        high = mh[128 * k : 128 * k + 128, :]
        modes = modes + (dot(lh, high) + (dot(lh, ml[128 * k : 128 * k + 128, :]) + dot(ll, high)))
    energies = jnp.broadcast_to(jnp.sum(energies, axis=1, keepdims=True), (32, 128))

    sends = []
    for ver in range(2):
        if ver == 0:
            klass = unit
        else:
            klass = jnp.where(unit == 0, 32, 64 - unit)
        to = bit_reverse(klass)
        base = 16 * ver
        energy_tile = jnp.where(low, energies[base : base + 8], energies[base + 8 : base + 16])
        for px in range(4):
            n = ver * 4 + px
            real = modes[base : base + 16, 128 * px : 128 * px + 128]
            imag = modes[base + 32 : base + 48, 128 * px : 128 * px + 128]
            fs[n, 0:16, :] = (
                real * by_real[base : base + 16]
                + pltpu.roll(imag, 64, 1) * by_imag[base : base + 16]
            )
            fs[n, 16:24, :] = energy_tile
            send = pltpu.make_async_remote_copy(
                fs.at[n], fb.at[z], s5.at[n], r5.at[z],
                device_id=(to, px), device_id_type=MESH,
            )
            kept = (to == me) & (px == sx)
            sends.append((send, kept))

            @pl.when(jnp.logical_not(kept))
            def _():
                send.start()

            @pl.when(kept)
            def _():
                fb[z] = fs[n]

    mine = bit_reverse(me)
    my_unit = jnp.where(mine == 32, 0, jnp.where(mine > 32, 64 - mine, mine))
    same_group = my_unit == unit
    for k in range(8):

        @pl.when(jnp.logical_not(same_group & (z == k)))
        def _():
            pltpu.make_async_copy(fb.at[k], fb.at[k], r5.at[k]).wait()

    for k in range(8):
        out_ref[k] = fb[k]

    for h in range(4):
        pltpu.make_async_copy(sb.at[h, pl.ds(0, 63)], sb.at[h, pl.ds(0, 63)], s1.at[h]).wait()
    pltpu.make_async_copy(db.at[pl.ds(0, 124 * 16)], db.at[pl.ds(0, 124 * 16)], s2).wait()
    pltpu.make_async_copy(gr.at[pl.ds(0, 7)], gr.at[pl.ds(0, 7)], s3).wait()
    pltpu.make_async_copy(va.at[pl.ds(0, 7)], va.at[pl.ds(0, 7)], s4).wait()
    for send, kept in sends:

        @pl.when(jnp.logical_not(kept))
        def _():
            send.wait_send()


def unpack(fb, w_ref, out_ref, e_ref):
    lane = lax.broadcasted_iota(jnp.int32, (8, 128), 1)
    row = lax.broadcasted_iota(jnp.int32, (8, 128), 0)
    low16 = lax.broadcasted_iota(jnp.int32, (16, 128), 1) < 64
    unscale = lax.rsqrt(w_ref[...])
    for q in range(4):
        real, imag = interleave(fb[2 * q, 0:16, :], fb[2 * q + 1, 0:16, :], low16)
        scale = unscale[:, 128 * q : 128 * q + 128]
        out_ref[0:16, 128 * q : 128 * q + 128] = real * scale
        out_ref[16:32, 128 * q : 128 * q + 128] = imag * scale
    tile = fb[0, 16:24, :]
    turned = pltpu.roll(tile, 64, 1)
    diagonal = jnp.where(lane == row, tile, 0.0) + jnp.where(lane == row + 8, turned, 0.0)
    e_ref[...] = jnp.sum(diagonal, axis=0, keepdims=True)[:, 0:16]


def body(snapshots, quad_weights):
    times, blocks, points = snapshots.shape
    table = jnp.asarray(transform_table())
    any_spec = pl.BlockSpec(memory_space=pl.ANY)
    vmem = pl.BlockSpec(memory_space=pltpu.VMEM)
    dma = pltpu.SemaphoreType.DMA
    weights = quad_weights.reshape(1, points)
    packed = pl.pallas_call(
        kernel,
        out_shape=jax.ShapeDtypeStruct((8, 24, 128), F32),
        in_specs=[any_spec, any_spec, vmem],
        out_specs=vmem,
        scratch_shapes=[
            pltpu.VMEM((4, 512, 128), F32),
            pltpu.VMEM((2, 1024, 512), BF16),
            pltpu.VMEM((4, 64, 8, 128), F32),
            pltpu.VMEM((4, 64, 8, 128), F32),
            pltpu.VMEM((2, 512, 128), BF16),
            pltpu.VMEM((4, 32, 16, 128), F32),
            pltpu.VMEM((2048, 128), F32),
            pltpu.VMEM((512, 512), BF16),
            pltpu.VMEM((512, 512), BF16),
            pltpu.VMEM((8, 32, 128), F32),
            pltpu.VMEM((8, 32, 128), F32),
            pltpu.VMEM((8, 128), F32),
            pltpu.VMEM((8, 8, 128), F32),
            pltpu.VMEM((8, 24, 128), F32),
            pltpu.VMEM((8, 24, 128), F32),
            dma((4,)), dma, pltpu.SemaphoreType.REGULAR,
            dma((4,)), dma((4,)),
            dma, dma, dma, dma, dma, dma,
            dma((8,)), dma((8,)),
        ],
        compiler_params=pltpu.CompilerParams(collective_id=0, has_side_effects=True),
        name="spod",
    )(snapshots.reshape(times * blocks, points), table, weights)
    modes, energies = pl.pallas_call(
        unpack,
        out_shape=(
            jax.ShapeDtypeStruct((32, points), F32),
            jax.ShapeDtypeStruct((1, 16), F32),
        ),
        in_specs=[vmem, vmem],
        out_specs=(vmem, vmem),
        name="unpack",
    )(packed, weights)
    return modes.reshape(2, 16, points), energies.reshape(16)


def solution(mesh):
    return jax.shard_map(
        body,
        mesh=mesh,
        in_specs=(P("tm", None, "space"), P("space")),
        out_specs=(P(None, "tm", "space"), P("tm")),
        check_vma=False,
    )
```

```python
import math

import jax
import jax.numpy as jnp
import numpy as np
from jax import lax
from jax.experimental import pallas as pl
from jax.experimental.pallas import tpu as pltpu
from jax.sharding import PartitionSpec as P

POWER = 3
F32 = jnp.float32
BF16 = jnp.bfloat16
MESH = pl.DeviceIdType.MESH
HIGHEST = lax.Precision.HIGHEST
NT = 1024
NX, NY, NZ, NC = 4, 4, 8, 2


def transform_table():
    t = np.arange(NT // 2).reshape(32, 2, 8).transpose(1, 0, 2).reshape(-1)
    rows = []
    for unit in list(range(0, 32, 2)) + list(range(1, 32, 2)):
        if unit == 0:
            freq = np.array([64 * j for j in range(8)] + [32 + 64 * j for j in range(8)])
        else:
            freq = unit + 64 * np.arange(16)
        angle = 2.0 * np.pi * ((freq[:, None] * t[None, :]) % NT) / NT
        real, imag = np.cos(angle), -np.sin(angle)
        if unit == 0:
            imag[0] = np.cos(np.pi * t)
        rows += [real, imag]
    table = np.concatenate(rows).astype(np.float32)
    high = table.astype(jnp.bfloat16)
    low = (table - high.astype(np.float32)).astype(jnp.bfloat16)
    return np.stack([high, low])


def split(x):
    high = x.astype(BF16)
    return high, (x - high.astype(F32)).astype(BF16)


def dot(a, b):
    return jnp.dot(a, b, preferred_element_type=F32)


def dot_nt(a, b):
    return lax.dot_general(a, b, (((1,), (1,)), ((), ())), preferred_element_type=F32)


def interleave(first, second, low):
    crossed = pltpu.roll(jnp.where(low, second, first), 64, 1)
    return jnp.where(low, first, crossed), jnp.where(low, crossed, second)


def bit_reverse(value):
    result = 0
    for position in range(6):
        result = result + ((value >> position) & 1) * (1 << (5 - position))
    return result


def unit_of(x, y, c):
    return c * 16 + x * 4 + ((y & 1) << 1) + (y >> 1)


def far_first(z, i):
    return (z + jnp.where((i & 1) == 1, 4 - ((i + 1) >> 1), 4 + (i >> 1))) & 7


def kernel(
    x_hbm, tab_hbm, w_ref, out_ref,
    xin, tab, sb, rb, eh, ob, db, mh, ml, go, gr, vs, va, fs, fb,
    in_sem, tab_sem, step_sem, s1, r1, s2, r2, s3, r3, s4, r4, s5, r5,
):
    me = lax.axis_index("tm")
    sx = lax.axis_index("space")
    y, z, c = me >> 4, (me >> 1) & 7, me & 1
    p = y * 2 + c
    unit = unit_of(sx, y, c)

    loads = [
        pltpu.make_async_copy(x_hbm.at[:, pl.ds(q * 128, 128)], xin.at[q], in_sem.at[q])
        for q in range(4)
    ]
    for load in loads:
        load.start()
    load_tab = pltpu.make_async_copy(tab_hbm, tab, tab_sem)
    load_tab.start()

    barrier = pltpu.get_barrier_semaphore()

    def greet(semaphore, tm, space):
        pl.semaphore_signal(semaphore, 1, device_id=(tm, space), device_id_type=MESH)

    def at(dz, dc):
        return (y << 4) + (((z + dz) & 7) << 1) + (c ^ dc)

    greet(barrier, me ^ 1, sx)
    for sign in (1, -1):
        greet(barrier, at(sign, 0), sx)
        greet(barrier, at(sign, 1), sx)
        greet(barrier, (me + 16 * sign) & 63, sx)
        greet(barrier, me, (sx + sign) & 3)
        greet(barrier, me ^ 1, (sx + sign) & 3)

    def peer(k):
        return (sx + k) & 3, (y + (k >> 3)) & 3, c ^ ((k >> 2) & 1)

    lane = lax.broadcasted_iota(jnp.int32, (8, 128), 1)
    row = lax.broadcasted_iota(jnp.int32, (8, 128), 0)
    low = lane < 64
    root_w = jnp.sqrt(w_ref[...])
    for load in loads:
        load.wait()
    factor = []
    for sh in range(2):
        phase = (row + (16 * me + 8 * sh - NT // 2)).astype(F32) * (math.pi / NT)
        square = phase * phase
        cosine = jnp.full((8, 128), 1.0 / math.factorial(16), F32)
        for n in range(14, -1, -2):
            cosine = cosine * square + (-1.0) ** (n // 2) / math.factorial(n)
        window = cosine * cosine * (1.0 / math.sqrt(0.375 * NT))
        factor.append([window * root_w[:, 128 * q : 128 * q + 128] for q in range(4)])

    @pl.loop(0, 32)
    def _(b):
        owner = b >> 2
        base = (owner >> 1) * 16 + (owner & 1)
        for q in range(4):
            t0 = xin[q, pl.ds(b, 8, stride=32), :] * factor[0][q]
            t1 = xin[q, pl.ds(256 + b, 8, stride=32), :] * factor[1][q]
            even, odd = interleave(t0, t1, low)
            sb[base + 4 * q, b & 3] = even
            sb[base + 4 * q + 2, b & 3] = odd

    groups = (pl.ds(0, 2), pl.ds(2, 1), pl.ds(3, 1))

    def send_columns(group, to):
        pltpu.make_async_remote_copy(
            sb.at[to, groups[group]], rb.at[me, groups[group]], s1.at[group], r1.at[group],
            device_id=(to, sx), device_id_type=MESH,
        ).start()

    def send_row(group, offsets):
        for dz, dc in offsets:
            send_columns(group, at(dz, dc))

    def target(k):
        i, row_step = k & 7, k >> 4
        dz = jnp.where((i & 1) == 1, (i + 1) >> 1, 8 - (i >> 1))
        dy = jnp.where(row_step == 1, 1, 5 - row_step)
        return (((y + dy) & 3) << 4) + (((z + dz) & 7) << 1) + (c ^ ((k >> 3) & 1))

    near = [(1, 0), (-1, 0), (1, 1), (-1, 1), (0, 1)]
    second = [(2, 0), (-2, 0), (2, 1), (-2, 1)]
    far = [(3, 0), (-3, 0), (4, 0), (3, 1), (-3, 1), (4, 1)]

    pl.semaphore_wait(barrier, 11)
    for sign in (1, -1):
        greet(step_sem.at[0], at(sign, 0), sx)
        greet(step_sem.at[1], me, (sx + sign) & 3)
    send_row(0, near)
    pl.semaphore_wait(step_sem.at[0], 2)
    for sign in (2, -2):
        greet(step_sem.at[2], at(sign, 0), sx)
    send_row(0, second)
    send_row(1, near)
    send_row(2, near)
    pl.semaphore_wait(step_sem.at[2], 2)
    pl.semaphore_wait(step_sem.at[1], 2)
    for sign in (1, -1):
        greet(step_sem.at[3], (me + 16 * sign) & 63, sx)
    send_row(0, far)
    pl.semaphore_wait(step_sem.at[3], 2)
    for sign in (1, -1):
        greet(step_sem.at[4], (me + 16 * sign) & 63, sx)

    @pl.loop(16, 48)
    def _(k):
        send_columns(0, target(k))

    pl.semaphore_wait(step_sem.at[4], 2)

    @pl.loop(48, 64)
    def _(k):
        send_columns(0, target(k))

    for group in (1, 2):
        send_row(group, second + far)

        @pl.loop(16, 64)
        def _(k):
            send_columns(group, target(k))

    rb[me] = sb[me]

    load_tab.wait()
    low64 = lax.broadcasted_iota(jnp.int32, (64, 128), 1) < 64
    low16 = lax.broadcasted_iota(jnp.int32, (16, 128), 1) < 64
    for h in range(4):
        if h != 1:
            landed = rb.at[pl.ds(0, 63), groups[max(h - 1, 0)]]
            pltpu.make_async_copy(landed, landed, r1.at[max(h - 1, 0)]).wait()

        @pl.loop(0, 4)
        def _(i):
            first = rb[pl.ds(i * 8, 8), h].reshape(64, 128)
            second = rb[pl.ds(32 + i * 8, 8), h].reshape(64, 128)
            for parity, value in enumerate((first + second, first - second)):
                high = value.astype(BF16).astype(F32)
                early, late = interleave(high, value - high, low64)
                eh[parity, pl.ds(i * 64, 64), :] = early.astype(BF16)
                eh[parity, pl.ds(256 + i * 64, 64), :] = late.astype(BF16)

        @pl.loop(0, 8)
        def _(i):
            data = eh[i >> 2]
            total = dot(tab[0, pl.ds(i * 128, 128), :], data)
            total = total + dot(tab[1, pl.ds(i * 128, 128), :], data)
            total = total + pltpu.roll(total, 64, 1)
            for n in range(4):
                ob[h, i * 4 + n] = jnp.where(
                    low16, total[32 * n : 32 * n + 16], total[32 * n + 16 : 32 * n + 32]
                )

        here = pl.ds(pl.multiple_of((sx * 32 + 4 * p + h) * 16, 16), 16)

        @pl.loop(1, 32)
        def _(k):
            px, py, pc = peer(k)
            g = unit_of(px, py, pc)
            pltpu.make_async_remote_copy(
                ob.at[h, (g & 1) * 16 + (g >> 1)], db.at[here], s2, r2,
                device_id=((py << 4) + (z << 1) + pc, px), device_id_type=MESH,
            ).start()

        db[here, :] = ob[h, (unit & 1) * 16 + (unit >> 1)]

    pltpu.make_async_copy(db.at[pl.ds(0, 124 * 16)], db.at[pl.ds(0, 124 * 16)], r2).wait()

    low32 = lax.broadcasted_iota(jnp.int32, (32, 128), 1) < 64

    @pl.loop(0, 8)
    def _(i):
        zt = far_first(z, i)
        grams = []
        for f in range(2):
            j = zt * 2 + f
            special = jnp.where((unit == 0) & (j == 0), 1.0, 0.0).astype(F32)
            left, same, across = [], [], []
            for x in range(NX):
                tile = db[pl.ds(x * 512 + j, 32, stride=16), :]
                turned = pltpu.roll(tile, 64, 1)
                left.append(tile)
                same.append(jnp.where(low32, tile, tile * (1.0 - special)))
                across.append(
                    jnp.where(
                        low32,
                        turned * (1.0 - special),
                        tile * special - turned * (1.0 - special),
                    )
                )
            left_h, left_l = split(jnp.concatenate(left, axis=1))
            base = pl.multiple_of(j * 32, 32)
            mh[pl.ds(base, 32), :] = left_h
            ml[pl.ds(base, 32), :] = left_l
            right = jnp.concatenate(
                [jnp.concatenate(same, axis=1), jnp.concatenate(across, axis=1)], axis=0
            )
            right_h, right_l = split(right)
            grams.append(
                dot_nt(left_h, right_h) + (dot_nt(left_h, right_l) + dot_nt(left_l, right_h))
            )
        pair = jnp.concatenate(grams, axis=1)

        @pl.when(i < 7)
        def _():
            go[zt] = pair
            pltpu.make_async_remote_copy(
                go.at[zt], gr.at[z], s3, r3,
                device_id=((y << 4) + (zt << 1) + c, sx), device_id_type=MESH,
            ).start()

        @pl.when(i == 7)
        def _():
            gr[z] = pair

    pltpu.make_async_copy(gr.at[pl.ds(0, 7)], gr.at[pl.ds(0, 7)], r3).wait()
    gram = gr[0]
    for k in range(1, 8):
        gram = gram + gr[k]
    gram = gram * (1.0 / 2048.0)

    even = row % 2 == 0
    lone = (row < 2) & (unit == 0) & (z == 0)
    valid = (lane < 32) & (row < 4)

    def swap_rows(v):
        return jnp.where(even, pltpu.roll(v, 7, 0), pltpu.roll(v, 1, 0))

    def image_of(v):
        product = jnp.dot(v[:, 0:32], gram, preferred_element_type=F32, precision=HIGHEST)
        chosen = jnp.where(row < 2, product, pltpu.roll(product, 64, 1))
        other = pltpu.roll(chosen, 96, 1)
        crossed = swap_rows(other)
        normal = jnp.where(even, chosen + crossed, chosen - crossed)
        alone = jnp.where(even, chosen, other)
        return jnp.where(valid, jnp.where(lone, alone, normal), 0.0)

    def pair_sum(v):
        total = jnp.broadcast_to(jnp.sum(v, axis=1, keepdims=True), (8, 128))
        return jnp.where(lone, total, total + swap_rows(total))

    vec = jnp.where(valid & (even | lone), 1.0 / math.sqrt(32.0), 0.0).astype(F32)
    for _ in range(POWER):
        new = image_of(vec)
        vec = new * lax.rsqrt(pair_sum(new * new) + 1e-06)
    energy = pair_sum(vec * image_of(vec))
    scaled = vec * lax.rsqrt(energy + 1e-06)
    spread = scaled + pltpu.roll(scaled, 32, 1)
    spread = spread + pltpu.roll(spread, 64, 1)
    place = (z & 1) * 2 + row // 2 == lane // 32
    message = jnp.zeros((8, 128), F32)
    for n, value in enumerate((spread, spread, energy, energy)):
        chosen = jnp.where(place & (row & 1 == n % 2), value, 0.0)
        message = jnp.where(row == n, jnp.sum(chosen, axis=0, keepdims=True), message)
    vs[...] = message
    va[z] = message

    @pl.loop(0, 7)
    def _(i):
        zt = far_first(z, i)
        pltpu.make_async_remote_copy(
            vs, va.at[z], s4, r4,
            device_id=((y << 4) + (zt << 1) + c, sx), device_id_type=MESH,
        ).start()

    rows = lax.broadcasted_iota(jnp.int32, (32, 128), 0)
    lanes = lax.broadcasted_iota(jnp.int32, (32, 128), 1)
    ver, j = rows // 16, rows % 16
    first_unit = unit == 0
    slot = jnp.where(ver == 0, j, 15 - j)
    slot_first = jnp.where(
        ver == 0,
        jnp.where(j < 8, j, jnp.where(j == 8, 0, 16 - j)),
        jnp.where(j < 8, 8 + j, 23 - j),
    )
    slot = jnp.where(first_unit, slot_first, slot)
    flip = jnp.where(jnp.where(first_unit, j // 8, ver) == 1, -1.0, 1.0)
    direct = first_unit & (ver == 0) & (j == 0)
    nyquist = first_unit & (ver == 0) & (j == 8)
    alone = direct | nyquist
    by_real = jnp.where(low32, jnp.where(nyquist, 0.0, 1.0), jnp.where(alone, 0.0, flip))
    by_imag = jnp.where(
        low32,
        jnp.where(alone, jnp.where(nyquist, 1.0, 0.0), -1.0),
        jnp.where(alone, 0.0, flip),
    )
    lane_slot = lanes // 32
    lead = lanes % 32 == 0

    pltpu.make_async_copy(va.at[pl.ds(0, 7)], va.at[pl.ds(0, 7)], r4).wait()

    modes = jnp.zeros((64, 512), F32)
    energies = jnp.zeros((32, 128), F32)
    for k in range(4):
        v = va[2 * k] + va[2 * k + 1]
        here = slot == 4 * k + lane_slot
        left = jnp.concatenate(
            [jnp.where(here, v[0:1, :], 0.0), jnp.where(here, v[1:2, :], 0.0)], axis=0
        )
        energy = jnp.where(nyquist, v[3:4, :], v[2:3, :])
        energies = energies + jnp.where(here & lead, energy, 0.0)
        lh, ll = split(left)
        high = mh[128 * k : 128 * k + 128, :]
        modes = modes + (dot(lh, high) + (dot(lh, ml[128 * k : 128 * k + 128, :]) + dot(ll, high)))
    energies = jnp.broadcast_to(jnp.sum(energies, axis=1, keepdims=True), (32, 128))

    sends = []
    for ver in range(2):
        if ver == 0:
            klass = unit
        else:
            klass = jnp.where(unit == 0, 32, 64 - unit)
        to = bit_reverse(klass)
        base = 16 * ver
        energy_tile = jnp.where(low, energies[base : base + 8], energies[base + 8 : base + 16])
        for px in range(4):
            n = ver * 4 + px
            real = modes[base : base + 16, 128 * px : 128 * px + 128]
            imag = modes[base + 32 : base + 48, 128 * px : 128 * px + 128]
            fs[n, 0:16, :] = (
                real * by_real[base : base + 16]
                + pltpu.roll(imag, 64, 1) * by_imag[base : base + 16]
            )
            fs[n, 16:24, :] = energy_tile
            send = pltpu.make_async_remote_copy(
                fs.at[n], fb.at[z], s5.at[n], r5.at[z],
                device_id=(to, px), device_id_type=MESH,
            )
            kept = (to == me) & (px == sx)
            sends.append((send, kept))

            @pl.when(jnp.logical_not(kept))
            def _():
                send.start()

            @pl.when(kept)
            def _():
                fb[z] = fs[n]

    mine = bit_reverse(me)
    my_unit = jnp.where(mine == 32, 0, jnp.where(mine > 32, 64 - mine, mine))
    same_group = my_unit == unit
    for k in range(8):

        @pl.when(jnp.logical_not(same_group & (z == k)))
        def _():
            pltpu.make_async_copy(fb.at[k], fb.at[k], r5.at[k]).wait()

    for k in range(8):
        out_ref[k] = fb[k]

    for group in range(3):
        left = sb.at[pl.ds(0, 63), groups[group]]
        pltpu.make_async_copy(left, left, s1.at[group]).wait()
    pltpu.make_async_copy(db.at[pl.ds(0, 124 * 16)], db.at[pl.ds(0, 124 * 16)], s2).wait()
    pltpu.make_async_copy(gr.at[pl.ds(0, 7)], gr.at[pl.ds(0, 7)], s3).wait()
    pltpu.make_async_copy(va.at[pl.ds(0, 7)], va.at[pl.ds(0, 7)], s4).wait()
    for send, kept in sends:

        @pl.when(jnp.logical_not(kept))
        def _():
            send.wait_send()


def unpack(fb, w_ref, out_ref, e_ref):
    lane = lax.broadcasted_iota(jnp.int32, (8, 128), 1)
    row = lax.broadcasted_iota(jnp.int32, (8, 128), 0)
    low16 = lax.broadcasted_iota(jnp.int32, (16, 128), 1) < 64
    unscale = lax.rsqrt(w_ref[...])
    for q in range(4):
        real, imag = interleave(fb[2 * q, 0:16, :], fb[2 * q + 1, 0:16, :], low16)
        scale = unscale[:, 128 * q : 128 * q + 128]
        out_ref[0:16, 128 * q : 128 * q + 128] = real * scale
        out_ref[16:32, 128 * q : 128 * q + 128] = imag * scale
    tile = fb[0, 16:24, :]
    turned = pltpu.roll(tile, 64, 1)
    diagonal = jnp.where(lane == row, tile, 0.0) + jnp.where(lane == row + 8, turned, 0.0)
    e_ref[...] = jnp.sum(diagonal, axis=0, keepdims=True)[:, 0:16]


def body(snapshots, quad_weights):
    times, blocks, points = snapshots.shape
    table = jnp.asarray(transform_table())
    any_spec = pl.BlockSpec(memory_space=pl.ANY)
    vmem = pl.BlockSpec(memory_space=pltpu.VMEM)
    dma = pltpu.SemaphoreType.DMA
    weights = quad_weights.reshape(1, points)
    packed = pl.pallas_call(
        kernel,
        out_shape=pltpu.VMEM((8, 24, 128), F32),
        in_specs=[any_spec, any_spec, vmem],
        out_specs=vmem,
        scratch_shapes=[
            pltpu.VMEM((4, 512, 128), F32),
            pltpu.VMEM((2, 1024, 512), BF16),
            pltpu.VMEM((64, 4, 8, 128), F32),
            pltpu.VMEM((64, 4, 8, 128), F32),
            pltpu.VMEM((2, 512, 128), BF16),
            pltpu.VMEM((4, 32, 16, 128), F32),
            pltpu.VMEM((2048, 128), F32),
            pltpu.VMEM((512, 512), BF16),
            pltpu.VMEM((512, 512), BF16),
            pltpu.VMEM((8, 32, 128), F32),
            pltpu.VMEM((8, 32, 128), F32),
            pltpu.VMEM((8, 128), F32),
            pltpu.VMEM((8, 8, 128), F32),
            pltpu.VMEM((8, 24, 128), F32),
            pltpu.VMEM((8, 24, 128), F32),
            dma((4,)), dma, pltpu.SemaphoreType.REGULAR((5,)),
            dma((3,)), dma((3,)),
            dma, dma, dma, dma, dma, dma,
            dma((8,)), dma((8,)),
        ],
        compiler_params=pltpu.CompilerParams(collective_id=0, has_side_effects=True),
        name="spod",
    )(snapshots.reshape(times * blocks, points), table, weights)
    modes, energies = pl.pallas_call(
        unpack,
        out_shape=(
            jax.ShapeDtypeStruct((32, points), F32),
            jax.ShapeDtypeStruct((1, 16), F32),
        ),
        in_specs=[vmem, vmem],
        out_specs=(vmem, vmem),
        name="unpack",
    )(pltpu.with_memory_space_constraint(packed, pltpu.VMEM), weights)
    return modes.reshape(2, 16, points), energies.reshape(16)


def solution(mesh):
    return jax.shard_map(
        body,
        mesh=mesh,
        in_specs=(P("tm", None, "space"), P("space")),
        out_specs=(P(None, "tm", "space"), P("tm")),
        check_vma=False,
    )
```

```python
import math

import jax
import jax.numpy as jnp
import numpy as np
from jax import lax
from jax.experimental import pallas as pl
from jax.experimental.pallas import tpu as pltpu
from jax.sharding import PartitionSpec as P

POWER = 3
F32 = jnp.float32
BF16 = jnp.bfloat16
MESH = pl.DeviceIdType.MESH
NT = 1024
NX, NY, NZ, NC = 4, 4, 8, 2


def transform_table():
    t = np.arange(NT // 2).reshape(32, 2, 8).transpose(1, 0, 2).reshape(-1)
    rows = []
    for unit in list(range(0, 32, 2)) + list(range(1, 32, 2)):
        if unit == 0:
            freq = np.array([64 * j for j in range(8)] + [32 + 64 * j for j in range(8)])
        else:
            freq = unit + 64 * np.arange(16)
        angle = 2.0 * np.pi * ((freq[:, None] * t[None, :]) % NT) / NT
        real, imag = np.cos(angle), -np.sin(angle)
        if unit == 0:
            imag[0] = np.cos(np.pi * t)
        rows += [real, imag]
    table = np.concatenate(rows).astype(np.float32)
    high = table.astype(jnp.bfloat16)
    low = (table - high.astype(np.float32)).astype(jnp.bfloat16)
    return np.stack([high.reshape(2, 512, 512), low.reshape(2, 512, 512)], axis=1).reshape(2, 1024, 512)


def split(x):
    high = x.astype(BF16)
    return high, (x - high.astype(F32)).astype(BF16)


def dot(a, b):
    return jnp.dot(a, b, preferred_element_type=F32)


def dot_nt(a, b):
    return lax.dot_general(a, b, (((1,), (1,)), ((), ())), preferred_element_type=F32)


def interleave(first, second, low):
    crossed = pltpu.roll(jnp.where(low, second, first), 64, 1)
    return jnp.where(low, first, crossed), jnp.where(low, crossed, second)


def bit_reverse(value):
    result = 0
    for position in range(6):
        result = result + ((value >> position) & 1) * (1 << (5 - position))
    return result


def unit_of(x, y, c):
    return c * 16 + x * 4 + ((y & 1) << 1) + (y >> 1)


def far_first(z, i):
    return (z + jnp.where((i & 1) == 1, 4 - ((i + 1) >> 1), 4 + (i >> 1))) & 7


def kernel(
    x_hbm, tab_hbm, w_ref, out_ref,
    xin, tab, sb, rb, eh, ob, db, mh, ml, go, gr, vs, va, fs, fb,
    in_sem, tab_sem, step_sem, s1, r1, s2, r2, s3, r3, s4, r4, s5, r5,
):
    me = lax.axis_index("tm")
    sx = lax.axis_index("space")
    y, z, c = me >> 4, (me >> 1) & 7, me & 1
    p = y * 2 + c
    unit = unit_of(sx, y, c)

    loads = [
        pltpu.make_async_copy(x_hbm.at[:, pl.ds(q * 128, 128)], xin.at[q], in_sem.at[q])
        for q in range(4)
    ]
    for load in loads:
        load.start()
    load_tab = pltpu.make_async_copy(tab_hbm, tab, tab_sem)
    load_tab.start()

    barrier = pltpu.get_barrier_semaphore()

    def greet(semaphore, tm, space):
        pl.semaphore_signal(semaphore, 1, device_id=(tm, space), device_id_type=MESH)

    @pl.loop(1, 16)
    def _(k):
        greet(barrier, (me & 48) + ((me + k) & 15), sx)

    @pl.loop(1, 4)
    def _(k):
        greet(barrier, (me + 16 * k) & 63, sx)
        greet(barrier, me, (sx + k) & 3)

    def peer(k):
        dx, dy = k & 3, k >> 3
        dx = jnp.where(dx < 2, 2 - dx, 3 * (3 - dx))
        dy = jnp.where(dy < 2, 2 - dy, 3 * (3 - dy))
        return (sx + dx) & 3, (y + dy) & 3, c ^ 1 ^ ((k >> 2) & 1)

    lane = lax.broadcasted_iota(jnp.int32, (8, 128), 1)
    row = lax.broadcasted_iota(jnp.int32, (8, 128), 0)
    low = lane < 64
    root_w = jnp.sqrt(w_ref[...])
    for load in loads:
        load.wait()
    factor = []
    for sh in range(2):
        phase = (row + (16 * me + 8 * sh - NT // 2)).astype(F32) * (math.pi / NT)
        square = phase * phase
        cosine = jnp.full((8, 128), 1.0 / math.factorial(16), F32)
        for n in range(14, -1, -2):
            cosine = cosine * square + (-1.0) ** (n // 2) / math.factorial(n)
        window = cosine * cosine * (1.0 / math.sqrt(0.375 * NT))
        factor.append([window * root_w[:, 128 * q : 128 * q + 128] for q in range(4)])

    @pl.loop(0, 32)
    def _(b):
        owner = b >> 2
        base = (owner >> 1) * 16 + (owner & 1)
        for q in range(4):
            t0 = xin[q, pl.ds(b, 8, stride=32), :] * factor[0][q]
            t1 = xin[q, pl.ds(256 + b, 8, stride=32), :] * factor[1][q]
            even, odd = interleave(t0, t1, low)
            sb[base + 4 * q, b & 3] = even
            sb[base + 4 * q + 2, b & 3] = odd

    groups = (pl.ds(0, 2), pl.ds(2, 1), pl.ds(3, 1))

    def send_columns(group, to):
        pltpu.make_async_remote_copy(
            sb.at[to, groups[group]], rb.at[me, groups[group]], s1.at[group], r1.at[group],
            device_id=(to, sx), device_id_type=MESH,
        ).start()

    def target(k):
        i = k & 7
        dz = jnp.where((i & 1) == 1, (i + 1) >> 1, 8 - (i >> 1))
        to = (((y + (k >> 4)) & 3) << 4) + (((z + dz) & 7) << 1)
        return to + (c ^ ((k >> 3) & 1))

    def send_rest(group):
        @pl.loop(1, 64)
        def _(k):
            send_columns(group, target(64 - k))

    pl.semaphore_wait(barrier, 15 + 3 + 3)
    for k in range(1, 4):
        greet(step_sem, (me + 16 * k) & 63, sx)

    @pl.loop(1, 16)
    def _(k):
        send_columns(0, target(k))

    pl.semaphore_wait(step_sem, 3)

    @pl.loop(16, 64)
    def _(k):
        send_columns(0, target(k))

    send_rest(1)
    send_rest(2)

    rb[me] = sb[me]

    load_tab.wait()
    low64 = lax.broadcasted_iota(jnp.int32, (64, 128), 1) < 64
    low16 = lax.broadcasted_iota(jnp.int32, (16, 128), 1) < 64
    for h in range(4):
        if h != 1:
            landed = rb.at[pl.ds(0, 63), groups[max(h - 1, 0)]]
            pltpu.make_async_copy(landed, landed, r1.at[max(h - 1, 0)]).wait()

        @pl.loop(0, 4)
        def _(i):
            first = rb[pl.ds(i * 8, 8), h].reshape(64, 128)
            second = rb[pl.ds(32 + i * 8, 8), h].reshape(64, 128)
            for parity, value in enumerate((first + second, first - second)):
                high = value.astype(BF16).astype(F32)
                early, late = interleave(high, value - high, low64)
                eh[parity, pl.ds(i * 64, 64), :] = early.astype(BF16)
                eh[parity, pl.ds(256 + i * 64, 64), :] = late.astype(BF16)

        @pl.loop(0, 2)
        def _(parity):
            product = dot(tab[parity], eh[parity])
            total = product[0:512] + product[512:1024]
            total = total + pltpu.roll(total, 64, 1)
            for n in range(16):
                ob[h, parity * 16 + n] = jnp.where(
                    low16, total[32 * n : 32 * n + 16], total[32 * n + 16 : 32 * n + 32]
                )

        here = pl.ds(pl.multiple_of((sx * 32 + 4 * p + h) * 16, 16), 16)

        @pl.loop(0, 31)
        def _(k):
            px, py, pc = peer(k)
            g = unit_of(px, py, pc)
            pltpu.make_async_remote_copy(
                ob.at[h, (g & 1) * 16 + (g >> 1)], db.at[here], s2, r2,
                device_id=((py << 4) + (z << 1) + pc, px), device_id_type=MESH,
            ).start()

        db[here, :] = ob[h, (unit & 1) * 16 + (unit >> 1)]

    pltpu.make_async_copy(db.at[pl.ds(0, 124 * 16)], db.at[pl.ds(0, 124 * 16)], r2).wait()

    low32 = lax.broadcasted_iota(jnp.int32, (32, 128), 1) < 64

    @pl.loop(0, 8)
    def _(i):
        zt = far_first(z, i)
        grams = []
        for f in range(2):
            j = zt * 2 + f
            keep = jnp.where((unit == 0) & (j == 0), 0.0, 1.0).astype(F32)
            real, imag = [], []
            for x in range(0, NX, 2):
                first = db[pl.ds(x * 512 + j, 32, stride=16), :]
                second = db[pl.ds(x * 512 + 512 + j, 32, stride=16), :]
                r, m = interleave(first, second, low32)
                real.append(r)
                imag.append(m)
            real_h, real_l = split(jnp.concatenate(real, axis=1))
            imag_h, imag_l = split(jnp.concatenate(imag, axis=1))
            left_h = jnp.concatenate([real_h, imag_h], axis=1)
            left_l = jnp.concatenate([real_l, imag_l], axis=1)
            base = pl.multiple_of(j * 32, 32)
            mh[pl.ds(base, 32), :] = left_h
            ml[pl.ds(base, 32), :] = left_l
            lone_part = (1.0 - keep).astype(BF16)
            keep = keep.astype(BF16)
            right = []
            for r, m in ((real_h, imag_h), (real_l, imag_l)):
                kept = m * keep
                right.append(jnp.concatenate([r, kept], axis=1))
                right.append(jnp.concatenate([kept, m * lone_part - r * keep], axis=1))
            product = dot_nt(
                jnp.concatenate([left_h, left_l], axis=0), jnp.concatenate(right, axis=0)
            )
            total = product[0:32] + product[32:64]
            grams.append(total + pltpu.roll(total, 64, 1))
        pair = jnp.where(low32, grams[0], grams[1])

        @pl.when(i < 7)
        def _():
            go[zt] = pair
            pltpu.make_async_remote_copy(
                go.at[zt], gr.at[z], s3, r3,
                device_id=((y << 4) + (zt << 1) + c, sx), device_id_type=MESH,
            ).start()

        @pl.when(i == 7)
        def _():
            gr[z] = pair

    pltpu.make_async_copy(gr.at[pl.ds(0, 7)], gr.at[pl.ds(0, 7)], r3).wait()
    gram = gr[0]
    for k in range(1, 8):
        gram = gram + gr[k]
    gram_h, gram_l = split(gram * (1.0 / 2048.0))
    gram = jnp.concatenate([gram_h, gram_l], axis=1)

    even = row % 2 == 0
    lone = (row < 2) & (unit == 0) & (z == 0)
    valid = (lane < 32) & (row < 4)

    def swap_rows(v):
        return jnp.where(even, pltpu.roll(v, 7, 0), pltpu.roll(v, 1, 0))

    def image_of(v):
        high = v.astype(BF16).astype(F32)
        both = jnp.where(row < 4, high, pltpu.roll(v - high, 4, 0)).astype(BF16)
        product = dot(both[:, 0:32], gram)
        product = product[:, 0:128] + product[:, 128:256]
        product = product + pltpu.roll(product, 4, 0)
        chosen = jnp.where(row < 2, product, pltpu.roll(product, 64, 1))
        other = pltpu.roll(chosen, 96, 1)
        crossed = swap_rows(other)
        normal = jnp.where(even, chosen + crossed, chosen - crossed)
        alone = jnp.where(even, chosen, other)
        return jnp.where(valid, jnp.where(lone, alone, normal), 0.0)

    def pair_sum(v):
        total = jnp.broadcast_to(jnp.sum(v, axis=1, keepdims=True), (8, 128))
        return jnp.where(lone, total, total + swap_rows(total))

    vec = jnp.where(valid & (even | lone), 1.0 / math.sqrt(32.0), 0.0).astype(F32)
    for _ in range(POWER):
        new = image_of(vec)
        vec = new * lax.rsqrt(pair_sum(new * new) + 1e-06)
    energy = pair_sum(vec * image_of(vec))
    scaled = vec * lax.rsqrt(energy + 1e-06)
    spread = scaled + pltpu.roll(scaled, 32, 1)
    spread = spread + pltpu.roll(spread, 64, 1)
    place = (z & 1) * 2 + row // 2 == lane // 32
    message = jnp.zeros((8, 128), F32)
    for n, value in enumerate((spread, spread, energy, energy)):
        chosen = jnp.where(place & (row & 1 == n % 2), value, 0.0)
        message = jnp.where(row == n, jnp.sum(chosen, axis=0, keepdims=True), message)
    vs[...] = message
    va[z] = message

    @pl.loop(0, 7)
    def _(i):
        zt = far_first(z, i)
        pltpu.make_async_remote_copy(
            vs, va.at[z], s4, r4,
            device_id=((y << 4) + (zt << 1) + c, sx), device_id_type=MESH,
        ).start()

    rows = lax.broadcasted_iota(jnp.int32, (32, 128), 0)
    lanes = lax.broadcasted_iota(jnp.int32, (32, 128), 1)
    ver, j = rows // 16, rows % 16
    first_unit = unit == 0
    slot = jnp.where(ver == 0, j, 15 - j)
    slot_first = jnp.where(
        ver == 0,
        jnp.where(j < 8, j, jnp.where(j == 8, 0, 16 - j)),
        jnp.where(j < 8, 8 + j, 23 - j),
    )
    slot = jnp.where(first_unit, slot_first, slot)
    flip = jnp.where(jnp.where(first_unit, j // 8, ver) == 1, -1.0, 1.0)
    direct = first_unit & (ver == 0) & (j == 0)
    nyquist = first_unit & (ver == 0) & (j == 8)
    alone = direct | nyquist
    real_by_real = jnp.where(nyquist, 0.0, 1.0)
    real_by_imag = jnp.where(direct, 0.0, jnp.where(nyquist, 1.0, -1.0))
    imag_by_any = jnp.where(alone, 0.0, flip)
    lane_slot = lanes // 32
    lead = lanes % 32 == 0

    pltpu.make_async_copy(va.at[pl.ds(0, 7)], va.at[pl.ds(0, 7)], r4).wait()

    modes = jnp.zeros((64, 512), F32)
    energies = jnp.zeros((32, 128), F32)
    for k in range(4):
        v = va[2 * k] + va[2 * k + 1]
        here = slot == 4 * k + lane_slot
        left = jnp.concatenate(
            [jnp.where(here, v[0:1, :], 0.0), jnp.where(here, v[1:2, :], 0.0)], axis=0
        )
        energy = jnp.where(nyquist, v[3:4, :], v[2:3, :])
        energies = energies + jnp.where(here & lead, energy, 0.0)
        lh, ll = split(left)
        high = mh[128 * k : 128 * k + 128, :]
        modes = modes + (dot(lh, high) + (dot(lh, ml[128 * k : 128 * k + 128, :]) + dot(ll, high)))
    energies = jnp.broadcast_to(jnp.sum(energies, axis=1, keepdims=True), (32, 128))

    sends = []
    for ver in range(2):
        if ver == 0:
            klass = unit
        else:
            klass = jnp.where(unit == 0, 32, 64 - unit)
        to = bit_reverse(klass)
        base = 16 * ver
        energy_tile = jnp.where(low, energies[base : base + 8], energies[base + 8 : base + 16])
        for px in range(4):
            n = ver * 4 + px
            at_real = 128 * (px // 2)
            at_imag = 256 + at_real
            part = slice(base, base + 16)
            twin = slice(base + 32, base + 48)
            real = (
                modes[part, at_real : at_real + 128] * real_by_real[part]
                + modes[twin, at_imag : at_imag + 128] * real_by_imag[part]
            )
            imag = (
                modes[part, at_imag : at_imag + 128] + modes[twin, at_real : at_real + 128]
            ) * imag_by_any[part]
            if px % 2 == 0:
                fs[n, 0:16, :] = jnp.where(low16, real, pltpu.roll(imag, 64, 1))
            else:
                fs[n, 0:16, :] = jnp.where(low16, pltpu.roll(real, 64, 1), imag)
            fs[n, 16:24, :] = energy_tile
            send = pltpu.make_async_remote_copy(
                fs.at[n], fb.at[z], s5.at[n], r5.at[z],
                device_id=(to, px), device_id_type=MESH,
            )
            kept = (to == me) & (px == sx)
            sends.append((send, kept))

            @pl.when(jnp.logical_not(kept))
            def _():
                send.start()

            @pl.when(kept)
            def _():
                fb[z] = fs[n]

    mine = bit_reverse(me)
    my_unit = jnp.where(mine == 32, 0, jnp.where(mine > 32, 64 - mine, mine))
    same_group = my_unit == unit
    for k in range(8):

        @pl.when(jnp.logical_not(same_group & (z == k)))
        def _():
            pltpu.make_async_copy(fb.at[k], fb.at[k], r5.at[k]).wait()

    for k in range(8):
        out_ref[k] = fb[k]

    for group in range(3):
        left = sb.at[pl.ds(0, 63), groups[group]]
        pltpu.make_async_copy(left, left, s1.at[group]).wait()
    pltpu.make_async_copy(db.at[pl.ds(0, 124 * 16)], db.at[pl.ds(0, 124 * 16)], s2).wait()
    pltpu.make_async_copy(gr.at[pl.ds(0, 7)], gr.at[pl.ds(0, 7)], s3).wait()
    pltpu.make_async_copy(va.at[pl.ds(0, 7)], va.at[pl.ds(0, 7)], s4).wait()
    for send, kept in sends:

        @pl.when(jnp.logical_not(kept))
        def _():
            send.wait_send()


def unpack(fb, w_ref, out_ref, e_ref):
    lane = lax.broadcasted_iota(jnp.int32, (8, 128), 1)
    row = lax.broadcasted_iota(jnp.int32, (8, 128), 0)
    low16 = lax.broadcasted_iota(jnp.int32, (16, 128), 1) < 64
    unscale = lax.rsqrt(w_ref[...])
    for q in range(4):
        real, imag = interleave(fb[2 * q, 0:16, :], fb[2 * q + 1, 0:16, :], low16)
        scale = unscale[:, 128 * q : 128 * q + 128]
        out_ref[0:16, 128 * q : 128 * q + 128] = real * scale
        out_ref[16:32, 128 * q : 128 * q + 128] = imag * scale
    tile = fb[0, 16:24, :]
    turned = pltpu.roll(tile, 64, 1)
    diagonal = jnp.where(lane == row, tile, 0.0) + jnp.where(lane == row + 8, turned, 0.0)
    e_ref[...] = jnp.sum(diagonal, axis=0, keepdims=True)[:, 0:16]


def body(snapshots, quad_weights):
    times, blocks, points = snapshots.shape
    table = jnp.asarray(transform_table())
    any_spec = pl.BlockSpec(memory_space=pl.ANY)
    vmem = pl.BlockSpec(memory_space=pltpu.VMEM)
    dma = pltpu.SemaphoreType.DMA
    weights = quad_weights.reshape(1, points)
    packed = pl.pallas_call(
        kernel,
        out_shape=pltpu.VMEM((8, 24, 128), F32),
        in_specs=[any_spec, any_spec, vmem],
        out_specs=vmem,
        scratch_shapes=[
            pltpu.VMEM((4, 512, 128), F32),
            pltpu.VMEM((2, 1024, 512), BF16),
            pltpu.VMEM((64, 4, 8, 128), F32),
            pltpu.VMEM((64, 4, 8, 128), F32),
            pltpu.VMEM((2, 512, 128), BF16),
            pltpu.VMEM((4, 32, 16, 128), F32),
            pltpu.VMEM((2048, 128), F32),
            pltpu.VMEM((512, 512), BF16),
            pltpu.VMEM((512, 512), BF16),
            pltpu.VMEM((8, 32, 128), F32),
            pltpu.VMEM((8, 32, 128), F32),
            pltpu.VMEM((8, 128), F32),
            pltpu.VMEM((8, 8, 128), F32),
            pltpu.VMEM((8, 24, 128), F32),
            pltpu.VMEM((8, 24, 128), F32),
            dma((4,)), dma, pltpu.SemaphoreType.REGULAR,
            dma((3,)), dma((3,)),
            dma, dma, dma, dma, dma, dma,
            dma((8,)), dma((8,)),
        ],
        compiler_params=pltpu.CompilerParams(collective_id=0, has_side_effects=True),
        name="spod",
    )(snapshots.reshape(times * blocks, points), table, weights)
    modes, energies = pl.pallas_call(
        unpack,
        out_shape=(
            jax.ShapeDtypeStruct((32, points), F32),
            jax.ShapeDtypeStruct((1, 16), F32),
        ),
        in_specs=[vmem, vmem],
        out_specs=(vmem, vmem),
        name="unpack",
    )(pltpu.with_memory_space_constraint(packed, pltpu.VMEM), weights)
    return modes.reshape(2, 16, points), energies.reshape(16)


def solution(mesh):
    return jax.shard_map(
        body,
        mesh=mesh,
        in_specs=(P("tm", None, "space"), P("space")),
        out_specs=(P(None, "tm", "space"), P("tm")),
        check_vma=False,
    )
```

```python
import math

import jax
import jax.numpy as jnp
import numpy as np
from jax import lax
from jax.experimental import pallas as pl
from jax.experimental.pallas import tpu as pltpu
from jax.sharding import PartitionSpec as P

POWER = 3
F32 = jnp.float32
BF16 = jnp.bfloat16
MESH = pl.DeviceIdType.MESH
NT = 1024
NX, NY, NZ, NC = 4, 4, 8, 2


def transform_table():
    t = np.arange(NT // 2).reshape(32, 2, 8).transpose(1, 0, 2).reshape(-1)
    rows = []
    for unit in list(range(0, 32, 2)) + list(range(1, 32, 2)):
        if unit == 0:
            freq = np.array([64 * j for j in range(8)] + [32 + 64 * j for j in range(8)])
        else:
            freq = unit + 64 * np.arange(16)
        angle = 2.0 * np.pi * ((freq[:, None] * t[None, :]) % NT) / NT
        real, imag = np.cos(angle), -np.sin(angle)
        if unit == 0:
            imag[0] = np.cos(np.pi * t)
        rows += [real, imag]
    table = np.concatenate(rows).astype(np.float32)
    high = table.astype(jnp.bfloat16)
    low = (table - high.astype(np.float32)).astype(jnp.bfloat16)
    return np.stack([high.reshape(2, 512, 512), low.reshape(2, 512, 512)], axis=1).reshape(2, 1024, 512)


def split(x):
    high = x.astype(BF16)
    return high, (x - high.astype(F32)).astype(BF16)


def dot(a, b):
    return jnp.dot(a, b, preferred_element_type=F32)


def dot_nt(a, b):
    return lax.dot_general(a, b, (((1,), (1,)), ((), ())), preferred_element_type=F32)


def interleave(first, second, low):
    crossed = pltpu.roll(jnp.where(low, second, first), 64, 1)
    return jnp.where(low, first, crossed), jnp.where(low, crossed, second)


def bit_reverse(value):
    result = 0
    for position in range(6):
        result = result + ((value >> position) & 1) * (1 << (5 - position))
    return result


def unit_of(x, y, c):
    return c * 16 + x * 4 + ((y & 1) << 1) + (y >> 1)


def far_first(z, i):
    return (z + jnp.where((i & 1) == 1, 4 - ((i + 1) >> 1), 4 + (i >> 1))) & 7


def kernel(
    x_hbm, tab_hbm, w_hbm, out_ref, e_ref,
    xin, w_ref, tab, sb, rb, eh, ob, db, mh, ml, go, gr, vs, va, fs, fb,
    in_sem, w_sem, tab_sem, step_sem, s1, r1, s2, r2, s3, r3, s4, r4, s5, r5,
):
    me = lax.axis_index("tm")
    sx = lax.axis_index("space")
    y, z, c = me >> 4, (me >> 1) & 7, me & 1
    p = y * 2 + c
    unit = unit_of(sx, y, c)

    loads = [
        pltpu.make_async_copy(x_hbm.at[:, pl.ds(q * 128, 128)], xin.at[q], in_sem.at[q])
        for q in range(4)
    ]
    for load in loads:
        load.start()
    load_w = pltpu.make_async_copy(w_hbm, w_ref, w_sem)
    load_w.start()
    load_tab = pltpu.make_async_copy(tab_hbm, tab, tab_sem)

    barrier = pltpu.get_barrier_semaphore()

    def greet(semaphore, tm, space):
        pl.semaphore_signal(semaphore, 1, device_id=(tm, space), device_id_type=MESH)

    @pl.loop(0, 15)
    def _(k):
        greet(barrier, (me & 48) + (far_first(z, k >> 1) << 1) + (c ^ 1 ^ (k & 1)), sx)

    @pl.loop(1, 4)
    def _(k):
        greet(barrier, (me + 16 * k) & 63, sx)
        greet(barrier, me, (sx + k) & 3)

    lane = lax.broadcasted_iota(jnp.int32, (8, 128), 1)
    row = lax.broadcasted_iota(jnp.int32, (8, 128), 0)
    low = lane < 64
    load_tab.start()
    load_w.wait()
    root_w = jnp.sqrt(w_ref[...])
    unscale = lax.rsqrt(w_ref[...])
    for load in loads:
        load.wait()
    factor = []
    for sh in range(2):
        phase = (row + (16 * me + 8 * sh - NT // 2)).astype(F32) * (math.pi / NT)
        square = phase * phase
        cosine = jnp.full((8, 128), 1.0 / math.factorial(16), F32)
        for n in range(14, -1, -2):
            cosine = cosine * square + (-1.0) ** (n // 2) / math.factorial(n)
        window = cosine * cosine * (1.0 / math.sqrt(0.375 * NT))
        factor.append([window * root_w[:, 128 * q : 128 * q + 128] for q in range(4)])

    @pl.loop(0, 32)
    def _(b):
        owner = b >> 2
        base = (owner >> 1) * 16 + (owner & 1)
        for q in range(4):
            t0 = xin[q, pl.ds(b, 8, stride=32), :] * factor[0][q]
            t1 = xin[q, pl.ds(256 + b, 8, stride=32), :] * factor[1][q]
            even, odd = interleave(t0, t1, low)
            sb[base + 4 * q, b & 3] = even
            sb[base + 4 * q + 2, b & 3] = odd

    groups = (pl.ds(0, 2), pl.ds(2, 1), pl.ds(3, 1))

    def send_columns(group, to):
        pltpu.make_async_remote_copy(
            sb.at[to, groups[group]], rb.at[me, groups[group]], s1.at[group], r1.at[group],
            device_id=(to, sx), device_id_type=MESH,
        ).start()

    def target(k):
        i = k & 7
        dz = jnp.where((i & 1) == 1, (i + 1) >> 1, 8 - (i >> 1))
        to = (((y + (k >> 4)) & 3) << 4) + (((z + dz) & 7) << 1)
        return to + (c ^ ((k >> 3) & 1))

    def send_rest(group):
        @pl.loop(1, 64)
        def _(k):
            send_columns(group, target(64 - k))

    pl.semaphore_wait(barrier, 15 + 3 + 3)
    for k in range(1, 4):
        greet(step_sem, (me + 16 * k) & 63, sx)

    @pl.loop(1, 16)
    def _(k):
        send_columns(0, target(k))

    pl.semaphore_wait(step_sem, 3)

    @pl.loop(16, 64)
    def _(k):
        send_columns(0, target(k))

    send_rest(1)
    send_rest(2)

    rb[me] = sb[me]

    load_tab.wait()
    low64 = lax.broadcasted_iota(jnp.int32, (64, 128), 1) < 64
    low16 = lax.broadcasted_iota(jnp.int32, (16, 128), 1) < 64
    for h in range(4):
        if h != 1:
            landed = rb.at[pl.ds(0, 63), groups[max(h - 1, 0)]]
            pltpu.make_async_copy(landed, landed, r1.at[max(h - 1, 0)]).wait()

        @pl.loop(0, 4)
        def _(i):
            first = rb[pl.ds(i * 8, 8), h].reshape(64, 128)
            second = rb[pl.ds(32 + i * 8, 8), h].reshape(64, 128)
            for parity, value in enumerate((first + second, first - second)):
                high = value.astype(BF16).astype(F32)
                early, late = interleave(high, value - high, low64)
                eh[parity, pl.ds(i * 64, 64), :] = early.astype(BF16)
                eh[parity, pl.ds(256 + i * 64, 64), :] = late.astype(BF16)

        here = pl.ds(pl.multiple_of((sx * 32 + 4 * p + h) * 16, 16), 16)

        @pl.loop(0, 2)
        def _(step):
            first_y = y ^ 2 ^ (3 * step)
            parity = first_y >> 1
            product = dot(tab[parity], eh[parity])
            total = product[0:512] + product[512:1024]
            total = total + pltpu.roll(total, 64, 1)
            for n in range(16):
                ob[h, parity * 16 + n] = jnp.where(
                    low16, total[32 * n : 32 * n + 16], total[32 * n + 16 : 32 * n + 32]
                )

            @pl.loop(0, 16 - step)
            def _(k):
                dx = k & 3
                dx = jnp.where(dx < 2, 2 - dx, 3 * (3 - dx))
                px, py, pc = (sx + dx) & 3, first_y ^ (k >> 3), c ^ 1 ^ ((k >> 2) & 1)
                g = unit_of(px, py, pc)
                pltpu.make_async_remote_copy(
                    ob.at[h, (g & 1) * 16 + (g >> 1)], db.at[here], s2, r2,
                    device_id=((py << 4) + (z << 1) + pc, px), device_id_type=MESH,
                ).start()

        db[here, :] = ob[h, (unit & 1) * 16 + (unit >> 1)]

    pltpu.make_async_copy(db.at[pl.ds(0, 124 * 16)], db.at[pl.ds(0, 124 * 16)], r2).wait()

    low32 = lax.broadcasted_iota(jnp.int32, (32, 128), 1) < 64

    @pl.loop(0, 8)
    def _(i):
        zt = far_first(z, i)
        grams = []
        for f in range(2):
            j = zt * 2 + f
            keep = jnp.where((unit == 0) & (j == 0), 0.0, 1.0).astype(F32)
            real, imag = [], []
            for x in range(0, NX, 2):
                first = db[pl.ds(x * 512 + j, 32, stride=16), :]
                second = db[pl.ds(x * 512 + 512 + j, 32, stride=16), :]
                r, m = interleave(first, second, low32)
                real.append(r)
                imag.append(m)
            real_h, real_l = split(jnp.concatenate(real, axis=1))
            imag_h, imag_l = split(jnp.concatenate(imag, axis=1))
            left_h = jnp.concatenate([real_h, imag_h], axis=1)
            left_l = jnp.concatenate([real_l, imag_l], axis=1)
            base = pl.multiple_of(j * 32, 32)
            mh[pl.ds(base, 32), :] = left_h
            ml[pl.ds(base, 32), :] = left_l
            lone_part = (1.0 - keep).astype(BF16)
            keep = keep.astype(BF16)
            right = []
            for r, m in ((real_h, imag_h), (real_l, imag_l)):
                kept = m * keep
                right.append(jnp.concatenate([r, kept], axis=1))
                right.append(jnp.concatenate([kept, m * lone_part - r * keep], axis=1))
            product = dot_nt(
                jnp.concatenate([left_h, left_l], axis=0), jnp.concatenate(right, axis=0)
            )
            total = product[0:32] + product[32:64]
            grams.append(total + pltpu.roll(total, 64, 1))
        pair = jnp.where(low32, grams[0], grams[1])

        @pl.when(i < 7)
        def _():
            go[zt] = pair
            pltpu.make_async_remote_copy(
                go.at[zt], gr.at[z], s3, r3,
                device_id=((y << 4) + (zt << 1) + c, sx), device_id_type=MESH,
            ).start()

        @pl.when(i == 7)
        def _():
            gr[z] = pair

    pltpu.make_async_copy(gr.at[pl.ds(0, 7)], gr.at[pl.ds(0, 7)], r3).wait()
    gram = gr[0]
    for k in range(1, 8):
        gram = gram + gr[k]
    gram_h, gram_l = split(gram * (1.0 / 2048.0))
    gram = jnp.concatenate([gram_h, gram_l], axis=1)

    even = row % 2 == 0
    lone = (row < 2) & (unit == 0) & (z == 0)
    valid = (lane < 32) & (row < 4)

    def swap_rows(v):
        return jnp.where(even, pltpu.roll(v, 7, 0), pltpu.roll(v, 1, 0))

    def image_of(v):
        high = v.astype(BF16).astype(F32)
        both = jnp.where(row < 4, high, pltpu.roll(v - high, 4, 0)).astype(BF16)
        product = dot(both[:, 0:32], gram)
        product = product[:, 0:128] + product[:, 128:256]
        product = product + pltpu.roll(product, 4, 0)
        chosen = jnp.where(row < 2, product, pltpu.roll(product, 64, 1))
        other = pltpu.roll(chosen, 96, 1)
        crossed = swap_rows(other)
        normal = jnp.where(even, chosen + crossed, chosen - crossed)
        alone = jnp.where(even, chosen, other)
        return jnp.where(valid, jnp.where(lone, alone, normal), 0.0)

    def pair_sum(v):
        total = jnp.broadcast_to(jnp.sum(v, axis=1, keepdims=True), (8, 128))
        return jnp.where(lone, total, total + swap_rows(total))

    vec = jnp.where(valid & (even | lone), 1.0 / math.sqrt(32.0), 0.0).astype(F32)
    for _ in range(POWER):
        new = image_of(vec)
        vec = new * lax.rsqrt(pair_sum(new * new) + 1e-06)
    energy = pair_sum(vec * image_of(vec))
    scaled = vec * lax.rsqrt(energy + 1e-06)
    spread = scaled + pltpu.roll(scaled, 32, 1)
    spread = spread + pltpu.roll(spread, 64, 1)
    place = (z & 1) * 2 + row // 2 == lane // 32
    message = jnp.zeros((8, 128), F32)
    for n, value in enumerate((spread, spread, energy, energy)):
        chosen = jnp.where(place & (row & 1 == n % 2), value, 0.0)
        message = jnp.where(row == n, jnp.sum(chosen, axis=0, keepdims=True), message)
    vs[...] = message
    va[z] = message

    @pl.loop(0, 7)
    def _(i):
        zt = far_first(z, i)
        pltpu.make_async_remote_copy(
            vs, va.at[z], s4, r4,
            device_id=((y << 4) + (zt << 1) + c, sx), device_id_type=MESH,
        ).start()

    rows = lax.broadcasted_iota(jnp.int32, (32, 128), 0)
    lanes = lax.broadcasted_iota(jnp.int32, (32, 128), 1)
    ver, j = rows // 16, rows % 16
    first_unit = unit == 0
    slot = jnp.where(ver == 0, j, 15 - j)
    slot_first = jnp.where(
        ver == 0,
        jnp.where(j < 8, j, jnp.where(j == 8, 0, 16 - j)),
        jnp.where(j < 8, 8 + j, 23 - j),
    )
    slot = jnp.where(first_unit, slot_first, slot)
    flip = jnp.where(jnp.where(first_unit, j // 8, ver) == 1, -1.0, 1.0)
    direct = first_unit & (ver == 0) & (j == 0)
    nyquist = first_unit & (ver == 0) & (j == 8)
    alone = direct | nyquist
    real_by_real = jnp.where(nyquist, 0.0, 1.0)
    real_by_imag = jnp.where(direct, 0.0, jnp.where(nyquist, 1.0, -1.0))
    imag_by_any = jnp.where(alone, 0.0, flip)
    lane_slot = lanes // 32
    lead = lanes % 32 == 0

    pltpu.make_async_copy(va.at[pl.ds(0, 7)], va.at[pl.ds(0, 7)], r4).wait()

    energies = jnp.zeros((32, 128), F32)
    lefts = []
    for k in range(4):
        v = va[2 * k] + va[2 * k + 1]
        here = slot == 4 * k + lane_slot
        lefts.append(
            jnp.concatenate(
                [jnp.where(here, v[0:1, :], 0.0), jnp.where(here, v[1:2, :], 0.0)], axis=0
            )
        )
        energy = jnp.where(nyquist, v[3:4, :], v[2:3, :])
        energies = energies + jnp.where(here & lead, energy, 0.0)
    lh, ll = split(jnp.concatenate(lefts, axis=1))
    modes = dot(jnp.concatenate([lh, ll], axis=0), mh[...])
    modes = modes[0:64] + (modes[64:128] + dot(lh, ml[...]))
    energies = jnp.broadcast_to(jnp.sum(energies, axis=1, keepdims=True), (32, 128))

    sends = []
    for ver in range(2):
        if ver == 0:
            klass = unit
        else:
            klass = jnp.where(unit == 0, 32, 64 - unit)
        to = bit_reverse(klass)
        base = 16 * ver
        energy_tile = jnp.where(low, energies[base : base + 8], energies[base + 8 : base + 16])
        for px in range(4):
            n = ver * 4 + px
            at_real = 128 * (px // 2)
            at_imag = 256 + at_real
            part = slice(base, base + 16)
            twin = slice(base + 32, base + 48)
            real = (
                modes[part, at_real : at_real + 128] * real_by_real[part]
                + modes[twin, at_imag : at_imag + 128] * real_by_imag[part]
            )
            imag = (
                modes[part, at_imag : at_imag + 128] + modes[twin, at_real : at_real + 128]
            ) * imag_by_any[part]
            if px % 2 == 0:
                fs[n, 0:16, :] = jnp.where(low16, real, pltpu.roll(imag, 64, 1))
            else:
                fs[n, 0:16, :] = jnp.where(low16, pltpu.roll(real, 64, 1), imag)
            fs[n, 16:24, :] = energy_tile
            send = pltpu.make_async_remote_copy(
                fs.at[n], fb.at[z], s5.at[n], r5.at[z],
                device_id=(to, px), device_id_type=MESH,
            )
            kept = (to == me) & (px == sx)
            sends.append((send, kept))

            @pl.when(jnp.logical_not(kept))
            def _():
                send.start()

            @pl.when(kept)
            def _():
                fb[z] = fs[n]

    mine = bit_reverse(me)
    my_unit = jnp.where(mine == 32, 0, jnp.where(mine > 32, 64 - mine, mine))
    same_group = my_unit == unit
    for k in range(8):

        @pl.when(jnp.logical_not(same_group & (z == k)))
        def _():
            pltpu.make_async_copy(fb.at[k], fb.at[k], r5.at[k]).wait()

    for q in range(4):
        real, imag = interleave(fb[2 * q, 0:16, :], fb[2 * q + 1, 0:16, :], low16)
        scale = unscale[:, 128 * q : 128 * q + 128]
        out_ref[0:16, 128 * q : 128 * q + 128] = real * scale
        out_ref[16:32, 128 * q : 128 * q + 128] = imag * scale
    tile = fb[0, 16:24, :]
    turned = pltpu.roll(tile, 64, 1)
    diagonal = jnp.where(lane == row, tile, 0.0) + jnp.where(lane == row + 8, turned, 0.0)
    e_ref[...] = jnp.sum(diagonal, axis=0, keepdims=True)[:, 0:16]

    for group in range(3):
        left = sb.at[pl.ds(0, 63), groups[group]]
        pltpu.make_async_copy(left, left, s1.at[group]).wait()
    pltpu.make_async_copy(db.at[pl.ds(0, 124 * 16)], db.at[pl.ds(0, 124 * 16)], s2).wait()
    pltpu.make_async_copy(gr.at[pl.ds(0, 7)], gr.at[pl.ds(0, 7)], s3).wait()
    pltpu.make_async_copy(va.at[pl.ds(0, 7)], va.at[pl.ds(0, 7)], s4).wait()
    for send, kept in sends:

        @pl.when(jnp.logical_not(kept))
        def _():
            send.wait_send()


def hand_over(modes_ref, e_ref, modes_hbm, e_hbm, sem):
    copies = [
        pltpu.make_async_copy(modes_ref, modes_hbm, sem.at[0]),
        pltpu.make_async_copy(e_ref, e_hbm, sem.at[1]),
    ]
    for copy in copies:
        copy.start()
    for copy in copies:
        copy.wait()


def body(snapshots, quad_weights):
    times, blocks, points = snapshots.shape
    table = jnp.asarray(transform_table())
    any_spec = pl.BlockSpec(memory_space=pl.ANY)
    vmem = pl.BlockSpec(memory_space=pltpu.VMEM)
    dma = pltpu.SemaphoreType.DMA
    weights = quad_weights.reshape(1, points)
    modes, energies = pl.pallas_call(
        kernel,
        out_shape=(pltpu.VMEM((32, 512), F32), pltpu.VMEM((1, 16), F32)),
        in_specs=[any_spec, any_spec, any_spec],
        out_specs=(vmem, vmem),
        scratch_shapes=[
            pltpu.VMEM((4, 512, 128), F32),
            pltpu.VMEM((1, 512), F32),
            pltpu.VMEM((2, 1024, 512), BF16),
            pltpu.VMEM((64, 4, 8, 128), F32),
            pltpu.VMEM((64, 4, 8, 128), F32),
            pltpu.VMEM((2, 512, 128), BF16),
            pltpu.VMEM((4, 32, 16, 128), F32),
            pltpu.VMEM((2048, 128), F32),
            pltpu.VMEM((512, 512), BF16),
            pltpu.VMEM((512, 512), BF16),
            pltpu.VMEM((8, 32, 128), F32),
            pltpu.VMEM((8, 32, 128), F32),
            pltpu.VMEM((8, 128), F32),
            pltpu.VMEM((8, 8, 128), F32),
            pltpu.VMEM((8, 24, 128), F32),
            pltpu.VMEM((8, 24, 128), F32),
            dma((4,)), dma, dma, pltpu.SemaphoreType.REGULAR,
            dma((3,)), dma((3,)),
            dma, dma, dma, dma, dma, dma,
            dma((8,)), dma((8,)),
        ],
        compiler_params=pltpu.CompilerParams(collective_id=0, has_side_effects=True),
        name="spod",
    )(snapshots.reshape(times * blocks, points), table, weights)
    modes, energies = pl.pallas_call(
        hand_over,
        out_shape=(
            jax.ShapeDtypeStruct((32, points), F32),
            jax.ShapeDtypeStruct((1, 16), F32),
        ),
        in_specs=[vmem, vmem],
        out_specs=(any_spec, any_spec),
        scratch_shapes=[dma((2,))],
        name="hand_over",
    )(
        pltpu.with_memory_space_constraint(modes, pltpu.VMEM),
        pltpu.with_memory_space_constraint(energies, pltpu.VMEM),
    )
    return modes.reshape(2, 16, points), energies.reshape(16)


def solution(mesh):
    return jax.shard_map(
        body,
        mesh=mesh,
        in_specs=(P("tm", None, "space"), P("space")),
        out_specs=(P(None, "tm", "space"), P("tm")),
        check_vma=False,
    )
```

```python
import functools
import math

import jax
import jax.numpy as jnp
import numpy as np
from jax import lax
from jax.experimental import pallas as pl
from jax.experimental.pallas import tpu as pltpu
from jax.sharding import PartitionSpec as P

POWER = 3
F32 = jnp.float32
BF16 = jnp.bfloat16
MESH = pl.DeviceIdType.MESH
NT = 1024
NX, NY, NZ, NC = 4, 4, 8, 2


def transform_table():
    t = np.arange(NT // 2).reshape(32, 2, 8).transpose(1, 0, 2).reshape(-1)
    rows = []
    for unit in list(range(0, 32, 2)) + list(range(1, 32, 2)):
        if unit == 0:
            freq = np.array([64 * j for j in range(8)] + [32 + 64 * j for j in range(8)])
        else:
            freq = unit + 64 * np.arange(16)
        angle = 2.0 * np.pi * ((freq[:, None] * t[None, :]) % NT) / NT
        real, imag = np.cos(angle), -np.sin(angle)
        if unit == 0:
            imag[0] = np.cos(np.pi * t)
        rows += [real, imag]
    table = np.concatenate(rows).astype(np.float32)
    high = table.astype(jnp.bfloat16)
    low = (table - high.astype(np.float32)).astype(jnp.bfloat16)
    return np.stack([high.reshape(2, 512, 512), low.reshape(2, 512, 512)], axis=1).reshape(2, 1024, 512)


def split(x):
    high = x.astype(BF16)
    return high, (x - high.astype(F32)).astype(BF16)


def dot(a, b):
    return jnp.dot(a, b, preferred_element_type=F32)


def dot_nt(a, b):
    return lax.dot_general(a, b, (((1,), (1,)), ((), ())), preferred_element_type=F32)


def interleave(first, second, low):
    crossed = pltpu.roll(jnp.where(low, second, first), 64, 1)
    return jnp.where(low, first, crossed), jnp.where(low, crossed, second)


def bit_reverse(value):
    result = 0
    for position in range(6):
        result = result + ((value >> position) & 1) * (1 << (5 - position))
    return result


def unit_of(x, y, c):
    return c * 16 + x * 4 + ((y & 1) << 1) + (y >> 1)


def far_first(z, i):
    return (z + jnp.where((i & 1) == 1, 4 - ((i + 1) >> 1), 4 + (i >> 1))) & 7


def kernel(
    x_hbm, tab_hbm, w_hbm, out_ref, e_ref,
    xin, w_ref, tab, sb, rb, eh, ob, db, mh, ml, go, gr, vs, va, fs, fb,
    in_sem, w_sem, tab_sem, step_sem, s1, r1, s2, r2, s3, r3, s4, r4, s5, r5,
):
    me = lax.axis_index("tm")
    sx = lax.axis_index("space")
    y, z, c = me >> 4, (me >> 1) & 7, me & 1
    p = y * 2 + c
    unit = unit_of(sx, y, c)

    loads = [
        pltpu.make_async_copy(x_hbm.at[:, pl.ds(q * 128, 128)], xin.at[q], in_sem.at[q])
        for q in range(4)
    ]
    for load in loads:
        load.start()
    load_w = pltpu.make_async_copy(w_hbm, w_ref, w_sem)
    load_w.start()
    load_tab = pltpu.make_async_copy(tab_hbm, tab, tab_sem)

    barrier = pltpu.get_barrier_semaphore()

    def greet(semaphore, tm, space):
        pl.semaphore_signal(semaphore, 1, device_id=(tm, space), device_id_type=MESH)

    @pl.loop(0, 15)
    def _(k):
        greet(barrier, (me & 48) + (far_first(z, k >> 1) << 1) + (c ^ 1 ^ (k & 1)), sx)

    @pl.loop(1, 4)
    def _(k):
        greet(barrier, (me + 16 * k) & 63, sx)
        greet(barrier, me, (sx + k) & 3)

    lane = lax.broadcasted_iota(jnp.int32, (8, 128), 1)
    row = lax.broadcasted_iota(jnp.int32, (8, 128), 0)
    low = lane < 64
    load_tab.start()
    load_w.wait()
    root_w = jnp.sqrt(w_ref[...])
    unscale = lax.rsqrt(w_ref[...])
    for load in loads:
        load.wait()
    factor = []
    for sh in range(2):
        phase = (row + (16 * me + 8 * sh - NT // 2)).astype(F32) * (math.pi / NT)
        square = phase * phase
        cosine = jnp.full((8, 128), 1.0 / math.factorial(16), F32)
        for n in range(14, -1, -2):
            cosine = cosine * square + (-1.0) ** (n // 2) / math.factorial(n)
        window = cosine * cosine * (1.0 / math.sqrt(0.375 * NT))
        factor.append([window * root_w[:, 128 * q : 128 * q + 128] for q in range(4)])

    def arrange(half, n):
        owner = n >> 1
        chunk = half * 2 + (n & 1)
        b = owner * 4 + chunk
        base = (owner >> 1) * 16 + (owner & 1)
        for q in range(4):
            t0 = xin[q, pl.ds(b, 8, stride=32), :] * factor[0][q]
            t1 = xin[q, pl.ds(256 + b, 8, stride=32), :] * factor[1][q]
            even, odd = interleave(t0, t1, low)
            sb[base + 4 * q, chunk] = even
            sb[base + 4 * q + 2, chunk] = odd

    pl.loop(0, 16)(functools.partial(arrange, 0))

    groups = (pl.ds(0, 2), pl.ds(2, 1), pl.ds(3, 1))

    def send_columns(group, to):
        pltpu.make_async_remote_copy(
            sb.at[to, groups[group]], rb.at[me, groups[group]], s1.at[group], r1.at[group],
            device_id=(to, sx), device_id_type=MESH,
        ).start()

    def target(k):
        i = k & 7
        dz = jnp.where((i & 1) == 1, (i + 1) >> 1, 8 - (i >> 1))
        to = (((y + (k >> 4)) & 3) << 4) + (((z + dz) & 7) << 1)
        return to + (c ^ ((k >> 3) & 1))

    def send_rest(group):
        @pl.loop(1, 64)
        def _(k):
            send_columns(group, target(64 - k))

    pl.semaphore_wait(barrier, 15 + 3 + 3)
    for k in range(1, 4):
        greet(step_sem, (me + 16 * k) & 63, sx)

    @pl.loop(1, 16)
    def _(k):
        send_columns(0, target(k))

    pl.loop(0, 16)(functools.partial(arrange, 1))
    pl.semaphore_wait(step_sem, 3)

    @pl.loop(16, 64)
    def _(k):
        send_columns(0, target(k))

    send_rest(1)
    send_rest(2)

    rb[me] = sb[me]

    load_tab.wait()
    low64 = lax.broadcasted_iota(jnp.int32, (64, 128), 1) < 64
    low16 = lax.broadcasted_iota(jnp.int32, (16, 128), 1) < 64
    for h in range(4):
        if h != 1:
            landed = rb.at[pl.ds(0, 63), groups[max(h - 1, 0)]]
            pltpu.make_async_copy(landed, landed, r1.at[max(h - 1, 0)]).wait()

        @pl.loop(0, 4)
        def _(i):
            first = rb[pl.ds(i * 8, 8), h].reshape(64, 128)
            second = rb[pl.ds(32 + i * 8, 8), h].reshape(64, 128)
            for parity, value in enumerate((first + second, first - second)):
                high = value.astype(BF16).astype(F32)
                early, late = interleave(high, value - high, low64)
                eh[parity, pl.ds(i * 64, 64), :] = early.astype(BF16)
                eh[parity, pl.ds(256 + i * 64, 64), :] = late.astype(BF16)

        here = pl.ds(pl.multiple_of((sx * 32 + 4 * p + h) * 16, 16), 16)

        @pl.loop(0, 2)
        def _(step):
            first_y = y ^ 2 ^ (3 * step)
            parity = first_y >> 1
            product = dot(tab[parity], eh[parity])
            total = product[0:512] + product[512:1024]
            total = total + pltpu.roll(total, 64, 1)
            for n in range(16):
                ob[h, parity * 16 + n] = jnp.where(
                    low16, total[32 * n : 32 * n + 16], total[32 * n + 16 : 32 * n + 32]
                )

            @pl.loop(0, 16 - step)
            def _(k):
                dx = k & 3
                dx = jnp.where(dx < 2, 2 - dx, 3 * (3 - dx))
                px, py, pc = (sx + dx) & 3, first_y ^ (k >> 3), c ^ 1 ^ ((k >> 2) & 1)
                g = unit_of(px, py, pc)
                pltpu.make_async_remote_copy(
                    ob.at[h, (g & 1) * 16 + (g >> 1)], db.at[here], s2, r2,
                    device_id=((py << 4) + (z << 1) + pc, px), device_id_type=MESH,
                ).start()

        db[here, :] = ob[h, (unit & 1) * 16 + (unit >> 1)]

    pltpu.make_async_copy(db.at[pl.ds(0, 124 * 16)], db.at[pl.ds(0, 124 * 16)], r2).wait()

    low32 = lax.broadcasted_iota(jnp.int32, (32, 128), 1) < 64

    @pl.loop(0, 8)
    def _(i):
        zt = far_first(z, i)
        grams = []
        for f in range(2):
            j = zt * 2 + f
            keep = jnp.where((unit == 0) & (j == 0), 0.0, 1.0).astype(F32)
            real, imag = [], []
            for x in range(0, NX, 2):
                first = db[pl.ds(x * 512 + j, 32, stride=16), :]
                second = db[pl.ds(x * 512 + 512 + j, 32, stride=16), :]
                r, m = interleave(first, second, low32)
                real.append(r)
                imag.append(m)
            real_h, real_l = split(jnp.concatenate(real, axis=1))
            imag_h, imag_l = split(jnp.concatenate(imag, axis=1))
            left_h = jnp.concatenate([real_h, imag_h], axis=1)
            left_l = jnp.concatenate([real_l, imag_l], axis=1)
            base = pl.multiple_of(j * 32, 32)
            mh[pl.ds(base, 32), :] = left_h
            ml[pl.ds(base, 32), :] = left_l
            lone_part = (1.0 - keep).astype(BF16)
            keep = keep.astype(BF16)
            right = []
            for r, m in ((real_h, imag_h), (real_l, imag_l)):
                kept = m * keep
                right.append(jnp.concatenate([r, kept], axis=1))
                right.append(jnp.concatenate([kept, m * lone_part - r * keep], axis=1))
            product = dot_nt(
                jnp.concatenate([left_h, left_l], axis=0), jnp.concatenate(right, axis=0)
            )
            total = product[0:32] + product[32:64]
            grams.append(total + pltpu.roll(total, 64, 1))
        pair = jnp.where(low32, grams[0], grams[1])

        @pl.when(i < 7)
        def _():
            go[zt] = pair
            pltpu.make_async_remote_copy(
                go.at[zt], gr.at[z], s3, r3,
                device_id=((y << 4) + (zt << 1) + c, sx), device_id_type=MESH,
            ).start()

        @pl.when(i == 7)
        def _():
            gr[z] = pair

    pltpu.make_async_copy(gr.at[pl.ds(0, 7)], gr.at[pl.ds(0, 7)], r3).wait()
    gram = gr[0]
    for k in range(1, 8):
        gram = gram + gr[k]
    gram_h, gram_l = split(gram * (1.0 / 2048.0))
    gram = jnp.concatenate([gram_h, gram_l], axis=1)

    even = row % 2 == 0
    lone = (row < 2) & (unit == 0) & (z == 0)
    valid = (lane < 32) & (row < 4)

    def swap_rows(v):
        return jnp.where(even, pltpu.roll(v, 7, 0), pltpu.roll(v, 1, 0))

    def image_of(v):
        high = v.astype(BF16).astype(F32)
        both = jnp.where(row < 4, high, pltpu.roll(v - high, 4, 0)).astype(BF16)
        product = dot(both[:, 0:32], gram)
        product = product[:, 0:128] + product[:, 128:256]
        product = product + pltpu.roll(product, 4, 0)
        chosen = jnp.where(row < 2, product, pltpu.roll(product, 64, 1))
        other = pltpu.roll(chosen, 96, 1)
        crossed = swap_rows(other)
        normal = jnp.where(even, chosen + crossed, chosen - crossed)
        alone = jnp.where(even, chosen, other)
        return jnp.where(valid, jnp.where(lone, alone, normal), 0.0)

    def pair_sum(v):
        total = jnp.broadcast_to(jnp.sum(v, axis=1, keepdims=True), (8, 128))
        return jnp.where(lone, total, total + swap_rows(total))

    vec = jnp.where(valid & (even | lone), 1.0 / math.sqrt(32.0), 0.0).astype(F32)
    for _ in range(POWER):
        new = image_of(vec)
        vec = new * lax.rsqrt(pair_sum(new * new) + 1e-06)
    energy = pair_sum(vec * image_of(vec))
    scaled = vec * lax.rsqrt(energy + 1e-06)
    spread = scaled + pltpu.roll(scaled, 32, 1)
    spread = spread + pltpu.roll(spread, 64, 1)
    place = (z & 1) * 2 + row // 2 == lane // 32
    message = jnp.zeros((8, 128), F32)
    for n, value in enumerate((spread, spread, energy, energy)):
        chosen = jnp.where(place & (row & 1 == n % 2), value, 0.0)
        message = jnp.where(row == n, jnp.sum(chosen, axis=0, keepdims=True), message)
    vs[...] = message
    va[z] = message

    @pl.loop(0, 7)
    def _(i):
        zt = far_first(z, i)
        pltpu.make_async_remote_copy(
            vs, va.at[z], s4, r4,
            device_id=((y << 4) + (zt << 1) + c, sx), device_id_type=MESH,
        ).start()

    rows = lax.broadcasted_iota(jnp.int32, (32, 128), 0)
    lanes = lax.broadcasted_iota(jnp.int32, (32, 128), 1)
    ver, j = rows // 16, rows % 16
    first_unit = unit == 0
    slot = jnp.where(ver == 0, j, 15 - j)
    slot_first = jnp.where(
        ver == 0,
        jnp.where(j < 8, j, jnp.where(j == 8, 0, 16 - j)),
        jnp.where(j < 8, 8 + j, 23 - j),
    )
    slot = jnp.where(first_unit, slot_first, slot)
    flip = jnp.where(jnp.where(first_unit, j // 8, ver) == 1, -1.0, 1.0)
    direct = first_unit & (ver == 0) & (j == 0)
    nyquist = first_unit & (ver == 0) & (j == 8)
    alone = direct | nyquist
    real_by_real = jnp.where(nyquist, 0.0, 1.0)
    real_by_imag = jnp.where(direct, 0.0, jnp.where(nyquist, 1.0, -1.0))
    imag_by_any = jnp.where(alone, 0.0, flip)
    lane_slot = lanes // 32
    lead = lanes % 32 == 0

    pltpu.make_async_copy(va.at[pl.ds(0, 7)], va.at[pl.ds(0, 7)], r4).wait()

    energies = jnp.zeros((32, 128), F32)
    lefts = []
    for k in range(4):
        v = va[2 * k] + va[2 * k + 1]
        here = slot == 4 * k + lane_slot
        lefts.append(
            jnp.concatenate(
                [jnp.where(here, v[0:1, :], 0.0), jnp.where(here, v[1:2, :], 0.0)], axis=0
            )
        )
        energy = jnp.where(nyquist, v[3:4, :], v[2:3, :])
        energies = energies + jnp.where(here & lead, energy, 0.0)
    lh, ll = split(jnp.concatenate(lefts, axis=1))
    modes = dot(jnp.concatenate([lh, ll], axis=0), mh[...])
    modes = modes[0:64] + (modes[64:128] + dot(lh, ml[...]))
    energies = jnp.broadcast_to(jnp.sum(energies, axis=1, keepdims=True), (32, 128))

    sends = []
    for ver in range(2):
        if ver == 0:
            klass = unit
        else:
            klass = jnp.where(unit == 0, 32, 64 - unit)
        to = bit_reverse(klass)
        base = 16 * ver
        energy_tile = jnp.where(low, energies[base : base + 8], energies[base + 8 : base + 16])
        for px in range(4):
            n = ver * 4 + px
            at_real = 128 * (px // 2)
            at_imag = 256 + at_real
            part = slice(base, base + 16)
            twin = slice(base + 32, base + 48)
            real = (
                modes[part, at_real : at_real + 128] * real_by_real[part]
                + modes[twin, at_imag : at_imag + 128] * real_by_imag[part]
            )
            imag = (
                modes[part, at_imag : at_imag + 128] + modes[twin, at_real : at_real + 128]
            ) * imag_by_any[part]
            if px % 2 == 0:
                fs[n, 0:16, :] = jnp.where(low16, real, pltpu.roll(imag, 64, 1))
            else:
                fs[n, 0:16, :] = jnp.where(low16, pltpu.roll(real, 64, 1), imag)
            fs[n, 16:24, :] = energy_tile
            send = pltpu.make_async_remote_copy(
                fs.at[n], fb.at[z], s5.at[n], r5.at[z],
                device_id=(to, px), device_id_type=MESH,
            )
            kept = (to == me) & (px == sx)
            sends.append((send, kept))

            @pl.when(jnp.logical_not(kept))
            def _():
                send.start()

            @pl.when(kept)
            def _():
                fb[z] = fs[n]

    mine = bit_reverse(me)
    my_unit = jnp.where(mine == 32, 0, jnp.where(mine > 32, 64 - mine, mine))
    same_group = my_unit == unit
    for k in range(8):

        @pl.when(jnp.logical_not(same_group & (z == k)))
        def _():
            pltpu.make_async_copy(fb.at[k], fb.at[k], r5.at[k]).wait()

    for q in range(4):
        real, imag = interleave(fb[2 * q, 0:16, :], fb[2 * q + 1, 0:16, :], low16)
        scale = unscale[:, 128 * q : 128 * q + 128]
        out_ref[0:16, 128 * q : 128 * q + 128] = real * scale
        out_ref[16:32, 128 * q : 128 * q + 128] = imag * scale
    tile = fb[0, 16:24, :]
    turned = pltpu.roll(tile, 64, 1)
    diagonal = jnp.where(lane == row, tile, 0.0) + jnp.where(lane == row + 8, turned, 0.0)
    e_ref[...] = jnp.sum(diagonal, axis=0, keepdims=True)[:, 0:16]

    for group in range(3):
        left = sb.at[pl.ds(0, 63), groups[group]]
        pltpu.make_async_copy(left, left, s1.at[group]).wait()
    pltpu.make_async_copy(db.at[pl.ds(0, 124 * 16)], db.at[pl.ds(0, 124 * 16)], s2).wait()
    pltpu.make_async_copy(gr.at[pl.ds(0, 7)], gr.at[pl.ds(0, 7)], s3).wait()
    pltpu.make_async_copy(va.at[pl.ds(0, 7)], va.at[pl.ds(0, 7)], s4).wait()
    for send, kept in sends:

        @pl.when(jnp.logical_not(kept))
        def _():
            send.wait_send()


def hand_over(modes_ref, e_ref, modes_hbm, e_hbm, sem):
    copies = [
        pltpu.make_async_copy(modes_ref, modes_hbm, sem.at[0]),
        pltpu.make_async_copy(e_ref, e_hbm, sem.at[1]),
    ]
    for copy in copies:
        copy.start()
    for copy in copies:
        copy.wait()


def body(snapshots, quad_weights):
    times, blocks, points = snapshots.shape
    table = jnp.asarray(transform_table())
    any_spec = pl.BlockSpec(memory_space=pl.ANY)
    vmem = pl.BlockSpec(memory_space=pltpu.VMEM)
    dma = pltpu.SemaphoreType.DMA
    weights = quad_weights.reshape(1, points)
    modes, energies = pl.pallas_call(
        kernel,
        out_shape=(pltpu.VMEM((32, 512), F32), pltpu.VMEM((1, 16), F32)),
        in_specs=[any_spec, any_spec, any_spec],
        out_specs=(vmem, vmem),
        scratch_shapes=[
            pltpu.VMEM((4, 512, 128), F32),
            pltpu.VMEM((1, 512), F32),
            pltpu.VMEM((2, 1024, 512), BF16),
            pltpu.VMEM((64, 4, 8, 128), F32),
            pltpu.VMEM((64, 4, 8, 128), F32),
            pltpu.VMEM((2, 512, 128), BF16),
            pltpu.VMEM((4, 32, 16, 128), F32),
            pltpu.VMEM((2048, 128), F32),
            pltpu.VMEM((512, 512), BF16),
            pltpu.VMEM((512, 512), BF16),
            pltpu.VMEM((8, 32, 128), F32),
            pltpu.VMEM((8, 32, 128), F32),
            pltpu.VMEM((8, 128), F32),
            pltpu.VMEM((8, 8, 128), F32),
            pltpu.VMEM((8, 24, 128), F32),
            pltpu.VMEM((8, 24, 128), F32),
            dma((4,)), dma, dma, pltpu.SemaphoreType.REGULAR,
            dma((3,)), dma((3,)),
            dma, dma, dma, dma, dma, dma,
            dma((8,)), dma((8,)),
        ],
        compiler_params=pltpu.CompilerParams(collective_id=0, has_side_effects=True),
        name="spod",
    )(snapshots.reshape(times * blocks, points), table, weights)
    modes, energies = pl.pallas_call(
        hand_over,
        out_shape=(
            jax.ShapeDtypeStruct((32, points), F32),
            jax.ShapeDtypeStruct((1, 16), F32),
        ),
        in_specs=[vmem, vmem],
        out_specs=(any_spec, any_spec),
        scratch_shapes=[dma((2,))],
        name="hand_over",
    )(
        pltpu.with_memory_space_constraint(modes, pltpu.VMEM),
        pltpu.with_memory_space_constraint(energies, pltpu.VMEM),
    )
    return modes.reshape(2, 16, points), energies.reshape(16)


def solution(mesh):
    return jax.shard_map(
        body,
        mesh=mesh,
        in_specs=(P("tm", None, "space"), P("space")),
        out_specs=(P(None, "tm", "space"), P("tm")),
        check_vma=False,
    )
```

```python
import functools
import math

import jax
import jax.numpy as jnp
import numpy as np
from jax import lax
from jax.experimental import pallas as pl
from jax.experimental.pallas import tpu as pltpu
from jax.sharding import PartitionSpec as P

POWER = 3
F32 = jnp.float32
BF16 = jnp.bfloat16
MESH = pl.DeviceIdType.MESH
NT = 1024
NX, NY, NZ, NC = 4, 4, 8, 2


def transform_table():
    t = np.arange(NT // 2).reshape(32, 2, 8).transpose(1, 0, 2).reshape(-1)
    rows = []
    for unit in list(range(0, 32, 2)) + list(range(1, 32, 2)):
        if unit == 0:
            freq = np.array([64 * j for j in range(8)] + [32 + 64 * j for j in range(8)])
        else:
            freq = unit + 64 * np.arange(16)
        angle = 2.0 * np.pi * ((freq[:, None] * t[None, :]) % NT) / NT
        real, imag = np.cos(angle), -np.sin(angle)
        if unit == 0:
            imag[0] = np.cos(np.pi * t)
        rows += [real, imag]
    table = np.concatenate(rows).astype(np.float32)
    high = table.astype(jnp.bfloat16)
    low = (table - high.astype(np.float32)).astype(jnp.bfloat16)
    return np.stack([high.reshape(2, 512, 512), low.reshape(2, 512, 512)], axis=1).reshape(2, 1024, 512)


def split(x):
    high = x.astype(BF16)
    return high, (x - high.astype(F32)).astype(BF16)


def dot(a, b):
    return jnp.dot(a, b, preferred_element_type=F32)


def dot_nt(a, b):
    return lax.dot_general(a, b, (((1,), (1,)), ((), ())), preferred_element_type=F32)


def interleave(first, second, low):
    crossed = pltpu.roll(jnp.where(low, second, first), 64, 1)
    return jnp.where(low, first, crossed), jnp.where(low, crossed, second)


def bit_reverse(value):
    result = 0
    for position in range(6):
        result = result + ((value >> position) & 1) * (1 << (5 - position))
    return result


def unit_of(x, y, c):
    return c * 16 + x * 4 + ((y & 1) << 1) + (y >> 1)


def far_first(z, i):
    return (z + jnp.where((i & 1) == 1, 4 - ((i + 1) >> 1), 4 + (i >> 1))) & 7


def kernel(
    x_hbm, tab_hbm, w_hbm, out_ref, e_ref,
    xin, w_ref, tab, sb, rb, eh, ob, db, mh, ml, go, gr, vs, va, fs, fb,
    in_sem, w_sem, tab_sem, step_sem, s1, r1, s2, r2, s3, r3, s4, r4, s5, r5,
):
    me = lax.axis_index("tm")
    sx = lax.axis_index("space")
    y, z, c = me >> 4, (me >> 1) & 7, me & 1
    p = y * 2 + c
    unit = unit_of(sx, y, c)

    loads = [
        pltpu.make_async_copy(x_hbm.at[:, :, pl.ds(q * 128, 128)], xin.at[q], in_sem.at[q])
        for q in range(4)
    ]
    for load in loads:
        load.start()
    load_w = pltpu.make_async_copy(w_hbm, w_ref, w_sem)
    load_w.start()
    load_tab = pltpu.make_async_copy(tab_hbm, tab, tab_sem)

    barrier = pltpu.get_barrier_semaphore()

    def greet(semaphore, tm, space):
        pl.semaphore_signal(semaphore, 1, device_id=(tm, space), device_id_type=MESH)

    @pl.loop(0, 15)
    def _(k):
        greet(barrier, (me & 48) + (far_first(z, k >> 1) << 1) + (c ^ 1 ^ (k & 1)), sx)

    @pl.loop(1, 4)
    def _(k):
        greet(barrier, (me + 16 * k) & 63, sx)
        greet(barrier, me, (sx + k) & 3)

    lane = lax.broadcasted_iota(jnp.int32, (8, 128), 1)
    row = lax.broadcasted_iota(jnp.int32, (8, 128), 0)
    low = lane < 64
    load_tab.start()
    load_w.wait()
    root_w = jnp.sqrt(w_ref[...])
    unscale = lax.rsqrt(w_ref[...])
    for load in loads:
        load.wait()
    factor = []
    for sh in range(2):
        phase = (row + (16 * me + 8 * sh - NT // 2)).astype(F32) * (math.pi / NT)
        square = phase * phase
        cosine = jnp.full((8, 128), 1.0 / math.factorial(16), F32)
        for n in range(14, -1, -2):
            cosine = cosine * square + (-1.0) ** (n // 2) / math.factorial(n)
        window = cosine * cosine * (1.0 / math.sqrt(0.375 * NT))
        factor.append([window * root_w[:, 128 * q : 128 * q + 128] for q in range(4)])

    def arrange(half, bt):
        rows = pl.ds(pl.multiple_of(bt * 8, 8), 8)
        base = bt * 16
        for q in range(4):
            early = jnp.swapaxes(xin[q, 0:8, rows, :], 0, 1)
            late = jnp.swapaxes(xin[q, 8:16, rows, :], 0, 1)
            for n in (0, 1, 4, 5):
                b = n + 2 * half
                even, odd = interleave(
                    early[b] * factor[0][q], late[b] * factor[1][q], low
                )
                sb[base + n // 4 + 4 * q, b % 4] = even
                sb[base + n // 4 + 4 * q + 2, b % 4] = odd

    pl.loop(0, 4)(functools.partial(arrange, 0))

    groups = (pl.ds(0, 2), pl.ds(2, 1), pl.ds(3, 1))

    def send_columns(group, to):
        pltpu.make_async_remote_copy(
            sb.at[to, groups[group]], rb.at[me, groups[group]], s1.at[group], r1.at[group],
            device_id=(to, sx), device_id_type=MESH,
        ).start()

    def target(k):
        i = k & 7
        dz = jnp.where((i & 1) == 1, (i + 1) >> 1, 8 - (i >> 1))
        to = (((y + (k >> 4)) & 3) << 4) + (((z + dz) & 7) << 1)
        return to + (c ^ ((k >> 3) & 1))

    def send_rest(group):
        @pl.loop(1, 64)
        def _(k):
            send_columns(group, target(64 - k))

    pl.semaphore_wait(barrier, 15 + 3 + 3)
    for k in range(1, 4):
        greet(step_sem, (me + 16 * k) & 63, sx)

    @pl.loop(1, 16)
    def _(k):
        send_columns(0, target(k))

    pl.loop(0, 4)(functools.partial(arrange, 1))
    pl.semaphore_wait(step_sem, 3)

    @pl.loop(16, 64)
    def _(k):
        send_columns(0, target(k))

    send_rest(1)
    send_rest(2)

    rb[me] = sb[me]

    load_tab.wait()
    low64 = lax.broadcasted_iota(jnp.int32, (64, 128), 1) < 64
    low16 = lax.broadcasted_iota(jnp.int32, (16, 128), 1) < 64
    for h in range(4):
        if h != 1:
            landed = rb.at[pl.ds(0, 63), groups[max(h - 1, 0)]]
            pltpu.make_async_copy(landed, landed, r1.at[max(h - 1, 0)]).wait()

        @pl.loop(0, 4)
        def _(i):
            first = rb[pl.ds(i * 8, 8), h].reshape(64, 128)
            second = rb[pl.ds(32 + i * 8, 8), h].reshape(64, 128)
            for parity, value in enumerate((first + second, first - second)):
                high = value.astype(BF16).astype(F32)
                early, late = interleave(high, value - high, low64)
                eh[parity, pl.ds(i * 64, 64), :] = early.astype(BF16)
                eh[parity, pl.ds(256 + i * 64, 64), :] = late.astype(BF16)

        here = pl.ds(pl.multiple_of((sx * 32 + 4 * p + h) * 16 + 8, 8), 16)
        turn = 4 * (p & 1) + h

        @pl.loop(0, 2)
        def _(step):
            first_y = y ^ 2 ^ (3 * step)
            parity = first_y >> 1
            product = dot(tab[parity], eh[parity])
            total = product[0:512] + product[512:1024]
            total = total + pltpu.roll(total, 64, 1)
            for n in range(16):
                for m in (32 * n, 32 * n + 8):
                    tile = jnp.where(low, total[m : m + 8], total[m + 16 : m + 24])
                    ob[h, parity * 16 + n, m % 32 : m % 32 + 8, :] = pltpu.roll(tile, turn, 0)

            @pl.loop(0, 16 - step)
            def _(k):
                dx = k & 3
                dx = jnp.where(dx < 2, 2 - dx, 3 * (3 - dx))
                px, py, pc = (sx + dx) & 3, first_y ^ (k >> 3), c ^ 1 ^ ((k >> 2) & 1)
                g = unit_of(px, py, pc)
                pltpu.make_async_remote_copy(
                    ob.at[h, (g & 1) * 16 + (g >> 1)], db.at[here], s2, r2,
                    device_id=((py << 4) + (z << 1) + pc, px), device_id_type=MESH,
                ).start()

        db[here, :] = ob[h, (unit & 1) * 16 + (unit >> 1)]

    pltpu.make_async_copy(db.at[pl.ds(0, 124 * 16)], db.at[pl.ds(0, 124 * 16)], r2).wait()

    low32 = lax.broadcasted_iota(jnp.int32, (32, 128), 1) < 64

    def slot_rows(x, j):
        wrapped = row + (j & 7) >= 8
        tiles = []
        for g in range(4):
            start = 8 + x * 512 + g * 128 + j
            plain = db[pl.ds(start, 8, stride=17), :]
            back = db[pl.ds(start - 8, 8, stride=17), :]
            tiles.append(jnp.where(wrapped, back, plain))
        return jnp.concatenate(tiles, axis=0)

    @pl.loop(0, 8)
    def _(i):
        zt = far_first(z, i)
        grams = []
        for f in range(2):
            j = zt * 2 + f
            keep = jnp.where((unit == 0) & (j == 0), 0.0, 1.0).astype(F32)
            real, imag = [], []
            for x in range(0, NX, 2):
                first = slot_rows(x, j)
                second = slot_rows(x + 1, j)
                r, m = interleave(first, second, low32)
                real.append(r)
                imag.append(m)
            real_h, real_l = split(jnp.concatenate(real, axis=1))
            imag_h, imag_l = split(jnp.concatenate(imag, axis=1))
            left_h = jnp.concatenate([real_h, imag_h], axis=1)
            left_l = jnp.concatenate([real_l, imag_l], axis=1)
            base = pl.multiple_of(j * 32, 32)
            mh[pl.ds(base, 32), :] = left_h
            ml[pl.ds(base, 32), :] = left_l
            lone_part = (1.0 - keep).astype(BF16)
            keep = keep.astype(BF16)
            right = []
            for r, m in ((real_h, imag_h), (real_l, imag_l)):
                kept = m * keep
                right.append(jnp.concatenate([r, kept], axis=1))
                right.append(jnp.concatenate([kept, m * lone_part - r * keep], axis=1))
            product = dot_nt(
                jnp.concatenate([left_h, left_l], axis=0), jnp.concatenate(right, axis=0)
            )
            total = product[0:32] + product[32:64]
            grams.append(total + pltpu.roll(total, 64, 1))
        pair = jnp.where(low32, grams[0], grams[1])

        @pl.when(i < 7)
        def _():
            go[zt] = pair
            pltpu.make_async_remote_copy(
                go.at[zt], gr.at[z], s3, r3,
                device_id=((y << 4) + (zt << 1) + c, sx), device_id_type=MESH,
            ).start()

        @pl.when(i == 7)
        def _():
            gr[z] = pair

    pltpu.make_async_copy(gr.at[pl.ds(0, 7)], gr.at[pl.ds(0, 7)], r3).wait()
    gram = gr[0]
    for k in range(1, 8):
        gram = gram + gr[k]
    gram_h, gram_l = split(gram * (1.0 / 2048.0))
    gram = jnp.concatenate([gram_h, gram_l], axis=1)

    even = row % 2 == 0
    lone = (row < 2) & (unit == 0) & (z == 0)
    valid = (lane < 32) & (row < 4)

    def swap_rows(v):
        return jnp.where(even, pltpu.roll(v, 7, 0), pltpu.roll(v, 1, 0))

    def image_of(v):
        high = v.astype(BF16).astype(F32)
        both = jnp.where(row < 4, high, pltpu.roll(v - high, 4, 0)).astype(BF16)
        product = dot(both[:, 0:32], gram)
        product = product[:, 0:128] + product[:, 128:256]
        product = product + pltpu.roll(product, 4, 0)
        chosen = jnp.where(row < 2, product, pltpu.roll(product, 64, 1))
        other = pltpu.roll(chosen, 96, 1)
        crossed = swap_rows(other)
        normal = jnp.where(even, chosen + crossed, chosen - crossed)
        alone = jnp.where(even, chosen, other)
        return jnp.where(valid, jnp.where(lone, alone, normal), 0.0)

    def pair_sum(v):
        total = jnp.broadcast_to(jnp.sum(v, axis=1, keepdims=True), (8, 128))
        return jnp.where(lone, total, total + swap_rows(total))

    vec = jnp.where(valid & (even | lone), 1.0 / math.sqrt(32.0), 0.0).astype(F32)
    for _ in range(POWER):
        new = image_of(vec)
        vec = new * lax.rsqrt(pair_sum(new * new) + 1e-06)
    energy = pair_sum(vec * image_of(vec))
    scaled = vec * lax.rsqrt(energy + 1e-06)
    spread = scaled + pltpu.roll(scaled, 32, 1)
    spread = spread + pltpu.roll(spread, 64, 1)
    place = (z & 1) * 2 + row // 2 == lane // 32
    message = jnp.zeros((8, 128), F32)
    for n, value in enumerate((spread, spread, energy, energy)):
        chosen = jnp.where(place & (row & 1 == n % 2), value, 0.0)
        message = jnp.where(row == n, jnp.sum(chosen, axis=0, keepdims=True), message)
    vs[...] = message
    va[z] = message

    @pl.loop(0, 7)
    def _(i):
        zt = far_first(z, i)
        pltpu.make_async_remote_copy(
            vs, va.at[z], s4, r4,
            device_id=((y << 4) + (zt << 1) + c, sx), device_id_type=MESH,
        ).start()

    rows = lax.broadcasted_iota(jnp.int32, (32, 128), 0)
    lanes = lax.broadcasted_iota(jnp.int32, (32, 128), 1)
    ver, j = rows // 16, rows % 16
    first_unit = unit == 0
    slot = jnp.where(ver == 0, j, 15 - j)
    slot_first = jnp.where(
        ver == 0,
        jnp.where(j < 8, j, jnp.where(j == 8, 0, 16 - j)),
        jnp.where(j < 8, 8 + j, 23 - j),
    )
    slot = jnp.where(first_unit, slot_first, slot)
    flip = jnp.where(jnp.where(first_unit, j // 8, ver) == 1, -1.0, 1.0)
    direct = first_unit & (ver == 0) & (j == 0)
    nyquist = first_unit & (ver == 0) & (j == 8)
    alone = direct | nyquist
    real_by_real = jnp.where(nyquist, 0.0, 1.0)
    real_by_imag = jnp.where(direct, 0.0, jnp.where(nyquist, 1.0, -1.0))
    imag_by_any = jnp.where(alone, 0.0, flip)
    lane_slot = lanes // 32
    lead = lanes % 32 == 0

    pltpu.make_async_copy(va.at[pl.ds(0, 7)], va.at[pl.ds(0, 7)], r4).wait()

    energies = jnp.zeros((32, 128), F32)
    lefts = []
    for k in range(4):
        v = va[2 * k] + va[2 * k + 1]
        here = slot == 4 * k + lane_slot
        lefts.append(
            jnp.concatenate(
                [jnp.where(here, v[0:1, :], 0.0), jnp.where(here, v[1:2, :], 0.0)], axis=0
            )
        )
        energy = jnp.where(nyquist, v[3:4, :], v[2:3, :])
        energies = energies + jnp.where(here & lead, energy, 0.0)
    lh, ll = split(jnp.concatenate(lefts, axis=1))
    modes = dot(jnp.concatenate([lh, ll], axis=0), mh[...])
    modes = modes[0:64] + (modes[64:128] + dot(lh, ml[...]))
    energies = jnp.broadcast_to(jnp.sum(energies, axis=1, keepdims=True), (32, 128))

    sends = []
    for ver in range(2):
        if ver == 0:
            klass = unit
        else:
            klass = jnp.where(unit == 0, 32, 64 - unit)
        to = bit_reverse(klass)
        base = 16 * ver
        energy_tile = jnp.where(low, energies[base : base + 8], energies[base + 8 : base + 16])
        for px in range(4):
            n = ver * 4 + px
            at_real = 128 * (px // 2)
            at_imag = 256 + at_real
            part = slice(base, base + 16)
            twin = slice(base + 32, base + 48)
            real = (
                modes[part, at_real : at_real + 128] * real_by_real[part]
                + modes[twin, at_imag : at_imag + 128] * real_by_imag[part]
            )
            imag = (
                modes[part, at_imag : at_imag + 128] + modes[twin, at_real : at_real + 128]
            ) * imag_by_any[part]
            if px % 2 == 0:
                fs[n, 0:16, :] = jnp.where(low16, real, pltpu.roll(imag, 64, 1))
            else:
                fs[n, 0:16, :] = jnp.where(low16, pltpu.roll(real, 64, 1), imag)
            fs[n, 16:24, :] = energy_tile
            send = pltpu.make_async_remote_copy(
                fs.at[n], fb.at[z], s5.at[n], r5.at[z],
                device_id=(to, px), device_id_type=MESH,
            )
            kept = (to == me) & (px == sx)
            sends.append((send, kept))

            @pl.when(jnp.logical_not(kept))
            def _():
                send.start()

            @pl.when(kept)
            def _():
                fb[z] = fs[n]

    mine = bit_reverse(me)
    my_unit = jnp.where(mine == 32, 0, jnp.where(mine > 32, 64 - mine, mine))
    same_group = my_unit == unit
    for k in range(8):

        @pl.when(jnp.logical_not(same_group & (z == k)))
        def _():
            pltpu.make_async_copy(fb.at[k], fb.at[k], r5.at[k]).wait()

    for q in range(4):
        real, imag = interleave(fb[2 * q, 0:16, :], fb[2 * q + 1, 0:16, :], low16)
        scale = unscale[:, 128 * q : 128 * q + 128]
        out_ref[0:16, 128 * q : 128 * q + 128] = real * scale
        out_ref[16:32, 128 * q : 128 * q + 128] = imag * scale
    tile = fb[0, 16:24, :]
    turned = pltpu.roll(tile, 64, 1)
    diagonal = jnp.where(lane == row, tile, 0.0) + jnp.where(lane == row + 8, turned, 0.0)
    e_ref[...] = jnp.sum(diagonal, axis=0, keepdims=True)[:, 0:16]

    for group in range(3):
        left = sb.at[pl.ds(0, 63), groups[group]]
        pltpu.make_async_copy(left, left, s1.at[group]).wait()
    pltpu.make_async_copy(db.at[pl.ds(0, 124 * 16)], db.at[pl.ds(0, 124 * 16)], s2).wait()
    pltpu.make_async_copy(gr.at[pl.ds(0, 7)], gr.at[pl.ds(0, 7)], s3).wait()
    pltpu.make_async_copy(va.at[pl.ds(0, 7)], va.at[pl.ds(0, 7)], s4).wait()
    for send, kept in sends:

        @pl.when(jnp.logical_not(kept))
        def _():
            send.wait_send()


def hand_over(modes_ref, e_ref, modes_hbm, e_hbm, sem):
    copies = [
        pltpu.make_async_copy(modes_ref, modes_hbm, sem.at[0]),
        pltpu.make_async_copy(e_ref, e_hbm, sem.at[1]),
    ]
    for copy in copies:
        copy.start()
    for copy in copies:
        copy.wait()


def body(snapshots, quad_weights):
    times, blocks, points = snapshots.shape
    table = jnp.asarray(transform_table())
    any_spec = pl.BlockSpec(memory_space=pl.ANY)
    vmem = pl.BlockSpec(memory_space=pltpu.VMEM)
    dma = pltpu.SemaphoreType.DMA
    weights = quad_weights.reshape(1, points)
    modes, energies = pl.pallas_call(
        kernel,
        out_shape=(pltpu.VMEM((32, 512), F32), pltpu.VMEM((1, 16), F32)),
        in_specs=[any_spec, any_spec, any_spec],
        out_specs=(vmem, vmem),
        scratch_shapes=[
            pltpu.VMEM((4, 16, 32, 128), F32),
            pltpu.VMEM((1, 512), F32),
            pltpu.VMEM((2, 1024, 512), BF16),
            pltpu.VMEM((64, 4, 8, 128), F32),
            pltpu.VMEM((64, 4, 8, 128), F32),
            pltpu.VMEM((2, 512, 128), BF16),
            pltpu.VMEM((4, 32, 16, 128), F32),
            pltpu.VMEM((2064, 128), F32),
            pltpu.VMEM((512, 512), BF16),
            pltpu.VMEM((512, 512), BF16),
            pltpu.VMEM((8, 32, 128), F32),
            pltpu.VMEM((8, 32, 128), F32),
            pltpu.VMEM((8, 128), F32),
            pltpu.VMEM((8, 8, 128), F32),
            pltpu.VMEM((8, 24, 128), F32),
            pltpu.VMEM((8, 24, 128), F32),
            dma((4,)), dma, dma, pltpu.SemaphoreType.REGULAR,
            dma((3,)), dma((3,)),
            dma, dma, dma, dma, dma, dma,
            dma((8,)), dma((8,)),
        ],
        compiler_params=pltpu.CompilerParams(collective_id=0, has_side_effects=True),
        name="spod",
    )(snapshots, table, weights)
    modes, energies = pl.pallas_call(
        hand_over,
        out_shape=(
            jax.ShapeDtypeStruct((32, points), F32),
            jax.ShapeDtypeStruct((1, 16), F32),
        ),
        in_specs=[vmem, vmem],
        out_specs=(any_spec, any_spec),
        scratch_shapes=[dma((2,))],
        name="hand_over",
    )(
        pltpu.with_memory_space_constraint(modes, pltpu.VMEM),
        pltpu.with_memory_space_constraint(energies, pltpu.VMEM),
    )
    return modes.reshape(2, 16, points), energies.reshape(16)


def solution(mesh):
    return jax.shard_map(
        body,
        mesh=mesh,
        in_specs=(P("tm", None, "space"), P("space")),
        out_specs=(P(None, "tm", "space"), P("tm")),
        check_vma=False,
    )
```

```python
import functools
import math

import jax
import jax.numpy as jnp
import numpy as np
from jax import lax
from jax.experimental import pallas as pl
from jax.experimental.pallas import tpu as pltpu
from jax.sharding import PartitionSpec as P

POWER = 3
F32 = jnp.float32
BF16 = jnp.bfloat16
MESH = pl.DeviceIdType.MESH
NT = 1024
NX, NY, NZ, NC = 4, 4, 8, 2


def transform_table():
    t = np.arange(NT // 2).reshape(32, 2, 8).transpose(1, 0, 2).reshape(-1)
    rows = []
    for unit in list(range(0, 32, 2)) + list(range(1, 32, 2)):
        if unit == 0:
            freq = np.array([64 * j for j in range(8)] + [32 + 64 * j for j in range(8)])
        else:
            freq = unit + 64 * np.arange(16)
        angle = 2.0 * np.pi * ((freq[:, None] * t[None, :]) % NT) / NT
        real, imag = np.cos(angle), -np.sin(angle)
        if unit == 0:
            imag[0] = np.cos(np.pi * t)
        rows += [real, imag]
    table = np.concatenate(rows).astype(np.float32)
    high = table.astype(jnp.bfloat16)
    low = (table - high.astype(np.float32)).astype(jnp.bfloat16)
    return np.stack([high.reshape(2, 512, 512), low.reshape(2, 512, 512)], axis=1).reshape(2, 1024, 512)


def split(x):
    high = x.astype(BF16)
    return high, (x - high.astype(F32)).astype(BF16)


def dot(a, b):
    return jnp.dot(a, b, preferred_element_type=F32)


def dot_nt(a, b):
    return lax.dot_general(a, b, (((1,), (1,)), ((), ())), preferred_element_type=F32)


def interleave(first, second, low):
    crossed = pltpu.roll(jnp.where(low, second, first), 64, 1)
    return jnp.where(low, first, crossed), jnp.where(low, crossed, second)


def bit_reverse(value):
    result = 0
    for position in range(6):
        result = result + ((value >> position) & 1) * (1 << (5 - position))
    return result


def unit_of(x, y, c):
    return c * 16 + x * 4 + ((y & 1) << 1) + (y >> 1)


def far_first(z, i):
    return (z + jnp.where((i & 1) == 1, 4 - ((i + 1) >> 1), 4 + (i >> 1))) & 7


def kernel(
    x_hbm, tab_hbm, w_hbm, out_ref, e_ref,
    xin, w_ref, tab, sb, rb, eh, ob, db, mh, ml, go, gr, vs, va, fs, fb,
    in_sem, w_sem, tab_sem, step_sem, s1, r1, s2, r2, s3, r3, s4, r4, s5, r5,
):
    me = lax.axis_index("tm")
    sx = lax.axis_index("space")
    y, z, c = me >> 4, (me >> 1) & 7, me & 1
    p = y * 2 + c
    unit = unit_of(sx, y, c)

    loads = [
        pltpu.make_async_copy(x_hbm.at[:, :, pl.ds(q * 128, 128)], xin.at[q], in_sem.at[q])
        for q in range(4)
    ]
    for load in loads:
        load.start()
    load_w = pltpu.make_async_copy(w_hbm, w_ref, w_sem)
    load_w.start()
    load_tab = pltpu.make_async_copy(tab_hbm, tab, tab_sem)

    barrier = pltpu.get_barrier_semaphore()

    def greet(semaphore, tm, space):
        pl.semaphore_signal(semaphore, 1, device_id=(tm, space), device_id_type=MESH)

    @pl.loop(0, 15)
    def _(k):
        greet(barrier, (me & 48) + (far_first(z, k >> 1) << 1) + (c ^ 1 ^ (k & 1)), sx)

    @pl.loop(1, 4)
    def _(k):
        greet(barrier, (me + 16 * k) & 63, sx)
        greet(barrier, me, (sx + k) & 3)

    lane = lax.broadcasted_iota(jnp.int32, (8, 128), 1)
    row = lax.broadcasted_iota(jnp.int32, (8, 128), 0)
    low = lane < 64
    load_tab.start()
    load_w.wait()
    root_w = jnp.sqrt(w_ref[...])
    unscale = lax.rsqrt(w_ref[...])
    for load in loads:
        load.wait()
    factor = []
    for sh in range(2):
        phase = (row + (16 * me + 8 * sh - NT // 2)).astype(F32) * (math.pi / NT)
        square = phase * phase
        cosine = jnp.full((8, 128), 1.0 / math.factorial(16), F32)
        for n in range(14, -1, -2):
            cosine = cosine * square + (-1.0) ** (n // 2) / math.factorial(n)
        window = cosine * cosine * (1.0 / math.sqrt(0.375 * NT))
        factor.append([window * root_w[:, 128 * q : 128 * q + 128] for q in range(4)])

    def arrange(half, bt):
        rows = pl.ds(pl.multiple_of(bt * 8, 8), 8)
        base = bt * 16
        for q in range(4):
            early = jnp.swapaxes(xin[q, 0:8, rows, :], 0, 1)
            late = jnp.swapaxes(xin[q, 8:16, rows, :], 0, 1)
            for n in (0, 1, 4, 5):
                b = n + 2 * half
                even, odd = interleave(
                    early[b] * factor[0][q], late[b] * factor[1][q], low
                )
                sb[base + n // 4 + 4 * q, b % 4] = even
                sb[base + n // 4 + 4 * q + 2, b % 4] = odd

    pl.loop(0, 4)(functools.partial(arrange, 0))

    groups = (pl.ds(0, 2), pl.ds(2, 1), pl.ds(3, 1))

    def send_columns(group, to):
        pltpu.make_async_remote_copy(
            sb.at[to, groups[group]], rb.at[me, groups[group]], s1.at[group], r1.at[group],
            device_id=(to, sx), device_id_type=MESH,
        ).start()

    def target(k):
        i = k & 7
        dz = jnp.where((i & 1) == 1, (i + 1) >> 1, 8 - (i >> 1))
        to = (((y + (k >> 4)) & 3) << 4) + (((z + dz) & 7) << 1)
        return to + (c ^ ((k >> 3) & 1))

    def send_rest(group):
        @pl.loop(1, 64)
        def _(k):
            send_columns(group, target(64 - k))

    pl.semaphore_wait(barrier, 15 + 3 + 3)
    for k in range(1, 4):
        greet(step_sem, (me + 16 * k) & 63, sx)

    @pl.loop(1, 16)
    def _(k):
        send_columns(0, target(k))

    pl.loop(0, 4)(functools.partial(arrange, 1))
    pl.semaphore_wait(step_sem, 3)

    @pl.loop(16, 64)
    def _(k):
        send_columns(0, target(79 - k))

    send_rest(1)
    send_rest(2)

    rb[me] = sb[me]

    load_tab.wait()
    low64 = lax.broadcasted_iota(jnp.int32, (64, 128), 1) < 64
    low16 = lax.broadcasted_iota(jnp.int32, (16, 128), 1) < 64
    for h in range(4):
        if h != 1:
            landed = rb.at[pl.ds(0, 63), groups[max(h - 1, 0)]]
            pltpu.make_async_copy(landed, landed, r1.at[max(h - 1, 0)]).wait()

        @pl.loop(0, 4)
        def _(i):
            first = rb[pl.ds(i * 8, 8), h].reshape(64, 128)
            second = rb[pl.ds(32 + i * 8, 8), h].reshape(64, 128)
            for parity, value in enumerate((first + second, first - second)):
                high = value.astype(BF16).astype(F32)
                early, late = interleave(high, value - high, low64)
                eh[parity, pl.ds(i * 64, 64), :] = early.astype(BF16)
                eh[parity, pl.ds(256 + i * 64, 64), :] = late.astype(BF16)

        here = pl.ds(pl.multiple_of((sx * 32 + 4 * p + h) * 16 + 8, 8), 16)
        turn = 4 * (p & 1) + h

        @pl.loop(0, 2)
        def _(step):
            first_y = y ^ 2 ^ (3 * step)
            parity = first_y >> 1
            product = dot(tab[parity], eh[parity])
            total = product[0:512] + product[512:1024]
            total = total + pltpu.roll(total, 64, 1)
            for n in range(16):
                for m in (32 * n, 32 * n + 8):
                    tile = jnp.where(low, total[m : m + 8], total[m + 16 : m + 24])
                    ob[h, parity * 16 + n, m % 32 : m % 32 + 8, :] = pltpu.roll(tile, turn, 0)

            @pl.loop(0, 16 - step)
            def _(k):
                dx = k & 3
                dx = jnp.where(dx < 2, 2 - dx, 3 * (3 - dx))
                px, py, pc = (sx + dx) & 3, first_y ^ (k >> 3), c ^ 1 ^ ((k >> 2) & 1)
                g = unit_of(px, py, pc)
                pltpu.make_async_remote_copy(
                    ob.at[h, (g & 1) * 16 + (g >> 1)], db.at[here], s2, r2,
                    device_id=((py << 4) + (z << 1) + pc, px), device_id_type=MESH,
                ).start()

        db[here, :] = ob[h, (unit & 1) * 16 + (unit >> 1)]

    pltpu.make_async_copy(db.at[pl.ds(0, 124 * 16)], db.at[pl.ds(0, 124 * 16)], r2).wait()

    low32 = lax.broadcasted_iota(jnp.int32, (32, 128), 1) < 64

    def slot_rows(x, j):
        wrapped = row + (j & 7) >= 8
        tiles = []
        for g in range(4):
            start = 8 + x * 512 + g * 128 + j
            plain = db[pl.ds(start, 8, stride=17), :]
            back = db[pl.ds(start - 8, 8, stride=17), :]
            tiles.append(jnp.where(wrapped, back, plain))
        return jnp.concatenate(tiles, axis=0)

    @pl.loop(0, 8)
    def _(i):
        zt = far_first(z, i)
        grams = []
        for f in range(2):
            j = zt * 2 + f
            keep = jnp.where((unit == 0) & (j == 0), 0.0, 1.0).astype(F32)
            real, imag = [], []
            for x in range(0, NX, 2):
                first = slot_rows(x, j)
                second = slot_rows(x + 1, j)
                r, m = interleave(first, second, low32)
                real.append(r)
                imag.append(m)
            real_h, real_l = split(jnp.concatenate(real, axis=1))
            imag_h, imag_l = split(jnp.concatenate(imag, axis=1))
            left_h = jnp.concatenate([real_h, imag_h], axis=1)
            left_l = jnp.concatenate([real_l, imag_l], axis=1)
            base = pl.multiple_of(j * 32, 32)
            mh[pl.ds(base, 32), :] = left_h
            ml[pl.ds(base, 32), :] = left_l
            lone_part = (1.0 - keep).astype(BF16)
            keep = keep.astype(BF16)
            right = []
            for r, m in ((real_h, imag_h), (real_l, imag_l)):
                kept = m * keep
                right.append(jnp.concatenate([r, kept], axis=1))
                right.append(jnp.concatenate([kept, m * lone_part - r * keep], axis=1))
            product = dot_nt(
                jnp.concatenate([left_h, left_l], axis=0), jnp.concatenate(right, axis=0)
            )
            total = product[0:32] + product[32:64]
            grams.append(total + pltpu.roll(total, 64, 1))
        pair = jnp.where(low32, grams[0], grams[1])

        @pl.when(i < 7)
        def _():
            go[zt] = pair
            pltpu.make_async_remote_copy(
                go.at[zt], gr.at[z], s3, r3,
                device_id=((y << 4) + (zt << 1) + c, sx), device_id_type=MESH,
            ).start()

        @pl.when(i == 7)
        def _():
            gr[z] = pair

    pltpu.make_async_copy(gr.at[pl.ds(0, 7)], gr.at[pl.ds(0, 7)], r3).wait()
    gram = gr[0]
    for k in range(1, 8):
        gram = gram + gr[k]
    gram_h, gram_l = split(gram * (1.0 / 2048.0))
    gram = jnp.concatenate([gram_h, gram_l], axis=1)

    even = row % 2 == 0
    lone = (row < 2) & (unit == 0) & (z == 0)
    valid = (lane < 32) & (row < 4)

    def swap_rows(v):
        return jnp.where(even, pltpu.roll(v, 7, 0), pltpu.roll(v, 1, 0))

    def image_of(v):
        high = v.astype(BF16).astype(F32)
        both = jnp.where(row < 4, high, pltpu.roll(v - high, 4, 0)).astype(BF16)
        product = dot(both[:, 0:32], gram)
        product = product[:, 0:128] + product[:, 128:256]
        product = product + pltpu.roll(product, 4, 0)
        chosen = jnp.where(row < 2, product, pltpu.roll(product, 64, 1))
        other = pltpu.roll(chosen, 96, 1)
        crossed = swap_rows(other)
        normal = jnp.where(even, chosen + crossed, chosen - crossed)
        alone = jnp.where(even, chosen, other)
        return jnp.where(valid, jnp.where(lone, alone, normal), 0.0)

    def pair_sum(v):
        total = jnp.broadcast_to(jnp.sum(v, axis=1, keepdims=True), (8, 128))
        return jnp.where(lone, total, total + swap_rows(total))

    vec = jnp.where(valid & (even | lone), 1.0 / math.sqrt(32.0), 0.0).astype(F32)
    for _ in range(POWER):
        new = image_of(vec)
        vec = new * lax.rsqrt(pair_sum(new * new) + 1e-06)
    energy = pair_sum(vec * image_of(vec))
    scaled = vec * lax.rsqrt(energy + 1e-06)
    spread = scaled + pltpu.roll(scaled, 32, 1)
    spread = spread + pltpu.roll(spread, 64, 1)
    place = (z & 1) * 2 + row // 2 == lane // 32
    message = jnp.zeros((8, 128), F32)
    for n, value in enumerate((spread, spread, energy, energy)):
        chosen = jnp.where(place & (row & 1 == n % 2), value, 0.0)
        message = jnp.where(row == n, jnp.sum(chosen, axis=0, keepdims=True), message)
    vs[...] = message
    va[z] = message

    @pl.loop(0, 7)
    def _(i):
        zt = far_first(z, i)
        pltpu.make_async_remote_copy(
            vs, va.at[z], s4, r4,
            device_id=((y << 4) + (zt << 1) + c, sx), device_id_type=MESH,
        ).start()

    rows = lax.broadcasted_iota(jnp.int32, (32, 128), 0)
    lanes = lax.broadcasted_iota(jnp.int32, (32, 128), 1)
    ver, j = rows // 16, rows % 16
    first_unit = unit == 0
    slot = jnp.where(ver == 0, j, 15 - j)
    slot_first = jnp.where(
        ver == 0,
        jnp.where(j < 8, j, jnp.where(j == 8, 0, 16 - j)),
        jnp.where(j < 8, 8 + j, 23 - j),
    )
    slot = jnp.where(first_unit, slot_first, slot)
    flip = jnp.where(jnp.where(first_unit, j // 8, ver) == 1, -1.0, 1.0)
    direct = first_unit & (ver == 0) & (j == 0)
    nyquist = first_unit & (ver == 0) & (j == 8)
    alone = direct | nyquist
    real_by_real = jnp.where(nyquist, 0.0, 1.0)
    real_by_imag = jnp.where(direct, 0.0, jnp.where(nyquist, 1.0, -1.0))
    imag_by_any = jnp.where(alone, 0.0, flip)
    lane_slot = lanes // 32
    lead = lanes % 32 == 0

    pltpu.make_async_copy(va.at[pl.ds(0, 7)], va.at[pl.ds(0, 7)], r4).wait()

    energies = jnp.zeros((32, 128), F32)
    lefts = []
    for k in range(4):
        v = va[2 * k] + va[2 * k + 1]
        here = slot == 4 * k + lane_slot
        lefts.append(
            jnp.concatenate(
                [jnp.where(here, v[0:1, :], 0.0), jnp.where(here, v[1:2, :], 0.0)], axis=0
            )
        )
        energy = jnp.where(nyquist, v[3:4, :], v[2:3, :])
        energies = energies + jnp.where(here & lead, energy, 0.0)
    lh, ll = split(jnp.concatenate(lefts, axis=1))
    modes = dot(jnp.concatenate([lh, ll], axis=0), mh[...])
    modes = modes[0:64] + (modes[64:128] + dot(lh, ml[...]))
    energies = jnp.broadcast_to(jnp.sum(energies, axis=1, keepdims=True), (32, 128))

    sends = []
    for ver in range(2):
        if ver == 0:
            klass = unit
        else:
            klass = jnp.where(unit == 0, 32, 64 - unit)
        to = bit_reverse(klass)
        base = 16 * ver
        energy_tile = jnp.where(low, energies[base : base + 8], energies[base + 8 : base + 16])
        for px in range(4):
            n = ver * 4 + px
            at_real = 128 * (px // 2)
            at_imag = 256 + at_real
            part = slice(base, base + 16)
            twin = slice(base + 32, base + 48)
            real = (
                modes[part, at_real : at_real + 128] * real_by_real[part]
                + modes[twin, at_imag : at_imag + 128] * real_by_imag[part]
            )
            imag = (
                modes[part, at_imag : at_imag + 128] + modes[twin, at_real : at_real + 128]
            ) * imag_by_any[part]
            if px % 2 == 0:
                fs[n, 0:16, :] = jnp.where(low16, real, pltpu.roll(imag, 64, 1))
            else:
                fs[n, 0:16, :] = jnp.where(low16, pltpu.roll(real, 64, 1), imag)
            fs[n, 16:24, :] = energy_tile
            send = pltpu.make_async_remote_copy(
                fs.at[n], fb.at[z], s5.at[n], r5.at[z],
                device_id=(to, px), device_id_type=MESH,
            )
            kept = (to == me) & (px == sx)
            sends.append((send, kept))

            @pl.when(jnp.logical_not(kept))
            def _():
                send.start()

            @pl.when(kept)
            def _():
                fb[z] = fs[n]

    mine = bit_reverse(me)
    my_unit = jnp.where(mine == 32, 0, jnp.where(mine > 32, 64 - mine, mine))
    same_group = my_unit == unit
    for k in range(8):

        @pl.when(jnp.logical_not(same_group & (z == k)))
        def _():
            pltpu.make_async_copy(fb.at[k], fb.at[k], r5.at[k]).wait()

    for q in range(4):
        real, imag = interleave(fb[2 * q, 0:16, :], fb[2 * q + 1, 0:16, :], low16)
        scale = unscale[:, 128 * q : 128 * q + 128]
        out_ref[0:16, 128 * q : 128 * q + 128] = real * scale
        out_ref[16:32, 128 * q : 128 * q + 128] = imag * scale
    tile = fb[0, 16:24, :]
    turned = pltpu.roll(tile, 64, 1)
    diagonal = jnp.where(lane == row, tile, 0.0) + jnp.where(lane == row + 8, turned, 0.0)
    e_ref[...] = jnp.sum(diagonal, axis=0, keepdims=True)[:, 0:16]

    for group in range(3):
        left = sb.at[pl.ds(0, 63), groups[group]]
        pltpu.make_async_copy(left, left, s1.at[group]).wait()
    pltpu.make_async_copy(db.at[pl.ds(0, 124 * 16)], db.at[pl.ds(0, 124 * 16)], s2).wait()
    pltpu.make_async_copy(gr.at[pl.ds(0, 7)], gr.at[pl.ds(0, 7)], s3).wait()
    pltpu.make_async_copy(va.at[pl.ds(0, 7)], va.at[pl.ds(0, 7)], s4).wait()
    for send, kept in sends:

        @pl.when(jnp.logical_not(kept))
        def _():
            send.wait_send()


def hand_over(modes_ref, e_ref, modes_hbm, e_hbm, sem):
    copies = [
        pltpu.make_async_copy(modes_ref, modes_hbm, sem.at[0]),
        pltpu.make_async_copy(e_ref, e_hbm, sem.at[1]),
    ]
    for copy in copies:
        copy.start()
    for copy in copies:
        copy.wait()


def body(snapshots, quad_weights):
    times, blocks, points = snapshots.shape
    table = jnp.asarray(transform_table())
    any_spec = pl.BlockSpec(memory_space=pl.ANY)
    vmem = pl.BlockSpec(memory_space=pltpu.VMEM)
    dma = pltpu.SemaphoreType.DMA
    weights = quad_weights.reshape(1, points)
    modes, energies = pl.pallas_call(
        kernel,
        out_shape=(pltpu.VMEM((32, 512), F32), pltpu.VMEM((1, 16), F32)),
        in_specs=[any_spec, any_spec, any_spec],
        out_specs=(vmem, vmem),
        scratch_shapes=[
            pltpu.VMEM((4, 16, 32, 128), F32),
            pltpu.VMEM((1, 512), F32),
            pltpu.VMEM((2, 1024, 512), BF16),
            pltpu.VMEM((64, 4, 8, 128), F32),
            pltpu.VMEM((64, 4, 8, 128), F32),
            pltpu.VMEM((2, 512, 128), BF16),
            pltpu.VMEM((4, 32, 16, 128), F32),
            pltpu.VMEM((2064, 128), F32),
            pltpu.VMEM((512, 512), BF16),
            pltpu.VMEM((512, 512), BF16),
            pltpu.VMEM((8, 32, 128), F32),
            pltpu.VMEM((8, 32, 128), F32),
            pltpu.VMEM((8, 128), F32),
            pltpu.VMEM((8, 8, 128), F32),
            pltpu.VMEM((8, 24, 128), F32),
            pltpu.VMEM((8, 24, 128), F32),
            dma((4,)), dma, dma, pltpu.SemaphoreType.REGULAR,
            dma((3,)), dma((3,)),
            dma, dma, dma, dma, dma, dma,
            dma((8,)), dma((8,)),
        ],
        compiler_params=pltpu.CompilerParams(collective_id=0, has_side_effects=True),
        name="spod",
    )(snapshots, table, weights)
    modes, energies = pl.pallas_call(
        hand_over,
        out_shape=(
            jax.ShapeDtypeStruct((32, points), F32),
            jax.ShapeDtypeStruct((1, 16), F32),
        ),
        in_specs=[vmem, vmem],
        out_specs=(any_spec, any_spec),
        scratch_shapes=[dma((2,))],
        name="hand_over",
    )(
        pltpu.with_memory_space_constraint(modes, pltpu.VMEM),
        pltpu.with_memory_space_constraint(energies, pltpu.VMEM),
    )
    return modes.reshape(2, 16, points), energies.reshape(16)


def solution(mesh):
    return jax.shard_map(
        body,
        mesh=mesh,
        in_specs=(P("tm", None, "space"), P("space")),
        out_specs=(P(None, "tm", "space"), P("tm")),
        check_vma=False,
    )
```

```python
import functools
import math

import jax
import jax.numpy as jnp
import numpy as np
from jax import lax
from jax.experimental import pallas as pl
from jax.experimental.pallas import tpu as pltpu
from jax.sharding import PartitionSpec as P

POWER = 3
F32 = jnp.float32
BF16 = jnp.bfloat16
MESH = pl.DeviceIdType.MESH
NT = 1024
NX, NY, NZ, NC = 4, 4, 8, 2


def transform_table():
    t = np.arange(NT // 2).reshape(32, 2, 8).transpose(1, 0, 2).reshape(-1)
    rows = []
    for unit in list(range(0, 32, 2)) + list(range(1, 32, 2)):
        if unit == 0:
            freq = np.array([64 * j for j in range(8)] + [32 + 64 * j for j in range(8)])
        else:
            freq = unit + 64 * np.arange(16)
        angle = 2.0 * np.pi * ((freq[:, None] * t[None, :]) % NT) / NT
        real, imag = np.cos(angle), -np.sin(angle)
        if unit == 0:
            imag[0] = np.cos(np.pi * t)
        rows += [real, imag]
    table = np.concatenate(rows).astype(np.float32)
    high = table.astype(jnp.bfloat16)
    low = (table - high.astype(np.float32)).astype(jnp.bfloat16)
    return np.stack([high.reshape(2, 512, 512), low.reshape(2, 512, 512)], axis=1).reshape(2, 1024, 512)


def split(x):
    high = x.astype(BF16)
    return high, (x - high.astype(F32)).astype(BF16)


def dot(a, b):
    return jnp.dot(a, b, preferred_element_type=F32)


def dot_nt(a, b):
    return lax.dot_general(a, b, (((1,), (1,)), ((), ())), preferred_element_type=F32)


def interleave(first, second, low):
    crossed = pltpu.roll(jnp.where(low, second, first), 64, 1)
    return jnp.where(low, first, crossed), jnp.where(low, crossed, second)


def bit_reverse(value):
    result = 0
    for position in range(6):
        result = result + ((value >> position) & 1) * (1 << (5 - position))
    return result


def unit_of(x, y, c):
    return c * 16 + x * 4 + ((y & 1) << 1) + (y >> 1)


def far_first(z, i):
    return (z + jnp.where((i & 1) == 1, 4 - ((i + 1) >> 1), 4 + (i >> 1))) & 7


def kernel(
    x_hbm, tab_hbm, w_hbm, out_ref, e_ref,
    xin, w_ref, tab, sb, rb, eh, ob, db, mh, ml, go, gr, vs, va, fs, fb,
    in_sem, w_sem, tab_sem, step_sem, s1, r1, s2, r2, s3, r3, s4, r4, s5, r5,
):
    me = lax.axis_index("tm")
    sx = lax.axis_index("space")
    y, z, c = me >> 4, (me >> 1) & 7, me & 1
    p = y * 2 + c
    unit = unit_of(sx, y, c)

    loads = [
        pltpu.make_async_copy(x_hbm.at[:, :, pl.ds(q * 128, 128)], xin.at[q], in_sem.at[q])
        for q in range(4)
    ]
    for load in loads:
        load.start()
    load_w = pltpu.make_async_copy(w_hbm, w_ref, w_sem)
    load_w.start()
    load_tab = pltpu.make_async_copy(tab_hbm, tab, tab_sem)

    barrier = pltpu.get_barrier_semaphore()

    def greet(semaphore, tm, space):
        pl.semaphore_signal(semaphore, 1, device_id=(tm, space), device_id_type=MESH)

    @pl.loop(0, 15)
    def _(k):
        greet(barrier, (me & 48) + (far_first(z, k >> 1) << 1) + (c ^ 1 ^ (k & 1)), sx)

    @pl.loop(1, 4)
    def _(k):
        greet(barrier, (me + 16 * k) & 63, sx)
        greet(barrier, me, (sx + k) & 3)

    lane = lax.broadcasted_iota(jnp.int32, (8, 128), 1)
    row = lax.broadcasted_iota(jnp.int32, (8, 128), 0)
    low = lane < 64
    load_tab.start()
    load_w.wait()
    root_w = jnp.sqrt(w_ref[...])
    unscale = lax.rsqrt(w_ref[...])
    for load in loads:
        load.wait()
    factor = []
    for sh in range(2):
        phase = (row + (16 * me + 8 * sh - NT // 2)).astype(F32) * (math.pi / NT)
        square = phase * phase
        cosine = jnp.full((8, 128), 1.0 / math.factorial(16), F32)
        for n in range(14, -1, -2):
            cosine = cosine * square + (-1.0) ** (n // 2) / math.factorial(n)
        window = cosine * cosine * (1.0 / math.sqrt(0.375 * NT))
        factor.append([window * root_w[:, 128 * q : 128 * q + 128] for q in range(4)])

    def arrange(half, bt):
        rows = pl.ds(pl.multiple_of(bt * 8, 8), 8)
        base = bt * 16
        for q in range(4):
            early = jnp.swapaxes(xin[q, 0:8, rows, :], 0, 1)
            late = jnp.swapaxes(xin[q, 8:16, rows, :], 0, 1)
            for n in (0, 1, 4, 5):
                b = n + 2 * half
                even, odd = interleave(
                    early[b] * factor[0][q], late[b] * factor[1][q], low
                )
                sb[base + n // 4 + 4 * q, b % 4] = even
                sb[base + n // 4 + 4 * q + 2, b % 4] = odd

    pl.loop(0, 4)(functools.partial(arrange, 0))

    groups = (pl.ds(0, 2), pl.ds(2, 1), pl.ds(3, 1))

    def send_columns(group, to):
        pltpu.make_async_remote_copy(
            sb.at[to, groups[group]], rb.at[me, groups[group]], s1.at[group], r1.at[group],
            device_id=(to, sx), device_id_type=MESH,
        ).start()

    def target(k):
        i = k & 7
        dz = jnp.where((i & 1) == 1, (i + 1) >> 1, 8 - (i >> 1))
        to = (((y + (k >> 4)) & 3) << 4) + (((z + dz) & 7) << 1)
        return to + (c ^ ((k >> 3) & 1))

    def send_rest(group):
        @pl.loop(1, 64)
        def _(k):
            send_columns(group, target((64 - k) ^ jnp.where(64 - k >= 32, 16, 0)))

    pl.semaphore_wait(barrier, 15 + 3 + 3)
    for k in range(1, 4):
        greet(step_sem, (me + 16 * k) & 63, sx)

    @pl.loop(1, 16)
    def _(k):
        send_columns(0, target(k))

    pl.loop(0, 4)(functools.partial(arrange, 1))
    pl.semaphore_wait(step_sem, 3)

    @pl.loop(16, 64)
    def _(k):
        send_columns(0, target(79 - k))

    send_rest(1)
    send_rest(2)

    rb[me] = sb[me]

    load_tab.wait()
    low64 = lax.broadcasted_iota(jnp.int32, (64, 128), 1) < 64
    low16 = lax.broadcasted_iota(jnp.int32, (16, 128), 1) < 64
    for h in range(4):
        if h != 1:
            landed = rb.at[pl.ds(0, 63), groups[max(h - 1, 0)]]
            pltpu.make_async_copy(landed, landed, r1.at[max(h - 1, 0)]).wait()

        @pl.loop(0, 4)
        def _(i):
            first = rb[pl.ds(i * 8, 8), h].reshape(64, 128)
            second = rb[pl.ds(32 + i * 8, 8), h].reshape(64, 128)
            for parity, value in enumerate((first + second, first - second)):
                high = value.astype(BF16).astype(F32)
                early, late = interleave(high, value - high, low64)
                eh[parity, pl.ds(i * 64, 64), :] = early.astype(BF16)
                eh[parity, pl.ds(256 + i * 64, 64), :] = late.astype(BF16)

        here = pl.ds(pl.multiple_of((sx * 32 + 4 * p + h) * 16 + 8, 8), 16)
        turn = 4 * (p & 1) + h

        @pl.loop(0, 2)
        def _(step):
            first_y = y ^ 2 ^ (3 * step)
            parity = first_y >> 1
            product = dot(tab[parity], eh[parity])
            total = product[0:512] + product[512:1024]
            total = total + pltpu.roll(total, 64, 1)
            for n in range(16):
                for m in (32 * n, 32 * n + 8):
                    tile = jnp.where(low, total[m : m + 8], total[m + 16 : m + 24])
                    ob[h, parity * 16 + n, m % 32 : m % 32 + 8, :] = pltpu.roll(tile, turn, 0)

            @pl.loop(0, 16 - step)
            def _(k):
                dx = k & 3
                dx = jnp.where(dx < 2, 2 - dx, 3 * (3 - dx))
                px, py, pc = (sx + dx) & 3, first_y ^ (k >> 3), c ^ 1 ^ ((k >> 2) & 1)
                g = unit_of(px, py, pc)
                pltpu.make_async_remote_copy(
                    ob.at[h, (g & 1) * 16 + (g >> 1)], db.at[here], s2, r2,
                    device_id=((py << 4) + (z << 1) + pc, px), device_id_type=MESH,
                ).start()

        db[here, :] = ob[h, (unit & 1) * 16 + (unit >> 1)]

    pltpu.make_async_copy(db.at[pl.ds(0, 124 * 16)], db.at[pl.ds(0, 124 * 16)], r2).wait()

    low32 = lax.broadcasted_iota(jnp.int32, (32, 128), 1) < 64

    def slot_rows(x, j):
        wrapped = row + (j & 7) >= 8
        tiles = []
        for g in range(4):
            start = 8 + x * 512 + g * 128 + j
            plain = db[pl.ds(start, 8, stride=17), :]
            back = db[pl.ds(start - 8, 8, stride=17), :]
            tiles.append(jnp.where(wrapped, back, plain))
        return jnp.concatenate(tiles, axis=0)

    @pl.loop(0, 8)
    def _(i):
        zt = far_first(z, i)
        grams = []
        for f in range(2):
            j = zt * 2 + f
            keep = jnp.where((unit == 0) & (j == 0), 0.0, 1.0).astype(F32)
            real, imag = [], []
            for x in range(0, NX, 2):
                first = slot_rows(x, j)
                second = slot_rows(x + 1, j)
                r, m = interleave(first, second, low32)
                real.append(r)
                imag.append(m)
            real_h, real_l = split(jnp.concatenate(real, axis=1))
            imag_h, imag_l = split(jnp.concatenate(imag, axis=1))
            left_h = jnp.concatenate([real_h, imag_h], axis=1)
            left_l = jnp.concatenate([real_l, imag_l], axis=1)
            base = pl.multiple_of(j * 32, 32)
            mh[pl.ds(base, 32), :] = left_h
            ml[pl.ds(base, 32), :] = left_l
            lone_part = (1.0 - keep).astype(BF16)
            keep = keep.astype(BF16)
            right = []
            for r, m in ((real_h, imag_h), (real_l, imag_l)):
                kept = m * keep
                right.append(jnp.concatenate([r, kept], axis=1))
                right.append(jnp.concatenate([kept, m * lone_part - r * keep], axis=1))
            product = dot_nt(
                jnp.concatenate([left_h, left_l], axis=0), jnp.concatenate(right, axis=0)
            )
            total = product[0:32] + product[32:64]
            grams.append(total + pltpu.roll(total, 64, 1))
        pair = jnp.where(low32, grams[0], grams[1])

        @pl.when(i < 7)
        def _():
            go[zt] = pair
            pltpu.make_async_remote_copy(
                go.at[zt], gr.at[z], s3, r3,
                device_id=((y << 4) + (zt << 1) + c, sx), device_id_type=MESH,
            ).start()

        @pl.when(i == 7)
        def _():
            gr[z] = pair

    pltpu.make_async_copy(gr.at[pl.ds(0, 7)], gr.at[pl.ds(0, 7)], r3).wait()
    gram = gr[0]
    for k in range(1, 8):
        gram = gram + gr[k]
    gram_h, gram_l = split(gram * (1.0 / 2048.0))
    gram = jnp.concatenate([gram_h, gram_l], axis=1)

    even = row % 2 == 0
    lone = (row < 2) & (unit == 0) & (z == 0)
    valid = (lane < 32) & (row < 4)

    def swap_rows(v):
        return jnp.where(even, pltpu.roll(v, 7, 0), pltpu.roll(v, 1, 0))

    def image_of(v):
        high = v.astype(BF16).astype(F32)
        both = jnp.where(row < 4, high, pltpu.roll(v - high, 4, 0)).astype(BF16)
        product = dot(both[:, 0:32], gram)
        product = product[:, 0:128] + product[:, 128:256]
        product = product + pltpu.roll(product, 4, 0)
        chosen = jnp.where(row < 2, product, pltpu.roll(product, 64, 1))
        other = pltpu.roll(chosen, 96, 1)
        crossed = swap_rows(other)
        normal = jnp.where(even, chosen + crossed, chosen - crossed)
        alone = jnp.where(even, chosen, other)
        return jnp.where(valid, jnp.where(lone, alone, normal), 0.0)

    def pair_sum(v):
        total = jnp.broadcast_to(jnp.sum(v, axis=1, keepdims=True), (8, 128))
        return jnp.where(lone, total, total + swap_rows(total))

    vec = jnp.where(valid & (even | lone), 1.0 / math.sqrt(32.0), 0.0).astype(F32)
    for _ in range(POWER):
        new = image_of(vec)
        vec = new * lax.rsqrt(pair_sum(new * new) + 1e-06)
    energy = pair_sum(vec * image_of(vec))
    scaled = vec * lax.rsqrt(energy + 1e-06)
    spread = scaled + pltpu.roll(scaled, 32, 1)
    spread = spread + pltpu.roll(spread, 64, 1)
    place = (z & 1) * 2 + row // 2 == lane // 32
    message = jnp.zeros((8, 128), F32)
    for n, value in enumerate((spread, spread, energy, energy)):
        chosen = jnp.where(place & (row & 1 == n % 2), value, 0.0)
        message = jnp.where(row == n, jnp.sum(chosen, axis=0, keepdims=True), message)
    vs[...] = message
    va[z] = message

    @pl.loop(0, 7)
    def _(i):
        zt = far_first(z, i)
        pltpu.make_async_remote_copy(
            vs, va.at[z], s4, r4,
            device_id=((y << 4) + (zt << 1) + c, sx), device_id_type=MESH,
        ).start()

    rows = lax.broadcasted_iota(jnp.int32, (32, 128), 0)
    lanes = lax.broadcasted_iota(jnp.int32, (32, 128), 1)
    ver, j = rows // 16, rows % 16
    first_unit = unit == 0
    slot = jnp.where(ver == 0, j, 15 - j)
    slot_first = jnp.where(
        ver == 0,
        jnp.where(j < 8, j, jnp.where(j == 8, 0, 16 - j)),
        jnp.where(j < 8, 8 + j, 23 - j),
    )
    slot = jnp.where(first_unit, slot_first, slot)
    flip = jnp.where(jnp.where(first_unit, j // 8, ver) == 1, -1.0, 1.0)
    direct = first_unit & (ver == 0) & (j == 0)
    nyquist = first_unit & (ver == 0) & (j == 8)
    alone = direct | nyquist
    real_by_real = jnp.where(nyquist, 0.0, 1.0)
    real_by_imag = jnp.where(direct, 0.0, jnp.where(nyquist, 1.0, -1.0))
    imag_by_any = jnp.where(alone, 0.0, flip)
    lane_slot = lanes // 32
    lead = lanes % 32 == 0

    pltpu.make_async_copy(va.at[pl.ds(0, 7)], va.at[pl.ds(0, 7)], r4).wait()

    energies = jnp.zeros((32, 128), F32)
    lefts = []
    for k in range(4):
        v = va[2 * k] + va[2 * k + 1]
        here = slot == 4 * k + lane_slot
        lefts.append(
            jnp.concatenate(
                [jnp.where(here, v[0:1, :], 0.0), jnp.where(here, v[1:2, :], 0.0)], axis=0
            )
        )
        energy = jnp.where(nyquist, v[3:4, :], v[2:3, :])
        energies = energies + jnp.where(here & lead, energy, 0.0)
    lh, ll = split(jnp.concatenate(lefts, axis=1))
    modes = dot(jnp.concatenate([lh, ll], axis=0), mh[...])
    modes = modes[0:64] + (modes[64:128] + dot(lh, ml[...]))
    energies = jnp.broadcast_to(jnp.sum(energies, axis=1, keepdims=True), (32, 128))

    sends = []
    for ver in range(2):
        if ver == 0:
            klass = unit
        else:
            klass = jnp.where(unit == 0, 32, 64 - unit)
        to = bit_reverse(klass)
        base = 16 * ver
        energy_tile = jnp.where(low, energies[base : base + 8], energies[base + 8 : base + 16])
        for px in range(4):
            n = ver * 4 + px
            at_real = 128 * (px // 2)
            at_imag = 256 + at_real
            part = slice(base, base + 16)
            twin = slice(base + 32, base + 48)
            real = (
                modes[part, at_real : at_real + 128] * real_by_real[part]
                + modes[twin, at_imag : at_imag + 128] * real_by_imag[part]
            )
            imag = (
                modes[part, at_imag : at_imag + 128] + modes[twin, at_real : at_real + 128]
            ) * imag_by_any[part]
            if px % 2 == 0:
                fs[n, 0:16, :] = jnp.where(low16, real, pltpu.roll(imag, 64, 1))
            else:
                fs[n, 0:16, :] = jnp.where(low16, pltpu.roll(real, 64, 1), imag)
            fs[n, 16:24, :] = energy_tile
            send = pltpu.make_async_remote_copy(
                fs.at[n], fb.at[z], s5.at[n], r5.at[z],
                device_id=(to, px), device_id_type=MESH,
            )
            kept = (to == me) & (px == sx)
            sends.append((send, kept))

            @pl.when(jnp.logical_not(kept))
            def _():
                send.start()

            @pl.when(kept)
            def _():
                fb[z] = fs[n]

    mine = bit_reverse(me)
    my_unit = jnp.where(mine == 32, 0, jnp.where(mine > 32, 64 - mine, mine))
    same_group = my_unit == unit
    for k in range(8):

        @pl.when(jnp.logical_not(same_group & (z == k)))
        def _():
            pltpu.make_async_copy(fb.at[k], fb.at[k], r5.at[k]).wait()

    for q in range(4):
        real, imag = interleave(fb[2 * q, 0:16, :], fb[2 * q + 1, 0:16, :], low16)
        scale = unscale[:, 128 * q : 128 * q + 128]
        out_ref[0:16, 128 * q : 128 * q + 128] = real * scale
        out_ref[16:32, 128 * q : 128 * q + 128] = imag * scale
    tile = fb[0, 16:24, :]
    turned = pltpu.roll(tile, 64, 1)
    diagonal = jnp.where(lane == row, tile, 0.0) + jnp.where(lane == row + 8, turned, 0.0)
    e_ref[...] = jnp.sum(diagonal, axis=0, keepdims=True)[:, 0:16]

    for group in range(3):
        left = sb.at[pl.ds(0, 63), groups[group]]
        pltpu.make_async_copy(left, left, s1.at[group]).wait()
    pltpu.make_async_copy(db.at[pl.ds(0, 124 * 16)], db.at[pl.ds(0, 124 * 16)], s2).wait()
    pltpu.make_async_copy(gr.at[pl.ds(0, 7)], gr.at[pl.ds(0, 7)], s3).wait()
    pltpu.make_async_copy(va.at[pl.ds(0, 7)], va.at[pl.ds(0, 7)], s4).wait()
    for send, kept in sends:

        @pl.when(jnp.logical_not(kept))
        def _():
            send.wait_send()


def hand_over(modes_ref, e_ref, modes_hbm, e_hbm, sem):
    copies = [
        pltpu.make_async_copy(modes_ref, modes_hbm, sem.at[0]),
        pltpu.make_async_copy(e_ref, e_hbm, sem.at[1]),
    ]
    for copy in copies:
        copy.start()
    for copy in copies:
        copy.wait()


def body(snapshots, quad_weights):
    times, blocks, points = snapshots.shape
    table = jnp.asarray(transform_table())
    any_spec = pl.BlockSpec(memory_space=pl.ANY)
    vmem = pl.BlockSpec(memory_space=pltpu.VMEM)
    dma = pltpu.SemaphoreType.DMA
    weights = quad_weights.reshape(1, points)
    modes, energies = pl.pallas_call(
        kernel,
        out_shape=(pltpu.VMEM((32, 512), F32), pltpu.VMEM((1, 16), F32)),
        in_specs=[any_spec, any_spec, any_spec],
        out_specs=(vmem, vmem),
        scratch_shapes=[
            pltpu.VMEM((4, 16, 32, 128), F32),
            pltpu.VMEM((1, 512), F32),
            pltpu.VMEM((2, 1024, 512), BF16),
            pltpu.VMEM((64, 4, 8, 128), F32),
            pltpu.VMEM((64, 4, 8, 128), F32),
            pltpu.VMEM((2, 512, 128), BF16),
            pltpu.VMEM((4, 32, 16, 128), F32),
            pltpu.VMEM((2064, 128), F32),
            pltpu.VMEM((512, 512), BF16),
            pltpu.VMEM((512, 512), BF16),
            pltpu.VMEM((8, 32, 128), F32),
            pltpu.VMEM((8, 32, 128), F32),
            pltpu.VMEM((8, 128), F32),
            pltpu.VMEM((8, 8, 128), F32),
            pltpu.VMEM((8, 24, 128), F32),
            pltpu.VMEM((8, 24, 128), F32),
            dma((4,)), dma, dma, pltpu.SemaphoreType.REGULAR,
            dma((3,)), dma((3,)),
            dma, dma, dma, dma, dma, dma,
            dma((8,)), dma((8,)),
        ],
        compiler_params=pltpu.CompilerParams(collective_id=0, has_side_effects=True),
        name="spod",
    )(snapshots, table, weights)
    modes, energies = pl.pallas_call(
        hand_over,
        out_shape=(
            jax.ShapeDtypeStruct((32, points), F32),
            jax.ShapeDtypeStruct((1, 16), F32),
        ),
        in_specs=[vmem, vmem],
        out_specs=(any_spec, any_spec),
        scratch_shapes=[dma((2,))],
        name="hand_over",
    )(
        pltpu.with_memory_space_constraint(modes, pltpu.VMEM),
        pltpu.with_memory_space_constraint(energies, pltpu.VMEM),
    )
    return modes.reshape(2, 16, points), energies.reshape(16)


def solution(mesh):
    return jax.shard_map(
        body,
        mesh=mesh,
        in_specs=(P("tm", None, "space"), P("space")),
        out_specs=(P(None, "tm", "space"), P("tm")),
        check_vma=False,
    )
```
